256 devices in a mesh: sp: 64 (over y, z, core), dp: 4 (over x).
Axes of the slice: x: 4, y: 4, z: 8, core: 2. Of those that a mesh axis runs over, the one named last changes fastest.
Arguments:
- volume: bfloat16 [4, 96, 256, 8, 128], P('dp', None, 'sp'), may hold values from -6 to 6
- cotangent: bfloat16 [4, 96, 256, 8, 128], P('dp', None, 'sp'), may hold values from -6 to 6
- kernels_xy: bfloat16 [2, 96, 3, 3], replicated, may hold values from -2 to 2
- kernels_z: bfloat16 [2, 96, 3], replicated, may hold values from -3.5 to 3.5
- mixing: bfloat16 [2, 96, 96], replicated, may hold values from -0.625 to 0.625
Outputs:
- volume_grad: bfloat16 [4, 96, 256, 8, 128], P('dp', None, 'sp')
- mixing_grad: float32 [2, 96, 96], replicated
- xy_grad: float32 [2, 96, 3, 3], replicated
- z_grad: float32 [2, 96, 3], replicated
The draws below stay inside these ranges and needn't reach their ends.
All inputs are finite; a program needn't handle non-finite values.
Results may differ from the reference program's by a relative error of at most 0.018.
Values may be sent and summed in bfloat16 or wider, within the bound.
A program may use at most 64 MiB of HBM per device.

```python
import math
import jax
import jax.numpy as jnp
from jax import lax

C = 96
NZ = 8
NY = 128
BLOCKS = 4
NX = 256


def shard_levels(key, dims, pieces, least, high):
    factor_of, own = 1.0, jax.random.fold_in(key, 6)
    for axis_at, blocks in pieces:
        heights = jnp.exp(jax.random.uniform(jax.random.fold_in(own, axis_at), (blocks,), jnp.float32, least / len(pieces), high / len(pieces)))
        factor_of = factor_of * jnp.repeat(heights, dims[axis_at] // blocks).reshape([-1 if axis == axis_at else 1 for axis in range(len(dims))])
    return factor_of


def bell_draw(rng, shape, spread, limit, split=(), held_as=jnp.bfloat16):
    drawn = jax.random.normal(rng, shape, jnp.float32) * spread
    if len(split) > 0:
        drawn = shard_levels(rng, shape, split, -0.22, 0.18) * drawn
    return jnp.clip(drawn, min=-limit, max=limit).astype(held_as)


def setup_inputs(seed: int = 0) -> dict:
    keys = jax.random.split(jax.random.key(seed), 6)
    volume = bell_draw(keys[0], (BLOCKS, C, NX, NZ, NY), 1.0, 6.0, ((0, 4), (2, 64)))
    cotangent = bell_draw(keys[1], (BLOCKS, C, NX, NZ, NY), 1.0, 6.0, ((0, 4), (2, 64)))
    kernels_xy = bell_draw(keys[2], (2, C, 3, 3), 9 ** -0.5, 2.0)
    kernels_z = bell_draw(keys[3], (2, C, 3), 3 ** -0.5, 3.5)
    mixing = bell_draw(keys[4], (2, C, C), C ** -0.5, 0.625)
    return dict(volume=volume, cotangent=cotangent, kernels_xy=kernels_xy, kernels_z=kernels_z, mixing=mixing)


def conv_plane(inputs, kernel):
    extent = inputs.shape[1] - 2
    across = inputs.shape[3]
    padded = jnp.pad(inputs, ((0, 0), (0, 0), (0, 0), (1, 1)))
    summed = jnp.zeros((inputs.shape[0], extent, inputs.shape[2], across), jnp.float32)
    for row_tap in range(3):
        for col_tap in range(3):
            summed = summed + kernel[:, row_tap, col_tap][:, None, None, None] * padded[:, row_tap:row_tap + extent, :, col_tap:col_tap + across].astype(jnp.float32)
    return summed

def conv_depth(inputs, kernel):
    depth_len = inputs.shape[2]
    padded = jnp.pad(inputs, ((0, 0), (0, 0), (1, 1), (0, 0)))
    summed = jnp.zeros(inputs.shape, jnp.float32)
    for depth_tap in range(3):
        summed = summed + kernel[:, depth_tap][:, None, None, None] * padded[:, :, depth_tap:depth_tap + depth_len, :].astype(jnp.float32)
    return summed

def mix_channels(weights, inputs):
    channels = inputs.shape[0]
    flat = inputs.reshape(channels, -1)
    return jnp.dot(weights, flat, preferred_element_type=jnp.float32).reshape(inputs.shape)

def forward_block(inputs, kernel_xy, kernel_z, weights):
    planar = conv_plane(inputs, kernel_xy)
    axial = conv_depth(planar, kernel_z).astype(jnp.bfloat16)
    preact = mix_channels(weights, axial)
    return (planar, axial, preact)

def silu_slope(preact):
    sigma = jax.nn.sigmoid(preact)
    return sigma * (1.0 + preact * (1.0 - sigma))

def backward_block(grad_out, planar, axial, preact, around, kernel_xy, kernel_z, weights, trim):
    grad_pre = (grad_out.astype(jnp.float32) * silu_slope(preact)).astype(jnp.bfloat16)
    channels = grad_pre.shape[0]
    grad_axial = jnp.dot(weights.T, grad_pre.reshape(channels, -1), preferred_element_type=jnp.float32).reshape(grad_pre.shape)
    grad_planar = conv_depth(grad_axial, kernel_z[:, ::-1]).astype(jnp.bfloat16)
    extent = grad_pre.shape[1]
    own_extent = extent - 2 * trim
    own_pre = grad_pre[:, trim:trim + own_extent].reshape(channels, -1)
    own_axial = axial[:, trim:trim + own_extent].reshape(channels, -1)
    grad_weights = lax.dot_general(own_pre, own_axial, (((1,), (1,)), ((), ())), preferred_element_type=jnp.float32)
    own_grad_axial = grad_axial[:, trim:trim + own_extent]
    depth_len = planar.shape[2]
    planar_pad = jnp.pad(planar[:, trim:trim + own_extent], ((0, 0), (0, 0), (1, 1), (0, 0)))
    grad_kz = jnp.stack([lax.optimization_barrier(jnp.sum(own_grad_axial * planar_pad[:, :, depth_tap:depth_tap + depth_len, :], axis=(1, 2, 3))) for depth_tap in range(3)], axis=1)
    own_grad_planar = grad_planar[:, trim:trim + own_extent].astype(jnp.float32)
    across = around.shape[3]
    around_pad = jnp.pad(around, ((0, 0), (0, 0), (0, 0), (1, 1)))
    rows_list = []
    for row_tap in range(3):
        cols_list = []
        for col_tap in range(3):
            cols_list.append(lax.optimization_barrier(jnp.sum(own_grad_planar * around_pad[:, row_tap:row_tap + own_extent, :, col_tap:col_tap + across].astype(jnp.float32), axis=(1, 2, 3))))
        rows_list.append(jnp.stack(cols_list, axis=1))
    grad_kxy = jnp.stack(rows_list, axis=1)
    return (grad_planar, grad_weights, grad_kxy, grad_kz)

def pad_slab(inputs):
    return jnp.pad(inputs, ((0, 0), (1, 1), (0, 0), (0, 0)))

def one_block(volume_part, grad_part, kernel_xy, kernel_z, mixing):
    planar1, axial1, preact1 = forward_block(pad_slab(volume_part), kernel_xy[0], kernel_z[0], mixing[0])
    hidden = jax.nn.silu(preact1).astype(jnp.bfloat16)
    planar2, axial2, preact2 = forward_block(pad_slab(hidden), kernel_xy[1], kernel_z[1], mixing[1])
    grad_planar2, weights2, plane2, depth2 = backward_block(grad_part, planar2, axial2, preact2, pad_slab(hidden), kernel_xy[1], kernel_z[1], mixing[1], 0)
    grad_hidden = conv_plane(pad_slab(grad_planar2), kernel_xy[1][:, ::-1, ::-1]).astype(jnp.bfloat16)
    grad_planar1, weights1, plane1, depth1 = backward_block(grad_hidden, planar1, axial1, preact1, pad_slab(volume_part), kernel_xy[0], kernel_z[0], mixing[0], 0)
    grad_volume = conv_plane(pad_slab(grad_planar1), kernel_xy[0][:, ::-1, ::-1]).astype(jnp.bfloat16)
    return (grad_volume, jnp.stack([weights1, weights2]), jnp.stack([plane1, plane2]), jnp.stack([depth1, depth2]))

def reference(volume, cotangent, kernels_xy, kernels_z, mixing):
    kernel_xy = kernels_xy.astype(jnp.float32)
    kernel_z = kernels_z.astype(jnp.float32)
    results = lax.map(lambda pair: one_block(pair[0], pair[1], kernel_xy, kernel_z, mixing), (volume, cotangent))
    factor = 1.0 / math.sqrt(BLOCKS * NX * NZ * NY)
    return (results[0], lax.optimization_barrier(jnp.sum(results[1], axis=0)) * factor, lax.optimization_barrier(jnp.sum(results[2], axis=0)) * factor, lax.optimization_barrier(jnp.sum(results[3], axis=0)) * factor)
```

```python
import functools
import math

import jax
import jax.numpy as jnp
from jax import lax
from jax.experimental import pallas as pl
from jax.experimental.pallas import tpu as pltpu
from jax.sharding import PartitionSpec as P

MESH = pl.DeviceIdType.MESH


def padded_2(x, sides, width):
    for axis, dim in sides:
        count, length = (lax.axis_size(axis), x.shape[dim])
        up = [(i, (i + 1) % count) for i in range(count - 1)]
        down = [(j, i) for i, j in up]
        last = lax.slice_in_dim(x, length - width, length, axis=dim)
        first = lax.slice_in_dim(x, 0, width, axis=dim)
        before = lax.ppermute(last, axis, up)
        after = lax.ppermute(first, axis, down)
        x = jnp.concatenate([before, x, after], axis=dim)
    return x


def conv_plane(inputs, kernel):
    extent = inputs.shape[1] - 2
    across = inputs.shape[3]
    padded = jnp.pad(inputs, ((0, 0), (0, 0), (0, 0), (1, 1)))
    summed = jnp.zeros((inputs.shape[0], extent, inputs.shape[2], across), jnp.float32)
    for row_tap in range(3):
        for col_tap in range(3):
            summed = summed + kernel[:, row_tap, col_tap][:, None, None, None] * padded[
                :, row_tap : row_tap + extent, :, col_tap : col_tap + across
            ].astype(jnp.float32)
    return summed


def conv_depth(inputs, kernel):
    depth_len = inputs.shape[2]
    padded = jnp.pad(inputs, ((0, 0), (0, 0), (1, 1), (0, 0)))
    summed = jnp.zeros(inputs.shape, jnp.float32)
    for depth_tap in range(3):
        summed = (
            summed
            + kernel[:, depth_tap][:, None, None, None]
            * padded[:, :, depth_tap : depth_tap + depth_len, :]
        )
    return summed


def mix_channels(weights, inputs):
    channels = inputs.shape[0]
    flat = inputs.reshape(channels, -1)
    return jnp.dot(weights, flat, preferred_element_type=jnp.float32).reshape(inputs.shape)


def forward_block(inputs, kernel_xy, kernel_z, weights):
    planar = conv_plane(inputs, kernel_xy)
    axial = conv_depth(planar, kernel_z).astype(jnp.bfloat16)
    preact = mix_channels(weights, axial)
    return (planar, axial, preact)


def silu_slope(preact):
    sigma = jax.nn.sigmoid(preact)
    return sigma * (1.0 + preact * (1.0 - sigma))


def backward_block(grad_out, planar, axial, preact, around, kernel_z, weights, trim):
    grad_pre = (grad_out.astype(jnp.float32) * silu_slope(preact)).astype(jnp.bfloat16)
    channels = grad_pre.shape[0]
    grad_axial = jnp.dot(
        weights.T, grad_pre.reshape(channels, -1), preferred_element_type=jnp.float32
    ).reshape(grad_pre.shape)
    grad_planar = conv_depth(grad_axial, kernel_z[:, ::-1]).astype(jnp.bfloat16)
    extent = grad_pre.shape[1]
    own_extent = extent - 2 * trim
    own_pre = grad_pre.reshape(channels, -1)
    own_axial = axial.reshape(channels, -1)
    grad_weights = lax.dot_general(
        own_pre, own_axial, (((1,), (1,)), ((), ())), preferred_element_type=jnp.float32
    )
    depth_len = planar.shape[2]
    planar_pad = jnp.pad(planar, ((0, 0), (0, 0), (1, 1), (0, 0)))
    grad_kz = jnp.stack(
        [
            jnp.sum(
                grad_axial * planar_pad[:, :, depth_tap : depth_tap + depth_len, :], axis=(1, 2, 3)
            )
            for depth_tap in range(3)
        ],
        axis=1,
    )
    own_grad_planar = grad_planar.astype(jnp.float32)
    across = around.shape[3]
    around_pad = jnp.pad(around, ((0, 0), (0, 0), (0, 0), (1, 1)))
    rows_list = []
    for row_tap in range(3):
        cols_list = []
        for col_tap in range(3):
            cols_list.append(
                jnp.sum(
                    own_grad_planar
                    * around_pad[
                        :, row_tap : row_tap + own_extent, :, col_tap : col_tap + across
                    ].astype(jnp.float32),
                    axis=(1, 2, 3),
                )
            )
        rows_list.append(jnp.stack(cols_list, axis=1))
    grad_kxy = jnp.stack(rows_list, axis=1)
    return (grad_planar, (grad_weights, grad_kxy, grad_kz))


def edge_grads(grad_planar):
    return padded_2(grad_planar, (("sp", 1),), 1)


def exchange_bits(axes):
    bits = []
    for name, size in axes:
        assert size & (size - 1) == 0
        for b in range(size.bit_length() - 1):
            bits.append((name, 1 << b))
    return bits


def allreduce_kernel(axes, x_ref, o_ref, recv, acc, send_sem, recv_sem):
    bits = exchange_bits(axes)
    here = {name: lax.axis_index(name) for name, _ in axes}
    partners = []
    for name, stride in bits:
        bit = (here[name] // stride) % 2
        where = dict(here)
        where[name] = here[name] + stride * (1 - 2 * bit)
        partners.append(tuple(where[n] for n, _ in axes))
    barrier = pltpu.get_barrier_semaphore()
    for partner in partners:
        pl.semaphore_signal(barrier, inc=1, device_id=partner, device_id_type=MESH)
    pl.semaphore_wait(barrier, len(partners))
    src = x_ref
    for k, partner in enumerate(partners):
        copy = pltpu.make_async_remote_copy(
            src_ref=src,
            dst_ref=recv.at[k],
            send_sem=send_sem.at[k],
            recv_sem=recv_sem.at[k],
            device_id=partner,
            device_id_type=MESH,
        )
        copy.start()
        copy.wait()
        dst = o_ref if k == len(partners) - 1 else acc.at[k]
        dst[...] = src[...] + recv[k]
        src = dst


def all_sum(flat, axes):
    steps = len(exchange_bits(axes))
    return pl.pallas_call(
        functools.partial(allreduce_kernel, axes),
        out_shape=jax.ShapeDtypeStruct(flat.shape, flat.dtype),
        in_specs=[pl.BlockSpec(memory_space=pltpu.VMEM)],
        out_specs=pl.BlockSpec(memory_space=pltpu.VMEM),
        scratch_shapes=[
            pltpu.VMEM((steps,) + flat.shape, flat.dtype),
            pltpu.VMEM((steps,) + flat.shape, flat.dtype),
            pltpu.SemaphoreType.DMA((steps,)),
            pltpu.SemaphoreType.DMA((steps,)),
        ],
        compiler_params=pltpu.CompilerParams(collective_id=0, has_side_effects=True),
    )(flat)


def settle_all(lower, upper):
    parts = (lower[0], lower[1], lower[2], upper[0], upper[1], upper[2])
    flat = jnp.concatenate([p.reshape(-1) for p in parts])
    rows = -(-flat.shape[0] // 1024) * 8
    flat = jnp.pad(flat, (0, rows * 128 - flat.shape[0])).reshape(rows, 128)
    axes = (("sp", lax.axis_size("sp")), ("dp", lax.axis_size("dp")))
    flat = all_sum(flat, axes).reshape(-1)
    summed, at = [], 0
    for p in parts:
        summed.append(flat[at : at + p.size].reshape(p.shape))
        at += p.size
    return ((summed[0], summed[1], summed[2]), (summed[3], summed[4], summed[5]))


def on_device(volume, cotangent, kernels_xy, kernels_z, mixing):
    inputs = volume[0]
    grad_top = cotangent[0]
    kernel_xy = kernels_xy.astype(jnp.float32)
    kernel_z = kernels_z.astype(jnp.float32)
    slab_len = inputs.shape[1]
    ranks = lax.axis_size("sp")
    place = lax.axis_index("sp")
    wide = padded_2(inputs, (("sp", 1),), 2)
    planar1, axial1, preact1 = forward_block(wide, kernel_xy[0], kernel_z[0], mixing[0])
    hidden = jax.nn.silu(preact1).astype(jnp.bfloat16)
    spots = place * slab_len - 1 + jnp.arange(slab_len + 2, dtype=jnp.int32)
    hidden = jnp.where(
        ((spots >= 0) & (spots < slab_len * ranks))[None, :, None, None],
        hidden,
        jnp.zeros_like(hidden),
    )
    planar2, axial2, preact2 = forward_block(hidden, kernel_xy[1], kernel_z[1], mixing[1])
    grad_planar2, upper = backward_block(
        grad_top, planar2, axial2, preact2, hidden, kernel_z[1], mixing[1], 0
    )
    grad_hidden = conv_plane(edge_grads(grad_planar2), kernel_xy[1][:, ::-1, ::-1]).astype(
        jnp.bfloat16
    )
    grad_planar1, lower = backward_block(
        grad_hidden,
        planar1[:, 1:-1],
        axial1[:, 1:-1],
        preact1[:, 1:-1],
        wide[:, 1:-1],
        kernel_z[0],
        mixing[0],
        0,
    )
    grad_inputs = conv_plane(edge_grads(grad_planar1), kernel_xy[0][:, ::-1, ::-1]).astype(
        jnp.bfloat16
    )
    lower, upper = settle_all(lower, upper)
    factor = 1.0 / math.sqrt(
        lax.axis_size("dp") * slab_len * ranks * inputs.shape[2] * inputs.shape[3]
    )
    mixing_grad = jnp.stack([lower[0], upper[0]]) * factor
    xy_grad = jnp.stack([lower[1], upper[1]]) * factor
    z_grad = jnp.stack([lower[2], upper[2]]) * factor
    return (grad_inputs[None], mixing_grad, xy_grad, z_grad)


def solution(mesh):
    return jax.shard_map(
        on_device,
        mesh=mesh,
        in_specs=(P("dp", None, "sp", None, None), P("dp", None, "sp", None, None), P(), P(), P()),
        out_specs=(P("dp", None, "sp", None, None), P(), P(), P()),
        check_vma=False,
    )
```

```python
import functools
import math

import jax
import jax.numpy as jnp
from jax import lax
from jax.experimental import pallas as pl
from jax.experimental.pallas import tpu as pltpu
from jax.sharding import PartitionSpec as P

MESH = pl.DeviceIdType.MESH


def exchange_bits(axes):
    bits = []
    for name, size in axes:
        assert size & (size - 1) == 0
        for b in range(size.bit_length() - 1):
            bits.append((name, 1 << b))
    return bits


def allreduce_kernel(axes, x_ref, o_ref, recv, acc, send_sem, recv_sem):
    bits = exchange_bits(axes)
    here = {name: lax.axis_index(name) for name, _ in axes}
    partners = []
    for name, stride in bits:
        bit = (here[name] // stride) % 2
        where = dict(here)
        where[name] = here[name] + stride * (1 - 2 * bit)
        partners.append(tuple(where[n] for n, _ in axes))
    barrier = pltpu.get_barrier_semaphore()
    for partner in partners:
        pl.semaphore_signal(barrier, inc=1, device_id=partner, device_id_type=MESH)
    pl.semaphore_wait(barrier, len(partners))
    src = x_ref
    for k, partner in enumerate(partners):
        copy = pltpu.make_async_remote_copy(
            src_ref=src,
            dst_ref=recv.at[k],
            send_sem=send_sem.at[k],
            recv_sem=recv_sem.at[k],
            device_id=partner,
            device_id_type=MESH,
        )
        copy.start()
        copy.wait()
        dst = o_ref if k == len(partners) - 1 else acc.at[k]
        dst[...] = src[...] + recv[k]
        src = dst


def all_sum(flat, axes):
    steps = len(exchange_bits(axes))
    return pl.pallas_call(
        functools.partial(allreduce_kernel, axes),
        out_shape=jax.ShapeDtypeStruct(flat.shape, flat.dtype),
        in_specs=[pl.BlockSpec(memory_space=pltpu.VMEM)],
        out_specs=pl.BlockSpec(memory_space=pltpu.VMEM),
        scratch_shapes=[
            pltpu.VMEM((steps,) + flat.shape, flat.dtype),
            pltpu.VMEM((steps,) + flat.shape, flat.dtype),
            pltpu.SemaphoreType.DMA((steps,)),
            pltpu.SemaphoreType.DMA((steps,)),
        ],
        compiler_params=pltpu.CompilerParams(collective_id=0, has_side_effects=True),
    )(flat)


def settle_all(*parts):
    flat = jnp.concatenate([p.reshape(-1) for p in parts])
    rows = -(-flat.shape[0] // 1024) * 8
    flat = jnp.pad(flat, (0, rows * 128 - flat.shape[0])).reshape(rows, 128)
    axes = (("sp", lax.axis_size("sp")), ("dp", lax.axis_size("dp")))
    flat = all_sum(flat, axes).reshape(-1)
    summed, at = [], 0
    for p in parts:
        summed.append(flat[at : at + p.size].reshape(p.shape))
        at += p.size
    return summed


VMEM_LIMIT = 56 * 1024 * 1024


def halo(x, width):
    count = lax.axis_size("sp")
    up = [(i, i + 1) for i in range(count - 1)]
    down = [(j, i) for i, j in up]
    before = lax.ppermute(x[x.shape[0] - width :], "sp", up)
    after = lax.ppermute(x[:width], "sp", down)
    return jnp.concatenate([before, x, after], axis=0)


def coords(shape):
    lane = lax.broadcasted_iota(jnp.int32, shape, 1)
    return jnp.bitwise_and(lane, 127), jnp.right_shift(lane, 7)


def at_y(a, d, y):
    if d == 0:
        return a
    rolled = pltpu.roll(a, (-d) % a.shape[1], 1)
    return jnp.where((y + d >= 0) & (y + d < 128), rolled, 0.0)


def at_z(a, d, z):
    if d == 0:
        return a
    rolled = pltpu.roll(a, (-128 * d) % a.shape[1], 1)
    return jnp.where((z + d >= 0) & (z + d < a.shape[1] // 128), rolled, 0.0)


def widen(k, lanes):
    return jnp.concatenate([k] * (lanes // k.shape[1]), axis=1)


def fold(a):
    total = a[:, :128]
    for g in range(1, a.shape[1] // 128):
        total = total + a[:, g * 128 : (g + 1) * 128]
    return total


def sigmoid(u):
    return 1.0 / (1.0 + jnp.exp(-u))


def plane_conv(planes, k_ref, b, flip, y):
    lanes = planes[0].shape[1]
    total = None
    for i in range(3):
        src = planes[i].astype(jnp.float32)
        for j in range(3):
            tap = (2 - i) * 3 + (2 - j) if flip else i * 3 + j
            term = widen(k_ref[b, tap], lanes) * at_y(src, j - 1, y)
            total = term if total is None else total + term
    return total


def depth_conv(a, kz_ref, b, flip, z):
    lanes = a.shape[1]
    total = None
    for t in range(3):
        tap = 2 - t if flip else t
        term = widen(kz_ref[b, tap], lanes) * at_z(a, t - 1, z)
        total = term if total is None else total + term
    return total


def silu_grad(g, pre):
    s = sigmoid(pre)
    return (g * (s * (1.0 + pre * (1.0 - s)))).astype(jnp.bfloat16)


def weight_grads(b, gpre, ax, gax, pl, gpl, around, mix_ref, kzg_ref, kxyg_ref, y, z):
    mix_ref[b] += lax.dot_general(
        gpre, ax, (((1,), (1,)), ((), ())), preferred_element_type=jnp.float32
    )
    for t in range(3):
        kzg_ref[b, t] += fold(gax * at_z(pl, t - 1, z))
    gplf = gpl.astype(jnp.float32)
    for i in range(3):
        src = around[i].astype(jnp.float32)
        for j in range(3):
            kxyg_ref[b, i * 3 + j] += fold(gplf * at_y(src, j - 1, y))


def upper_kernel(mask_ref, wide_ref, cot_ref, kxy_ref, kz_ref, w_ref, wt_ref,
                 gp2_ref, pre1_ref, ax1_ref, pl1_ref, mix_ref, kzg_ref, kxyg_ref, h2_ref):
    own = cot_ref.shape[0]
    y, z = coords(cot_ref.shape[1:])
    mix_ref[...] = jnp.zeros_like(mix_ref)
    kzg_ref[...] = jnp.zeros_like(kzg_ref)
    kxyg_ref[...] = jnp.zeros_like(kxyg_ref)

    def forward1(p, carry):
        planar = plane_conv([wide_ref[p + i] for i in range(3)], kxy_ref, 0, False, y)
        axial = depth_conv(planar, kz_ref, 0, False, z).astype(jnp.bfloat16)
        pre = jnp.dot(w_ref[0], axial, preferred_element_type=jnp.float32)
        pl1_ref[p] = planar
        ax1_ref[p] = axial
        pre1_ref[p] = pre
        h2_ref[p] = (pre * sigmoid(pre) * mask_ref[p]).astype(jnp.bfloat16)
        return carry

    lax.fori_loop(0, own + 2, forward1, 0)

    def block2(q, carry):
        around = [h2_ref[q + i] for i in range(3)]
        planar = plane_conv(around, kxy_ref, 1, False, y)
        axial = depth_conv(planar, kz_ref, 1, False, z).astype(jnp.bfloat16)
        pre = jnp.dot(w_ref[1], axial, preferred_element_type=jnp.float32)
        gpre = silu_grad(cot_ref[q].astype(jnp.float32), pre)
        gax = jnp.dot(wt_ref[1], gpre, preferred_element_type=jnp.float32)
        gpl = depth_conv(gax, kz_ref, 1, True, z).astype(jnp.bfloat16)
        gp2_ref[q] = gpl
        weight_grads(1, gpre, axial, gax, planar, gpl, around, mix_ref, kzg_ref, kxyg_ref, y, z)
        return carry

    lax.fori_loop(0, own, block2, 0)


def lower_kernel(gp2_ref, wide_ref, pre1_ref, ax1_ref, pl1_ref, kxy_ref, kz_ref, w_ref, wt_ref, mix_in, kzg_in, kxyg_in,
                 gp1_ref, mix_ref, kzg_ref, kxyg_ref):
    own = gp1_ref.shape[0]
    y, z = coords(gp1_ref.shape[1:])
    mix_ref[...] = mix_in[...]
    kzg_ref[...] = kzg_in[...]
    kxyg_ref[...] = kxyg_in[...]

    def block1(q, carry):
        g1 = plane_conv([gp2_ref[q + i] for i in range(3)], kxy_ref, 1, True, y).astype(jnp.bfloat16)
        gpre = silu_grad(g1.astype(jnp.float32), pre1_ref[q + 1])
        gax = jnp.dot(wt_ref[0], gpre, preferred_element_type=jnp.float32)
        gpl = depth_conv(gax, kz_ref, 0, True, z).astype(jnp.bfloat16)
        gp1_ref[q] = gpl
        around = [wide_ref[q + 1 + i] for i in range(3)]
        weight_grads(0, gpre, ax1_ref[q + 1], gax, pl1_ref[q + 1], gpl, around, mix_ref, kzg_ref, kxyg_ref, y, z)
        return carry

    lax.fori_loop(0, own, block1, 0)


def input_kernel(gp1_ref, kxy_ref, out_ref):
    y, _ = coords(out_ref.shape[1:])

    def plane(q, carry):
        out_ref[q] = plane_conv([gp1_ref[q + i] for i in range(3)], kxy_ref, 0, True, y).astype(out_ref.dtype)
        return carry

    lax.fori_loop(0, out_ref.shape[0], plane, 0)


def vmem_call(kernel, args, outs, scratch=(), smem=0, aliases=None):
    specs = [pl.BlockSpec(memory_space=pltpu.SMEM)] * smem + [pl.BlockSpec(memory_space=pltpu.VMEM)] * (len(args) - smem)
    return pl.pallas_call(
        kernel,
        out_shape=outs,
        in_specs=specs,
        out_specs=[pl.BlockSpec(memory_space=pltpu.VMEM)] * len(outs),
        scratch_shapes=list(scratch),
        input_output_aliases=aliases or {},
        compiler_params=pltpu.CompilerParams(vmem_limit_bytes=VMEM_LIMIT),
    )(*args)


def on_device(volume, cotangent, kernels_xy, kernels_z, mixing):
    _, chans, own, depth, across = volume.shape
    lanes = depth * across
    f32, bf16 = jnp.float32, jnp.bfloat16
    vol = volume[0].reshape(chans, own, lanes).transpose(1, 0, 2)
    cot = cotangent[0].reshape(chans, own, lanes).transpose(1, 0, 2)
    kxy = jnp.broadcast_to(
        kernels_xy.astype(f32).reshape(2, chans, 9).transpose(0, 2, 1)[..., None], (2, 9, chans, 128)
    )
    kz = jnp.broadcast_to(kernels_z.astype(f32).transpose(0, 2, 1)[..., None], (2, 3, chans, 128))
    wt = mixing.transpose(0, 2, 1)
    ranks = lax.axis_size("sp")
    place = lax.axis_index("sp")
    spots = place * own - 1 + jnp.arange(own + 2, dtype=jnp.int32)
    mask = ((spots >= 0) & (spots < own * ranks)).astype(f32)
    wide = halo(vol, 2)
    plane = lambda n, t: jax.ShapeDtypeStruct((n, chans, lanes), t)
    gp2, pre1, ax1, pl1, mix, kzg, kxyg = vmem_call(
        upper_kernel,
        (mask, wide, cot, kxy, kz, mixing, wt),
        (
            plane(own, bf16), plane(own + 2, f32), plane(own + 2, bf16), plane(own + 2, f32),
            jax.ShapeDtypeStruct((2, chans, chans), f32),
            jax.ShapeDtypeStruct((2, 3, chans, 128), f32),
            jax.ShapeDtypeStruct((2, 9, chans, 128), f32),
        ),
        scratch=[pltpu.VMEM((own + 2, chans, lanes), bf16)],
        smem=1,
    )
    gp1, mix, kzg, kxyg = vmem_call(
        lower_kernel,
        (halo(gp2, 1), wide, pre1, ax1, pl1, kxy, kz, mixing, wt, mix, kzg, kxyg),
        (plane(own, bf16), jax.ShapeDtypeStruct((2, chans, chans), f32),
         jax.ShapeDtypeStruct((2, 3, chans, 128), f32), jax.ShapeDtypeStruct((2, 9, chans, 128), f32)),
    )
    grad_in = vmem_call(input_kernel, (halo(gp1, 1), kxy), (plane(own, bf16),))[0]
    grad_in = grad_in.transpose(1, 0, 2).reshape(1, chans, own, depth, across)
    kz_sum = kzg.sum(axis=3).transpose(0, 2, 1)
    kxy_sum = kxyg.sum(axis=3).transpose(0, 2, 1).reshape(2, chans, 3, 3)
    summed = settle_all(mix, kxy_sum, kz_sum)
    factor = 1.0 / math.sqrt(lax.axis_size("dp") * own * ranks * depth * across)
    return (grad_in, summed[0] * factor, summed[1] * factor, summed[2] * factor)


def solution(mesh):
    return jax.shard_map(
        on_device,
        mesh=mesh,
        in_specs=(P("dp", None, "sp", None, None), P("dp", None, "sp", None, None), P(), P(), P()),
        out_specs=(P("dp", None, "sp", None, None), P(), P(), P()),
        check_vma=False,
    )
```

```python
import functools
import math

import jax
import jax.numpy as jnp
from jax import lax
from jax.experimental import pallas as pl
from jax.experimental.pallas import tpu as pltpu
from jax.sharding import PartitionSpec as P

MESH = pl.DeviceIdType.MESH


def exchange_groups(axes, radix_bits):
    bits = []
    for name, size in axes:
        assert size & (size - 1) == 0
        for b in range(size.bit_length() - 1):
            bits.append((name, 1 << b))
    return [bits[i : i + radix_bits] for i in range(0, len(bits), radix_bits)]


def allreduce_kernel(axes, groups, x_ref, o_ref, recv, acc, send_sem, recv_sem):
    here = {name: lax.axis_index(name) for name, _ in axes}
    steps = []
    for group in groups:
        partners = []
        for offset in range(1, 1 << len(group)):
            where = dict(here)
            for k, (name, stride) in enumerate(group):
                if (offset >> k) & 1:
                    bit = (where[name] // stride) % 2
                    where[name] = where[name] + stride * (1 - 2 * bit)
            partners.append(tuple(where[n] for n, _ in axes))
        steps.append(partners)
    barrier = pltpu.get_barrier_semaphore()
    count = 0
    for partners in steps:
        for partner in partners:
            pl.semaphore_signal(barrier, inc=1, device_id=partner, device_id_type=MESH)
            count += 1
    pl.semaphore_wait(barrier, count)
    src = x_ref
    copies = []
    slot = 0
    for g, partners in enumerate(steps):
        here_copies = []
        for k, partner in enumerate(partners):
            copy = pltpu.make_async_remote_copy(
                src_ref=src,
                dst_ref=recv.at[slot + k],
                send_sem=send_sem.at[slot + k],
                recv_sem=recv_sem.at[slot + k],
                device_id=partner,
                device_id_type=MESH,
            )
            copy.start()
            here_copies.append(copy)
        for copy in here_copies:
            copy.wait_recv()
        copies += here_copies
        vals = [src[...]] + [recv[slot + k] for k in range(len(partners))]
        while len(vals) > 1:
            vals = [vals[i] + vals[i + 1] for i in range(0, len(vals), 2)]
        dst = o_ref if g == len(steps) - 1 else acc.at[g]
        dst[...] = vals[0]
        src = dst
        slot += len(partners)
    for copy in copies:
        copy.wait_send()


def all_sum(flat, axes, radix_bits=2):
    groups = exchange_groups(axes, radix_bits)
    slots = sum((1 << len(g)) - 1 for g in groups)
    return pl.pallas_call(
        functools.partial(allreduce_kernel, axes, groups),
        out_shape=jax.ShapeDtypeStruct(flat.shape, flat.dtype),
        in_specs=[pl.BlockSpec(memory_space=pltpu.VMEM)],
        out_specs=pl.BlockSpec(memory_space=pltpu.VMEM),
        scratch_shapes=[
            pltpu.VMEM((slots,) + flat.shape, flat.dtype),
            pltpu.VMEM((len(groups),) + flat.shape, flat.dtype),
            pltpu.SemaphoreType.DMA((slots,)),
            pltpu.SemaphoreType.DMA((slots,)),
        ],
        compiler_params=pltpu.CompilerParams(collective_id=0, has_side_effects=True),
    )(flat)


def settle_all(*parts):
    flat = jnp.concatenate([p.reshape(-1) for p in parts])
    rows = -(-flat.shape[0] // 1024) * 8
    flat = jnp.pad(flat, (0, rows * 128 - flat.shape[0])).reshape(rows, 128)
    axes = (("sp", lax.axis_size("sp")), ("dp", lax.axis_size("dp")))
    flat = all_sum(flat, axes).reshape(-1)
    summed, at = [], 0
    for p in parts:
        summed.append(flat[at : at + p.size].reshape(p.shape))
        at += p.size
    return summed


VMEM_LIMIT = 56 * 1024 * 1024


def halo(x, width):
    count = lax.axis_size("sp")
    up = [(i, i + 1) for i in range(count - 1)]
    down = [(j, i) for i, j in up]
    before = lax.ppermute(x[x.shape[0] - width :], "sp", up)
    after = lax.ppermute(x[:width], "sp", down)
    return jnp.concatenate([before, x, after], axis=0)


def coords(shape):
    lane = lax.broadcasted_iota(jnp.int32, shape, 1)
    return jnp.bitwise_and(lane, 127), jnp.right_shift(lane, 7)


def at_y(a, d, y):
    if d == 0:
        return a
    rolled = pltpu.roll(a, (-d) % a.shape[1], 1)
    return jnp.where((y + d >= 0) & (y + d < 128), rolled, 0.0)


def at_z(a, d, z):
    if d == 0:
        return a
    rolled = pltpu.roll(a, (-128 * d) % a.shape[1], 1)
    return jnp.where((z + d >= 0) & (z + d < a.shape[1] // 128), rolled, 0.0)


def widen(k, lanes):
    return jnp.concatenate([k] * (lanes // k.shape[1]), axis=1)


def fold(a):
    total = a[:, :128]
    for g in range(1, a.shape[1] // 128):
        total = total + a[:, g * 128 : (g + 1) * 128]
    return total


def sigmoid(u):
    return 1.0 / (1.0 + jnp.exp(-u))


def plane_conv(planes, k_ref, b, flip, y):
    lanes = planes[0].shape[1]
    total = None
    for i in range(3):
        src = planes[i].astype(jnp.float32)
        for j in range(3):
            tap = (2 - i) * 3 + (2 - j) if flip else i * 3 + j
            term = widen(k_ref[b, tap], lanes) * at_y(src, j - 1, y)
            total = term if total is None else total + term
    return total


def depth_conv(a, kz_ref, b, flip, z):
    lanes = a.shape[1]
    total = None
    for t in range(3):
        tap = 2 - t if flip else t
        term = widen(kz_ref[b, tap], lanes) * at_z(a, t - 1, z)
        total = term if total is None else total + term
    return total


def silu_grad(g, pre):
    s = sigmoid(pre)
    return (g * (s * (1.0 + pre * (1.0 - s)))).astype(jnp.bfloat16)


def weight_grads(b, gpre, ax, gax, pl, gpl, around, mix_ref, kzg_ref, kxyg_ref, y, z):
    mix_ref[b] += lax.dot_general(
        gpre, ax, (((1,), (1,)), ((), ())), preferred_element_type=jnp.float32
    )
    for t in range(3):
        kzg_ref[b, t] += fold(gax * at_z(pl, t - 1, z))
    gplf = gpl.astype(jnp.float32)
    for i in range(3):
        src = around[i].astype(jnp.float32)
        for j in range(3):
            kxyg_ref[b, i * 3 + j] += fold(gplf * at_y(src, j - 1, y))


def upper_kernel(mask_ref, wide_ref, cot_ref, kxy_ref, kz_ref, w_ref, wt_ref,
                 gp2_ref, pre1_ref, ax1_ref, pl1_ref, mix_ref, kzg_ref, kxyg_ref, h2_ref):
    own = cot_ref.shape[0]
    y, z = coords(cot_ref.shape[1:])
    mix_ref[...] = jnp.zeros_like(mix_ref)
    kzg_ref[...] = jnp.zeros_like(kzg_ref)
    kxyg_ref[...] = jnp.zeros_like(kxyg_ref)

    def forward1(p, carry):
        planar = plane_conv([wide_ref[p + i] for i in range(3)], kxy_ref, 0, False, y)
        axial = depth_conv(planar, kz_ref, 0, False, z).astype(jnp.bfloat16)
        pre = jnp.dot(w_ref[0], axial, preferred_element_type=jnp.float32)
        pl1_ref[p] = planar
        ax1_ref[p] = axial
        pre1_ref[p] = pre
        h2_ref[p] = (pre * sigmoid(pre) * mask_ref[p]).astype(jnp.bfloat16)
        return carry

    lax.fori_loop(0, own + 2, forward1, 0)

    def block2(q, carry):
        around = [h2_ref[q + i] for i in range(3)]
        planar = plane_conv(around, kxy_ref, 1, False, y)
        axial = depth_conv(planar, kz_ref, 1, False, z).astype(jnp.bfloat16)
        pre = jnp.dot(w_ref[1], axial, preferred_element_type=jnp.float32)
        gpre = silu_grad(cot_ref[q].astype(jnp.float32), pre)
        gax = jnp.dot(wt_ref[1], gpre, preferred_element_type=jnp.float32)
        gpl = depth_conv(gax, kz_ref, 1, True, z).astype(jnp.bfloat16)
        gp2_ref[q] = gpl
        weight_grads(1, gpre, axial, gax, planar, gpl, around, mix_ref, kzg_ref, kxyg_ref, y, z)
        return carry

    lax.fori_loop(0, own, block2, 0)


def lower_kernel(gp2_ref, wide_ref, pre1_ref, ax1_ref, pl1_ref, kxy_ref, kz_ref, w_ref, wt_ref, mix_in, kzg_in, kxyg_in,
                 gp1_ref, mix_ref, kzg_ref, kxyg_ref):
    own = gp1_ref.shape[0]
    y, z = coords(gp1_ref.shape[1:])
    mix_ref[...] = mix_in[...]
    kzg_ref[...] = kzg_in[...]
    kxyg_ref[...] = kxyg_in[...]

    def block1(q, carry):
        g1 = plane_conv([gp2_ref[q + i] for i in range(3)], kxy_ref, 1, True, y).astype(jnp.bfloat16)
        gpre = silu_grad(g1.astype(jnp.float32), pre1_ref[q + 1])
        gax = jnp.dot(wt_ref[0], gpre, preferred_element_type=jnp.float32)
        gpl = depth_conv(gax, kz_ref, 0, True, z).astype(jnp.bfloat16)
        gp1_ref[q] = gpl
        around = [wide_ref[q + 1 + i] for i in range(3)]
        weight_grads(0, gpre, ax1_ref[q + 1], gax, pl1_ref[q + 1], gpl, around, mix_ref, kzg_ref, kxyg_ref, y, z)
        return carry

    lax.fori_loop(0, own, block1, 0)


def input_kernel(gp1_ref, kxy_ref, out_ref):
    y, _ = coords(out_ref.shape[1:])

    def plane(q, carry):
        out_ref[q] = plane_conv([gp1_ref[q + i] for i in range(3)], kxy_ref, 0, True, y).astype(out_ref.dtype)
        return carry

    lax.fori_loop(0, out_ref.shape[0], plane, 0)


def vmem_call(kernel, args, outs, scratch=(), smem=0, aliases=None):
    specs = [pl.BlockSpec(memory_space=pltpu.SMEM)] * smem + [pl.BlockSpec(memory_space=pltpu.VMEM)] * (len(args) - smem)
    return pl.pallas_call(
        kernel,
        out_shape=outs,
        in_specs=specs,
        out_specs=[pl.BlockSpec(memory_space=pltpu.VMEM)] * len(outs),
        scratch_shapes=list(scratch),
        input_output_aliases=aliases or {},
        compiler_params=pltpu.CompilerParams(vmem_limit_bytes=VMEM_LIMIT),
    )(*args)


def on_device(volume, cotangent, kernels_xy, kernels_z, mixing):
    _, chans, own, depth, across = volume.shape
    lanes = depth * across
    f32, bf16 = jnp.float32, jnp.bfloat16
    vol = volume[0].reshape(chans, own, lanes).transpose(1, 0, 2)
    cot = cotangent[0].reshape(chans, own, lanes).transpose(1, 0, 2)
    kxy = jnp.broadcast_to(
        kernels_xy.astype(f32).reshape(2, chans, 9).transpose(0, 2, 1)[..., None], (2, 9, chans, 128)
    )
    kz = jnp.broadcast_to(kernels_z.astype(f32).transpose(0, 2, 1)[..., None], (2, 3, chans, 128))
    wt = mixing.transpose(0, 2, 1)
    ranks = lax.axis_size("sp")
    place = lax.axis_index("sp")
    spots = place * own - 1 + jnp.arange(own + 2, dtype=jnp.int32)
    mask = ((spots >= 0) & (spots < own * ranks)).astype(f32)
    wide = halo(vol, 2)
    plane = lambda n, t: jax.ShapeDtypeStruct((n, chans, lanes), t)
    gp2, pre1, ax1, pl1, mix, kzg, kxyg = vmem_call(
        upper_kernel,
        (mask, wide, cot, kxy, kz, mixing, wt),
        (
            plane(own, bf16), plane(own + 2, f32), plane(own + 2, bf16), plane(own + 2, f32),
            jax.ShapeDtypeStruct((2, chans, chans), f32),
            jax.ShapeDtypeStruct((2, 3, chans, 128), f32),
            jax.ShapeDtypeStruct((2, 9, chans, 128), f32),
        ),
        scratch=[pltpu.VMEM((own + 2, chans, lanes), bf16)],
        smem=1,
    )
    gp1, mix, kzg, kxyg = vmem_call(
        lower_kernel,
        (halo(gp2, 1), wide, pre1, ax1, pl1, kxy, kz, mixing, wt, mix, kzg, kxyg),
        (plane(own, bf16), jax.ShapeDtypeStruct((2, chans, chans), f32),
         jax.ShapeDtypeStruct((2, 3, chans, 128), f32), jax.ShapeDtypeStruct((2, 9, chans, 128), f32)),
    )
    grad_in = vmem_call(input_kernel, (halo(gp1, 1), kxy), (plane(own, bf16),))[0]
    grad_in = grad_in.transpose(1, 0, 2).reshape(1, chans, own, depth, across)
    kz_sum = kzg.sum(axis=3).transpose(0, 2, 1)
    kxy_sum = kxyg.sum(axis=3).transpose(0, 2, 1).reshape(2, chans, 3, 3)
    summed = settle_all(mix, kxy_sum, kz_sum)
    factor = 1.0 / math.sqrt(lax.axis_size("dp") * own * ranks * depth * across)
    return (grad_in, summed[0] * factor, summed[1] * factor, summed[2] * factor)


def solution(mesh):
    return jax.shard_map(
        on_device,
        mesh=mesh,
        in_specs=(P("dp", None, "sp", None, None), P("dp", None, "sp", None, None), P(), P(), P()),
        out_specs=(P("dp", None, "sp", None, None), P(), P(), P()),
        check_vma=False,
    )
```

```python
import functools
import math

import jax
import jax.numpy as jnp
from jax import lax
from jax.experimental import pallas as pl
from jax.experimental.pallas import tpu as pltpu
from jax.sharding import PartitionSpec as P

MESH = pl.DeviceIdType.MESH
VMEM_LIMIT = 56 * 1024 * 1024


def exchange_groups(axes, radix_bits):
    bits = []
    for name, size in axes:
        assert size & (size - 1) == 0
        for b in range(size.bit_length() - 1):
            bits.append((name, 1 << b))
    return [bits[i : i + radix_bits] for i in range(0, len(bits), radix_bits)]


def allreduce_kernel(axes, groups, x_ref, gp1_ref, kxy_ref, o_ref, vg_ref, recv, acc, send_sem, recv_sem):
    here = {name: lax.axis_index(name) for name, _ in axes}
    steps = []
    for group in groups:
        partners = []
        for offset in range(1, 1 << len(group)):
            where = dict(here)
            for k, (name, stride) in enumerate(group):
                if (offset >> k) & 1:
                    bit = (where[name] // stride) % 2
                    where[name] = where[name] + stride * (1 - 2 * bit)
            partners.append(tuple(where[n] for n, _ in axes))
        steps.append(partners)
    barrier = pltpu.get_barrier_semaphore()
    count = 0
    for partners in steps:
        for partner in partners:
            pl.semaphore_signal(barrier, inc=1, device_id=partner, device_id_type=MESH)
            count += 1
    pl.semaphore_wait(barrier, count)
    src = x_ref
    copies = []
    slot = 0
    for g, partners in enumerate(steps):
        here_copies = []
        for k, partner in enumerate(partners):
            copy = pltpu.make_async_remote_copy(
                src_ref=src,
                dst_ref=recv.at[slot + k],
                send_sem=send_sem.at[slot + k],
                recv_sem=recv_sem.at[slot + k],
                device_id=partner,
                device_id_type=MESH,
            )
            copy.start()
            here_copies.append(copy)
        planes = vg_ref.shape[0]
        for q in range(g * planes // len(steps), (g + 1) * planes // len(steps)):
            y, _ = coords(vg_ref.shape[1:])
            vg_ref[q] = plane_conv([gp1_ref[q + i] for i in range(3)], kxy_ref, 0, True, y).astype(vg_ref.dtype)
        for copy in here_copies:
            copy.wait_recv()
        copies += here_copies
        vals = [src[...]] + [recv[slot + k] for k in range(len(partners))]
        while len(vals) > 1:
            vals = [vals[i] + vals[i + 1] for i in range(0, len(vals), 2)]
        dst = o_ref if g == len(steps) - 1 else acc.at[g]
        dst[...] = vals[0]
        src = dst
        slot += len(partners)
    for copy in copies:
        copy.wait_send()


def all_sum(flat, gp1, kxy, axes, radix_bits=2):
    groups = exchange_groups(axes, radix_bits)
    slots = sum((1 << len(g)) - 1 for g in groups)
    own = gp1.shape[0] - 2
    return pl.pallas_call(
        functools.partial(allreduce_kernel, axes, groups),
        out_shape=(
            jax.ShapeDtypeStruct(flat.shape, flat.dtype),
            jax.ShapeDtypeStruct((own,) + gp1.shape[1:], gp1.dtype),
        ),
        in_specs=[pl.BlockSpec(memory_space=pltpu.VMEM)] * 3,
        out_specs=[pl.BlockSpec(memory_space=pltpu.VMEM)] * 2,
        scratch_shapes=[
            pltpu.VMEM((slots,) + flat.shape, flat.dtype),
            pltpu.VMEM((len(groups),) + flat.shape, flat.dtype),
            pltpu.SemaphoreType.DMA((slots,)),
            pltpu.SemaphoreType.DMA((slots,)),
        ],
        compiler_params=pltpu.CompilerParams(
            collective_id=0, has_side_effects=True, vmem_limit_bytes=VMEM_LIMIT
        ),
    )(flat, gp1, kxy)


def settle_all(parts, gp1, kxy):
    flat = jnp.concatenate([p.reshape(-1) for p in parts])
    rows = -(-flat.shape[0] // 1024) * 8
    flat = jnp.pad(flat, (0, rows * 128 - flat.shape[0])).reshape(rows, 128)
    axes = (("sp", lax.axis_size("sp")), ("dp", lax.axis_size("dp")))
    flat, grad_in = all_sum(flat, gp1, kxy, axes)
    flat = flat.reshape(-1)
    summed, at = [], 0
    for p in parts:
        summed.append(flat[at : at + p.size].reshape(p.shape))
        at += p.size
    return summed, grad_in


def halo(x, width):
    count = lax.axis_size("sp")
    up = [(i, i + 1) for i in range(count - 1)]
    down = [(j, i) for i, j in up]
    before = lax.ppermute(x[x.shape[0] - width :], "sp", up)
    after = lax.ppermute(x[:width], "sp", down)
    return jnp.concatenate([before, x, after], axis=0)


def coords(shape):
    lane = lax.broadcasted_iota(jnp.int32, shape, 1)
    return jnp.bitwise_and(lane, 127), jnp.right_shift(lane, 7)


def at_y(a, d, y):
    if d == 0:
        return a
    rolled = pltpu.roll(a, (-d) % a.shape[1], 1)
    return jnp.where((y + d >= 0) & (y + d < 128), rolled, 0.0)


def at_z(a, d, z):
    if d == 0:
        return a
    rolled = pltpu.roll(a, (-128 * d) % a.shape[1], 1)
    return jnp.where((z + d >= 0) & (z + d < a.shape[1] // 128), rolled, 0.0)


def widen(k, lanes):
    return jnp.concatenate([k] * (lanes // k.shape[1]), axis=1)


def fold(a):
    total = a[:, :128]
    for g in range(1, a.shape[1] // 128):
        total = total + a[:, g * 128 : (g + 1) * 128]
    return total


def sigmoid(u):
    return 1.0 / (1.0 + jnp.exp(-u))


def plane_conv(planes, k_ref, b, flip, y):
    lanes = planes[0].shape[1]
    total = None
    for i in range(3):
        src = planes[i].astype(jnp.float32)
        for j in range(3):
            tap = (2 - i) * 3 + (2 - j) if flip else i * 3 + j
            term = widen(k_ref[b, tap], lanes) * at_y(src, j - 1, y)
            total = term if total is None else total + term
    return total


def depth_conv(a, kz_ref, b, flip, z):
    lanes = a.shape[1]
    total = None
    for t in range(3):
        tap = 2 - t if flip else t
        term = widen(kz_ref[b, tap], lanes) * at_z(a, t - 1, z)
        total = term if total is None else total + term
    return total


def silu_grad(g, pre):
    s = sigmoid(pre)
    return (g * (s * (1.0 + pre * (1.0 - s)))).astype(jnp.bfloat16)


def weight_grads(b, gpre, ax, gax, pl, gpl, around, mix_ref, kzg_ref, kxyg_ref, y, z):
    mix_ref[b] += lax.dot_general(
        gpre, ax, (((1,), (1,)), ((), ())), preferred_element_type=jnp.float32
    )
    for t in range(3):
        kzg_ref[b, t] += fold(gax * at_z(pl, t - 1, z))
    gplf = gpl.astype(jnp.float32)
    for i in range(3):
        src = around[i].astype(jnp.float32)
        for j in range(3):
            kxyg_ref[b, i * 3 + j] += fold(gplf * at_y(src, j - 1, y))


def upper_kernel(mask_ref, wide_ref, cot_ref, kxy_ref, kz_ref, w_ref, wt_ref,
                 gp2_ref, pre1_ref, ax1_ref, pl1_ref, mix_ref, kzg_ref, kxyg_ref, h2_ref):
    own = cot_ref.shape[0]
    y, z = coords(cot_ref.shape[1:])
    mix_ref[...] = jnp.zeros_like(mix_ref)
    kzg_ref[...] = jnp.zeros_like(kzg_ref)
    kxyg_ref[...] = jnp.zeros_like(kxyg_ref)

    def forward1(p, carry):
        planar = plane_conv([wide_ref[p + i] for i in range(3)], kxy_ref, 0, False, y)
        axial = depth_conv(planar, kz_ref, 0, False, z).astype(jnp.bfloat16)
        pre = jnp.dot(w_ref[0], axial, preferred_element_type=jnp.float32)
        pl1_ref[p] = planar
        ax1_ref[p] = axial
        pre1_ref[p] = pre
        h2_ref[p] = (pre * sigmoid(pre) * mask_ref[p]).astype(jnp.bfloat16)
        return carry

    lax.fori_loop(0, own + 2, forward1, 0)

    def block2(q, carry):
        around = [h2_ref[q + i] for i in range(3)]
        planar = plane_conv(around, kxy_ref, 1, False, y)
        axial = depth_conv(planar, kz_ref, 1, False, z).astype(jnp.bfloat16)
        pre = jnp.dot(w_ref[1], axial, preferred_element_type=jnp.float32)
        gpre = silu_grad(cot_ref[q].astype(jnp.float32), pre)
        gax = jnp.dot(wt_ref[1], gpre, preferred_element_type=jnp.float32)
        gpl = depth_conv(gax, kz_ref, 1, True, z).astype(jnp.bfloat16)
        gp2_ref[q] = gpl
        weight_grads(1, gpre, axial, gax, planar, gpl, around, mix_ref, kzg_ref, kxyg_ref, y, z)
        return carry

    lax.fori_loop(0, own, block2, 0)


def lower_kernel(gp2_ref, wide_ref, pre1_ref, ax1_ref, pl1_ref, kxy_ref, kz_ref, w_ref, wt_ref, mix_in, kzg_in, kxyg_in,
                 gp1_ref, mix_ref, kzg_ref, kxyg_ref):
    own = gp1_ref.shape[0]
    y, z = coords(gp1_ref.shape[1:])
    mix_ref[...] = mix_in[...]
    kzg_ref[...] = kzg_in[...]
    kxyg_ref[...] = kxyg_in[...]

    def block1(q, carry):
        g1 = plane_conv([gp2_ref[q + i] for i in range(3)], kxy_ref, 1, True, y).astype(jnp.bfloat16)
        gpre = silu_grad(g1.astype(jnp.float32), pre1_ref[q + 1])
        gax = jnp.dot(wt_ref[0], gpre, preferred_element_type=jnp.float32)
        gpl = depth_conv(gax, kz_ref, 0, True, z).astype(jnp.bfloat16)
        gp1_ref[q] = gpl
        around = [wide_ref[q + 1 + i] for i in range(3)]
        weight_grads(0, gpre, ax1_ref[q + 1], gax, pl1_ref[q + 1], gpl, around, mix_ref, kzg_ref, kxyg_ref, y, z)
        return carry

    lax.fori_loop(0, own, block1, 0)


def vmem_call(kernel, args, outs, scratch=(), smem=0, aliases=None):
    specs = [pl.BlockSpec(memory_space=pltpu.SMEM)] * smem + [pl.BlockSpec(memory_space=pltpu.VMEM)] * (len(args) - smem)
    return pl.pallas_call(
        kernel,
        out_shape=outs,
        in_specs=specs,
        out_specs=[pl.BlockSpec(memory_space=pltpu.VMEM)] * len(outs),
        scratch_shapes=list(scratch),
        input_output_aliases=aliases or {},
        compiler_params=pltpu.CompilerParams(vmem_limit_bytes=VMEM_LIMIT),
    )(*args)


def on_device(volume, cotangent, kernels_xy, kernels_z, mixing):
    _, chans, own, depth, across = volume.shape
    lanes = depth * across
    f32, bf16 = jnp.float32, jnp.bfloat16
    vol = volume[0].reshape(chans, own, lanes).transpose(1, 0, 2)
    cot = cotangent[0].reshape(chans, own, lanes).transpose(1, 0, 2)
    kxy = jnp.broadcast_to(
        kernels_xy.astype(f32).reshape(2, chans, 9).transpose(0, 2, 1)[..., None], (2, 9, chans, 128)
    )
    kz = jnp.broadcast_to(kernels_z.astype(f32).transpose(0, 2, 1)[..., None], (2, 3, chans, 128))
    wt = mixing.transpose(0, 2, 1)
    ranks = lax.axis_size("sp")
    place = lax.axis_index("sp")
    spots = place * own - 1 + jnp.arange(own + 2, dtype=jnp.int32)
    mask = ((spots >= 0) & (spots < own * ranks)).astype(f32)
    wide = halo(vol, 2)
    plane = lambda n, t: jax.ShapeDtypeStruct((n, chans, lanes), t)
    gp2, pre1, ax1, pl1, mix, kzg, kxyg = vmem_call(
        upper_kernel,
        (mask, wide, cot, kxy, kz, mixing, wt),
        (
            plane(own, bf16), plane(own + 2, f32), plane(own + 2, bf16), plane(own + 2, f32),
            jax.ShapeDtypeStruct((2, chans, chans), f32),
            jax.ShapeDtypeStruct((2, 3, chans, 128), f32),
            jax.ShapeDtypeStruct((2, 9, chans, 128), f32),
        ),
        scratch=[pltpu.VMEM((own + 2, chans, lanes), bf16)],
        smem=1,
    )
    gp1, mix, kzg, kxyg = vmem_call(
        lower_kernel,
        (halo(gp2, 1), wide, pre1, ax1, pl1, kxy, kz, mixing, wt, mix, kzg, kxyg),
        (plane(own, bf16), jax.ShapeDtypeStruct((2, chans, chans), f32),
         jax.ShapeDtypeStruct((2, 3, chans, 128), f32), jax.ShapeDtypeStruct((2, 9, chans, 128), f32)),
    )
    kz_sum = kzg.sum(axis=3).transpose(0, 2, 1)
    kxy_sum = kxyg.sum(axis=3).transpose(0, 2, 1).reshape(2, chans, 3, 3)
    summed, grad_in = settle_all((mix, kxy_sum, kz_sum), halo(gp1, 1), kxy)
    grad_in = grad_in.transpose(1, 0, 2).reshape(1, chans, own, depth, across)
    factor = 1.0 / math.sqrt(lax.axis_size("dp") * own * ranks * depth * across)
    return (grad_in, summed[0] * factor, summed[1] * factor, summed[2] * factor)


def solution(mesh):
    return jax.shard_map(
        on_device,
        mesh=mesh,
        in_specs=(P("dp", None, "sp", None, None), P("dp", None, "sp", None, None), P(), P(), P()),
        out_specs=(P("dp", None, "sp", None, None), P(), P(), P()),
        check_vma=False,
    )
```

```python
import functools
import math

import jax
import jax.numpy as jnp
from jax import lax
from jax.experimental import pallas as pl
from jax.experimental.pallas import tpu as pltpu
from jax.sharding import PartitionSpec as P

MESH = pl.DeviceIdType.MESH
VMEM_LIMIT = 56 * 1024 * 1024


def exchange_groups(axes, radix_bits):
    bits = []
    for name, size in axes:
        assert size & (size - 1) == 0
        for b in range(size.bit_length() - 1):
            bits.append((name, 1 << b))
    return [bits[i : i + radix_bits] for i in range(0, len(bits), radix_bits)]


def allreduce_kernel(axes, groups, x_ref, gp1_ref, kxy_ref, o_ref, vg_ref, recv, acc, edge, send_sem, recv_sem, edge_send, edge_recv):
    here = {name: lax.axis_index(name) for name, _ in axes}
    steps = []
    for group in groups:
        partners = []
        for offset in range(1, 1 << len(group)):
            where = dict(here)
            for k, (name, stride) in enumerate(group):
                if (offset >> k) & 1:
                    bit = (where[name] // stride) % 2
                    where[name] = where[name] + stride * (1 - 2 * bit)
            partners.append(tuple(where[n] for n, _ in axes))
        steps.append(partners)
    sp, last = here["sp"], axes[0][1] - 1
    left = tuple(sp - 1 if n == "sp" else here[n] for n, _ in axes)
    right = tuple(sp + 1 if n == "sp" else here[n] for n, _ in axes)
    span = 1 << len(groups[0])
    extra_left = (sp > 0) & (sp % span == 0)
    extra_right = (sp < last) & (sp % span == span - 1)
    barrier = pltpu.get_barrier_semaphore()
    count = 0
    for partners in steps:
        for partner in partners:
            pl.semaphore_signal(barrier, inc=1, device_id=partner, device_id_type=MESH)
            count += 1

    @pl.when(extra_left)
    def _():
        pl.semaphore_signal(barrier, inc=1, device_id=left, device_id_type=MESH)

    @pl.when(extra_right)
    def _():
        pl.semaphore_signal(barrier, inc=1, device_id=right, device_id_type=MESH)

    pl.semaphore_wait(barrier, count + extra_left.astype(jnp.int32) + extra_right.astype(jnp.int32))

    own = vg_ref.shape[0]
    to_left = pltpu.make_async_remote_copy(
        src_ref=gp1_ref.at[0], dst_ref=edge.at[1], send_sem=edge_send.at[0], recv_sem=edge_recv.at[1],
        device_id=left, device_id_type=MESH,
    )
    to_right = pltpu.make_async_remote_copy(
        src_ref=gp1_ref.at[own - 1], dst_ref=edge.at[0], send_sem=edge_send.at[1], recv_sem=edge_recv.at[0],
        device_id=right, device_id_type=MESH,
    )

    @pl.when(sp > 0)
    def _():
        to_left.start()

    @pl.when(sp < last)
    def _():
        to_right.start()

    y, _ = coords(vg_ref.shape[1:])

    def conv_plane(q):
        planes = [edge.at[0] if q == 0 else gp1_ref.at[q - 1], gp1_ref.at[q], edge.at[1] if q == own - 1 else gp1_ref.at[q + 1]]
        vg_ref[q] = plane_conv([p[...] for p in planes], kxy_ref, 0, True, y).astype(vg_ref.dtype)

    order = list(range(1, own - 1)) + [0, own - 1]
    src = x_ref
    copies = []
    slot = 0
    for g, partners in enumerate(steps):
        here_copies = []
        for k, partner in enumerate(partners):
            copy = pltpu.make_async_remote_copy(
                src_ref=src,
                dst_ref=recv.at[slot + k],
                send_sem=send_sem.at[slot + k],
                recv_sem=recv_sem.at[slot + k],
                device_id=partner,
                device_id_type=MESH,
            )
            copy.start()
            here_copies.append(copy)
        todo = order[g * own // len(steps) : (g + 1) * own // len(steps)]
        if 0 in todo:
            @pl.when(sp > 0)
            def _():
                to_right.wait_recv()

            @pl.when(sp == 0)
            def _():
                edge[0] = jnp.zeros(edge.shape[1:], edge.dtype)

        if own - 1 in todo:
            @pl.when(sp < last)
            def _():
                to_left.wait_recv()

            @pl.when(sp == last)
            def _():
                edge[1] = jnp.zeros(edge.shape[1:], edge.dtype)

        for q in todo:
            conv_plane(q)
        for copy in here_copies:
            copy.wait_recv()
        copies += here_copies
        vals = [src[...]] + [recv[slot + k] for k in range(len(partners))]
        while len(vals) > 1:
            vals = [vals[i] + vals[i + 1] for i in range(0, len(vals), 2)]
        dst = o_ref if g == len(steps) - 1 else acc.at[g]
        dst[...] = vals[0]
        src = dst
        slot += len(partners)
    for copy in copies:
        copy.wait_send()

    @pl.when(sp > 0)
    def _():
        to_left.wait_send()

    @pl.when(sp < last)
    def _():
        to_right.wait_send()


def all_sum(flat, gp1, kxy, axes, radix_bits=2):
    groups = exchange_groups(axes, radix_bits)
    slots = sum((1 << len(g)) - 1 for g in groups)
    own = gp1.shape[0]
    assert own >= 2 and own % len(groups) == 0
    return pl.pallas_call(
        functools.partial(allreduce_kernel, axes, groups),
        out_shape=(
            jax.ShapeDtypeStruct(flat.shape, flat.dtype),
            jax.ShapeDtypeStruct((own,) + gp1.shape[1:], gp1.dtype),
        ),
        in_specs=[pl.BlockSpec(memory_space=pltpu.VMEM)] * 3,
        out_specs=[pl.BlockSpec(memory_space=pltpu.VMEM)] * 2,
        scratch_shapes=[
            pltpu.VMEM((slots,) + flat.shape, flat.dtype),
            pltpu.VMEM((len(groups),) + flat.shape, flat.dtype),
            pltpu.VMEM((2,) + gp1.shape[1:], gp1.dtype),
            pltpu.SemaphoreType.DMA((slots,)),
            pltpu.SemaphoreType.DMA((slots,)),
            pltpu.SemaphoreType.DMA((2,)),
            pltpu.SemaphoreType.DMA((2,)),
        ],
        compiler_params=pltpu.CompilerParams(
            collective_id=0, has_side_effects=True, vmem_limit_bytes=VMEM_LIMIT
        ),
    )(flat, gp1, kxy)


def settle_all(parts, gp1, kxy):
    flat = jnp.concatenate([p.reshape(-1) for p in parts])
    rows = -(-flat.shape[0] // 1024) * 8
    flat = jnp.pad(flat, (0, rows * 128 - flat.shape[0])).reshape(rows, 128)
    axes = (("sp", lax.axis_size("sp")), ("dp", lax.axis_size("dp")))
    flat, grad_in = all_sum(flat, gp1, kxy, axes)
    flat = flat.reshape(-1)
    summed, at = [], 0
    for p in parts:
        summed.append(flat[at : at + p.size].reshape(p.shape))
        at += p.size
    return summed, grad_in


def halo(x, width):
    count = lax.axis_size("sp")
    up = [(i, i + 1) for i in range(count - 1)]
    down = [(j, i) for i, j in up]
    before = lax.ppermute(x[x.shape[0] - width :], "sp", up)
    after = lax.ppermute(x[:width], "sp", down)
    return jnp.concatenate([before, x, after], axis=0)


def coords(shape):
    lane = lax.broadcasted_iota(jnp.int32, shape, 1)
    return jnp.bitwise_and(lane, 127), jnp.right_shift(lane, 7)


def at_y(a, d, y):
    if d == 0:
        return a
    rolled = pltpu.roll(a, (-d) % a.shape[1], 1)
    return jnp.where((y + d >= 0) & (y + d < 128), rolled, 0.0)


def at_z(a, d, z):
    if d == 0:
        return a
    rolled = pltpu.roll(a, (-128 * d) % a.shape[1], 1)
    return jnp.where((z + d >= 0) & (z + d < a.shape[1] // 128), rolled, 0.0)


def widen(k, lanes):
    return jnp.concatenate([k] * (lanes // k.shape[1]), axis=1)


def fold(a):
    total = a[:, :128]
    for g in range(1, a.shape[1] // 128):
        total = total + a[:, g * 128 : (g + 1) * 128]
    return total


def sigmoid(u):
    return 1.0 / (1.0 + jnp.exp(-u))


def plane_conv(planes, k_ref, b, flip, y):
    lanes = planes[0].shape[1]
    total = None
    for i in range(3):
        src = planes[i].astype(jnp.float32)
        for j in range(3):
            tap = (2 - i) * 3 + (2 - j) if flip else i * 3 + j
            term = widen(k_ref[b, tap], lanes) * at_y(src, j - 1, y)
            total = term if total is None else total + term
    return total


def depth_conv(a, kz_ref, b, flip, z):
    lanes = a.shape[1]
    total = None
    for t in range(3):
        tap = 2 - t if flip else t
        term = widen(kz_ref[b, tap], lanes) * at_z(a, t - 1, z)
        total = term if total is None else total + term
    return total


def silu_grad(g, pre):
    s = sigmoid(pre)
    return (g * (s * (1.0 + pre * (1.0 - s)))).astype(jnp.bfloat16)


def weight_grads(b, gpre, ax, gax, pl, gpl, around, mix_ref, kzg_ref, kxyg_ref, y, z):
    mix_ref[b] += lax.dot_general(
        gpre, ax, (((1,), (1,)), ((), ())), preferred_element_type=jnp.float32
    )
    for t in range(3):
        kzg_ref[b, t] += fold(gax * at_z(pl, t - 1, z))
    gplf = gpl.astype(jnp.float32)
    for i in range(3):
        src = around[i].astype(jnp.float32)
        for j in range(3):
            kxyg_ref[b, i * 3 + j] += fold(gplf * at_y(src, j - 1, y))


def upper_kernel(mask_ref, wide_ref, cot_ref, kxy_ref, kz_ref, w_ref, wt_ref,
                 gp2_ref, pre1_ref, ax1_ref, pl1_ref, mix_ref, kzg_ref, kxyg_ref, h2_ref):
    own = cot_ref.shape[0]
    y, z = coords(cot_ref.shape[1:])
    mix_ref[...] = jnp.zeros_like(mix_ref)
    kzg_ref[...] = jnp.zeros_like(kzg_ref)
    kxyg_ref[...] = jnp.zeros_like(kxyg_ref)

    def forward1(p, carry):
        planar = plane_conv([wide_ref[p + i] for i in range(3)], kxy_ref, 0, False, y)
        axial = depth_conv(planar, kz_ref, 0, False, z).astype(jnp.bfloat16)
        pre = jnp.dot(w_ref[0], axial, preferred_element_type=jnp.float32)
        pl1_ref[p] = planar
        ax1_ref[p] = axial
        pre1_ref[p] = pre
        h2_ref[p] = (pre * sigmoid(pre) * mask_ref[p]).astype(jnp.bfloat16)
        return carry

    lax.fori_loop(0, own + 2, forward1, 0)

    def block2(q, carry):
        around = [h2_ref[q + i] for i in range(3)]
        planar = plane_conv(around, kxy_ref, 1, False, y)
        axial = depth_conv(planar, kz_ref, 1, False, z).astype(jnp.bfloat16)
        pre = jnp.dot(w_ref[1], axial, preferred_element_type=jnp.float32)
        gpre = silu_grad(cot_ref[q].astype(jnp.float32), pre)
        gax = jnp.dot(wt_ref[1], gpre, preferred_element_type=jnp.float32)
        gpl = depth_conv(gax, kz_ref, 1, True, z).astype(jnp.bfloat16)
        gp2_ref[q] = gpl
        weight_grads(1, gpre, axial, gax, planar, gpl, around, mix_ref, kzg_ref, kxyg_ref, y, z)
        return carry

    lax.fori_loop(0, own, block2, 0)


def lower_kernel(gp2_ref, wide_ref, pre1_ref, ax1_ref, pl1_ref, kxy_ref, kz_ref, w_ref, wt_ref, mix_in, kzg_in, kxyg_in,
                 gp1_ref, mix_ref, kzg_ref, kxyg_ref):
    own = gp1_ref.shape[0]
    y, z = coords(gp1_ref.shape[1:])
    mix_ref[...] = mix_in[...]
    kzg_ref[...] = kzg_in[...]
    kxyg_ref[...] = kxyg_in[...]

    def block1(q, carry):
        g1 = plane_conv([gp2_ref[q + i] for i in range(3)], kxy_ref, 1, True, y).astype(jnp.bfloat16)
        gpre = silu_grad(g1.astype(jnp.float32), pre1_ref[q + 1])
        gax = jnp.dot(wt_ref[0], gpre, preferred_element_type=jnp.float32)
        gpl = depth_conv(gax, kz_ref, 0, True, z).astype(jnp.bfloat16)
        gp1_ref[q] = gpl
        around = [wide_ref[q + 1 + i] for i in range(3)]
        weight_grads(0, gpre, ax1_ref[q + 1], gax, pl1_ref[q + 1], gpl, around, mix_ref, kzg_ref, kxyg_ref, y, z)
        return carry

    lax.fori_loop(0, own, block1, 0)


def vmem_call(kernel, args, outs, scratch=(), smem=0, aliases=None):
    specs = [pl.BlockSpec(memory_space=pltpu.SMEM)] * smem + [pl.BlockSpec(memory_space=pltpu.VMEM)] * (len(args) - smem)
    return pl.pallas_call(
        kernel,
        out_shape=outs,
        in_specs=specs,
        out_specs=[pl.BlockSpec(memory_space=pltpu.VMEM)] * len(outs),
        scratch_shapes=list(scratch),
        input_output_aliases=aliases or {},
        compiler_params=pltpu.CompilerParams(vmem_limit_bytes=VMEM_LIMIT),
    )(*args)


def on_device(volume, cotangent, kernels_xy, kernels_z, mixing):
    _, chans, own, depth, across = volume.shape
    lanes = depth * across
    f32, bf16 = jnp.float32, jnp.bfloat16
    vol = volume[0].reshape(chans, own, lanes).transpose(1, 0, 2)
    cot = cotangent[0].reshape(chans, own, lanes).transpose(1, 0, 2)
    kxy = jnp.broadcast_to(
        kernels_xy.astype(f32).reshape(2, chans, 9).transpose(0, 2, 1)[..., None], (2, 9, chans, 128)
    )
    kz = jnp.broadcast_to(kernels_z.astype(f32).transpose(0, 2, 1)[..., None], (2, 3, chans, 128))
    wt = mixing.transpose(0, 2, 1)
    ranks = lax.axis_size("sp")
    place = lax.axis_index("sp")
    spots = place * own - 1 + jnp.arange(own + 2, dtype=jnp.int32)
    mask = ((spots >= 0) & (spots < own * ranks)).astype(f32)
    wide = halo(vol, 2)
    plane = lambda n, t: jax.ShapeDtypeStruct((n, chans, lanes), t)
    gp2, pre1, ax1, pl1, mix, kzg, kxyg = vmem_call(
        upper_kernel,
        (mask, wide, cot, kxy, kz, mixing, wt),
        (
            plane(own, bf16), plane(own + 2, f32), plane(own + 2, bf16), plane(own + 2, f32),
            jax.ShapeDtypeStruct((2, chans, chans), f32),
            jax.ShapeDtypeStruct((2, 3, chans, 128), f32),
            jax.ShapeDtypeStruct((2, 9, chans, 128), f32),
        ),
        scratch=[pltpu.VMEM((own + 2, chans, lanes), bf16)],
        smem=1,
    )
    gp1, mix, kzg, kxyg = vmem_call(
        lower_kernel,
        (halo(gp2, 1), wide, pre1, ax1, pl1, kxy, kz, mixing, wt, mix, kzg, kxyg),
        (plane(own, bf16), jax.ShapeDtypeStruct((2, chans, chans), f32),
         jax.ShapeDtypeStruct((2, 3, chans, 128), f32), jax.ShapeDtypeStruct((2, 9, chans, 128), f32)),
    )
    kz_sum = kzg.sum(axis=3).transpose(0, 2, 1)
    kxy_sum = kxyg.sum(axis=3).transpose(0, 2, 1).reshape(2, chans, 3, 3)
    summed, grad_in = settle_all((mix, kxy_sum, kz_sum), gp1, kxy)
    grad_in = grad_in.transpose(1, 0, 2).reshape(1, chans, own, depth, across)
    factor = 1.0 / math.sqrt(lax.axis_size("dp") * own * ranks * depth * across)
    return (grad_in, summed[0] * factor, summed[1] * factor, summed[2] * factor)


def solution(mesh):
    return jax.shard_map(
        on_device,
        mesh=mesh,
        in_specs=(P("dp", None, "sp", None, None), P("dp", None, "sp", None, None), P(), P(), P()),
        out_specs=(P("dp", None, "sp", None, None), P(), P(), P()),
        check_vma=False,
    )
```

```python
import functools
import math

import jax
import jax.numpy as jnp
from jax import lax
from jax.experimental import pallas as pl
from jax.experimental.pallas import tpu as pltpu
from jax.sharding import PartitionSpec as P

MESH = pl.DeviceIdType.MESH
VMEM_LIMIT = 56 * 1024 * 1024


def exchange_groups(axes, radix_bits):
    bits = []
    for name, size in axes:
        assert size & (size - 1) == 0
        for b in range(size.bit_length() - 1):
            bits.append((name, 1 << b))
    return [bits[i : i + radix_bits] for i in range(0, len(bits), radix_bits)]


def allreduce_kernel(axes, groups, x_ref, gp1_ref, kxy_ref, o_ref, vg_ref, recv, acc, edge, send_sem, recv_sem, edge_send, edge_recv):
    here = {name: lax.axis_index(name) for name, _ in axes}
    steps = []
    for group in groups:
        partners = []
        for offset in range(1, 1 << len(group)):
            where = dict(here)
            for k, (name, stride) in enumerate(group):
                if (offset >> k) & 1:
                    bit = (where[name] // stride) % 2
                    where[name] = where[name] + stride * (1 - 2 * bit)
            partners.append(tuple(where[n] for n, _ in axes))
        steps.append(partners)
    sp, last = here["sp"], axes[0][1] - 1
    left = tuple(sp - 1 if n == "sp" else here[n] for n, _ in axes)
    right = tuple(sp + 1 if n == "sp" else here[n] for n, _ in axes)
    span = 1 << len(groups[0])
    extra_left = (sp > 0) & (sp % span == 0)
    extra_right = (sp < last) & (sp % span == span - 1)
    barrier = pltpu.get_barrier_semaphore()
    count = 0
    for partners in steps:
        for partner in partners:
            pl.semaphore_signal(barrier, inc=1, device_id=partner, device_id_type=MESH)
            count += 1

    @pl.when(extra_left)
    def _():
        pl.semaphore_signal(barrier, inc=1, device_id=left, device_id_type=MESH)

    @pl.when(extra_right)
    def _():
        pl.semaphore_signal(barrier, inc=1, device_id=right, device_id_type=MESH)

    pl.semaphore_wait(barrier, count + extra_left.astype(jnp.int32) + extra_right.astype(jnp.int32))

    own = vg_ref.shape[0]
    to_left = pltpu.make_async_remote_copy(
        src_ref=gp1_ref.at[0], dst_ref=edge.at[1], send_sem=edge_send.at[0], recv_sem=edge_recv.at[1],
        device_id=left, device_id_type=MESH,
    )
    to_right = pltpu.make_async_remote_copy(
        src_ref=gp1_ref.at[own - 1], dst_ref=edge.at[0], send_sem=edge_send.at[1], recv_sem=edge_recv.at[0],
        device_id=right, device_id_type=MESH,
    )

    @pl.when(sp > 0)
    def _():
        to_left.start()

    @pl.when(sp < last)
    def _():
        to_right.start()

    y, _ = coords(vg_ref.shape[1:])

    def conv_plane(q):
        planes = [edge.at[0] if q == 0 else gp1_ref.at[q - 1], gp1_ref.at[q], edge.at[1] if q == own - 1 else gp1_ref.at[q + 1]]
        vg_ref[q] = plane_conv([p[...] for p in planes], kxy_ref, 0, True, y).astype(vg_ref.dtype)

    order = list(range(1, own - 1)) + [0, own - 1]
    src = x_ref
    copies = []
    slot = 0
    for g, partners in enumerate(steps):
        here_copies = []
        for k, partner in enumerate(partners):
            copy = pltpu.make_async_remote_copy(
                src_ref=src,
                dst_ref=recv.at[slot + k],
                send_sem=send_sem.at[slot + k],
                recv_sem=recv_sem.at[slot + k],
                device_id=partner,
                device_id_type=MESH,
            )
            copy.start()
            here_copies.append(copy)
        todo = order[g * own // len(steps) : (g + 1) * own // len(steps)]
        if 0 in todo:
            @pl.when(sp > 0)
            def _():
                to_right.wait_recv()

            @pl.when(sp == 0)
            def _():
                edge[0] = jnp.zeros(edge.shape[1:], edge.dtype)

        if own - 1 in todo:
            @pl.when(sp < last)
            def _():
                to_left.wait_recv()

            @pl.when(sp == last)
            def _():
                edge[1] = jnp.zeros(edge.shape[1:], edge.dtype)

        for q in todo:
            conv_plane(q)
        for copy in here_copies:
            copy.wait_recv()
        copies += here_copies
        vals = [src[...]] + [recv[slot + k] for k in range(len(partners))]
        while len(vals) > 1:
            vals = [vals[i] + vals[i + 1] for i in range(0, len(vals), 2)]
        dst = o_ref if g == len(steps) - 1 else acc.at[g]
        dst[...] = vals[0]
        src = dst
        slot += len(partners)
    for copy in copies:
        copy.wait_send()

    @pl.when(sp > 0)
    def _():
        to_left.wait_send()

    @pl.when(sp < last)
    def _():
        to_right.wait_send()


def all_sum(flat, gp1, kxy, axes, radix_bits=2):
    groups = exchange_groups(axes, radix_bits)
    slots = sum((1 << len(g)) - 1 for g in groups)
    own = gp1.shape[0]
    assert own >= 2 and own % len(groups) == 0
    return pl.pallas_call(
        functools.partial(allreduce_kernel, axes, groups),
        out_shape=(
            jax.ShapeDtypeStruct(flat.shape, flat.dtype),
            jax.ShapeDtypeStruct((own,) + gp1.shape[1:], gp1.dtype),
        ),
        in_specs=[pl.BlockSpec(memory_space=pltpu.VMEM)] * 3,
        out_specs=[pl.BlockSpec(memory_space=pltpu.VMEM)] * 2,
        scratch_shapes=[
            pltpu.VMEM((slots,) + flat.shape, flat.dtype),
            pltpu.VMEM((len(groups),) + flat.shape, flat.dtype),
            pltpu.VMEM((2,) + gp1.shape[1:], gp1.dtype),
            pltpu.SemaphoreType.DMA((slots,)),
            pltpu.SemaphoreType.DMA((slots,)),
            pltpu.SemaphoreType.DMA((2,)),
            pltpu.SemaphoreType.DMA((2,)),
        ],
        compiler_params=pltpu.CompilerParams(
            collective_id=0, has_side_effects=True, vmem_limit_bytes=VMEM_LIMIT
        ),
    )(flat, gp1, kxy)


def settle_all(parts, gp1, kxy):
    flat = jnp.concatenate([p.reshape(-1) for p in parts])
    rows = -(-flat.shape[0] // 1024) * 8
    flat = jnp.pad(flat, (0, rows * 128 - flat.shape[0])).reshape(rows, 128)
    axes = (("sp", lax.axis_size("sp")), ("dp", lax.axis_size("dp")))
    flat, grad_in = all_sum(flat, gp1, kxy, axes)
    flat = flat.reshape(-1)
    summed, at = [], 0
    for p in parts:
        summed.append(flat[at : at + p.size].reshape(p.shape))
        at += p.size
    return summed, grad_in


def coords(shape):
    lane = lax.broadcasted_iota(jnp.int32, shape, 1)
    return jnp.bitwise_and(lane, 127), jnp.right_shift(lane, 7)


def at_y(a, d, y):
    if d == 0:
        return a
    rolled = pltpu.roll(a, (-d) % a.shape[1], 1)
    return jnp.where((y + d >= 0) & (y + d < 128), rolled, 0.0)


def at_z(a, d, z):
    if d == 0:
        return a
    rolled = pltpu.roll(a, (-128 * d) % a.shape[1], 1)
    return jnp.where((z + d >= 0) & (z + d < a.shape[1] // 128), rolled, 0.0)


def widen(k, lanes):
    return jnp.concatenate([k] * (lanes // k.shape[1]), axis=1)


def fold(a):
    total = a[:, :128]
    for g in range(1, a.shape[1] // 128):
        total = total + a[:, g * 128 : (g + 1) * 128]
    return total


def sigmoid(u):
    return 1.0 / (1.0 + jnp.exp(-u))


def plane_conv(planes, k_ref, b, flip, y):
    lanes = planes[0].shape[1]
    total = None
    for i in range(3):
        src = planes[i].astype(jnp.float32)
        for j in range(3):
            tap = (2 - i) * 3 + (2 - j) if flip else i * 3 + j
            term = widen(k_ref[b, tap], lanes) * at_y(src, j - 1, y)
            total = term if total is None else total + term
    return total


def depth_conv(a, kz_ref, b, flip, z):
    lanes = a.shape[1]
    total = None
    for t in range(3):
        tap = 2 - t if flip else t
        term = widen(kz_ref[b, tap], lanes) * at_z(a, t - 1, z)
        total = term if total is None else total + term
    return total


def silu_grad(g, pre):
    s = sigmoid(pre)
    return (g * (s * (1.0 + pre * (1.0 - s)))).astype(jnp.bfloat16)


def weight_grads(b, gpre, ax, gax, pl, gpl, around, mix_ref, kzg_ref, kxyg_ref, y, z):
    mix_ref[b] += lax.dot_general(
        gpre, ax, (((1,), (1,)), ((), ())), preferred_element_type=jnp.float32
    )
    for t in range(3):
        kzg_ref[b, t] += fold(gax * at_z(pl, t - 1, z))
    gplf = gpl.astype(jnp.float32)
    for i in range(3):
        src = around[i].astype(jnp.float32)
        for j in range(3):
            kxyg_ref[b, i * 3 + j] += fold(gplf * at_y(src, j - 1, y))


def fused_kernel(mask_ref, vol_ref, cot_ref, kxy_ref, kz_ref, w_ref, wt_ref,
                 gp1_ref, mix_ref, kzg_ref, kxyg_ref,
                 wide, h2, pl1, ax1, pre1, gp2, in_send, in_recv, g_send, g_recv):
    own = cot_ref.shape[0]
    y, z = coords(cot_ref.shape[1:])
    sp, last, dp = lax.axis_index("sp"), lax.axis_size("sp") - 1, lax.axis_index("dp")
    left, right = (sp - 1, dp), (sp + 1, dp)
    has_left, has_right = sp > 0, sp < last

    barrier = pltpu.get_barrier_semaphore()

    @pl.when(has_left)
    def _():
        pl.semaphore_signal(barrier, inc=1, device_id=left, device_id_type=MESH)

    @pl.when(has_right)
    def _():
        pl.semaphore_signal(barrier, inc=1, device_id=right, device_id_type=MESH)

    pl.semaphore_wait(barrier, has_left.astype(jnp.int32) + has_right.astype(jnp.int32))

    def exchange(buf, first, count, send, recv, src, src_first):
        to_left = pltpu.make_async_remote_copy(
            src_ref=src.at[pl.ds(src_first, count)], dst_ref=buf.at[pl.ds(first + own, count)],
            send_sem=send.at[0], recv_sem=recv.at[1], device_id=left, device_id_type=MESH,
        )
        to_right = pltpu.make_async_remote_copy(
            src_ref=src.at[pl.ds(src_first + own - count, count)], dst_ref=buf.at[pl.ds(first - count, count)],
            send_sem=send.at[1], recv_sem=recv.at[0], device_id=right, device_id_type=MESH,
        )
        pl.when(has_left)(to_left.start)
        pl.when(has_right)(to_right.start)

        def finish():
            pl.when(has_left)(to_right.wait_recv)
            pl.when(has_right)(to_left.wait_recv)
            zeros = jnp.zeros((count,) + buf.shape[1:], buf.dtype)

            @pl.when(sp == 0)
            def _():
                buf[pl.ds(first - count, count)] = zeros

            @pl.when(sp == last)
            def _():
                buf[pl.ds(first + own, count)] = zeros

        def drain():
            pl.when(has_left)(to_left.wait_send)
            pl.when(has_right)(to_right.wait_send)

        return finish, drain

    mix_ref[...] = jnp.zeros_like(mix_ref)
    kzg_ref[...] = jnp.zeros_like(kzg_ref)
    kxyg_ref[...] = jnp.zeros_like(kxyg_ref)

    finish_in, drain_in = exchange(wide, 2, 2, in_send, in_recv, vol_ref, 0)
    wide[pl.ds(2, own)] = vol_ref[...]

    def forward1(p):
        planar = plane_conv([wide[p + i] for i in range(3)], kxy_ref, 0, False, y)
        axial = depth_conv(planar, kz_ref, 0, False, z).astype(jnp.bfloat16)
        pre = jnp.dot(w_ref[0], axial, preferred_element_type=jnp.float32)
        pl1[p] = planar
        ax1[p] = axial
        pre1[p] = pre
        h2[p] = (pre * sigmoid(pre) * mask_ref[p]).astype(jnp.bfloat16)

    def block2(q):
        around = [h2[q + i] for i in range(3)]
        planar = plane_conv(around, kxy_ref, 1, False, y)
        axial = depth_conv(planar, kz_ref, 1, False, z).astype(jnp.bfloat16)
        pre = jnp.dot(w_ref[1], axial, preferred_element_type=jnp.float32)
        gpre = silu_grad(cot_ref[q].astype(jnp.float32), pre)
        gax = jnp.dot(wt_ref[1], gpre, preferred_element_type=jnp.float32)
        gpl = depth_conv(gax, kz_ref, 1, True, z).astype(jnp.bfloat16)
        gp2[q + 1] = gpl
        weight_grads(1, gpre, axial, gax, planar, gpl, around, mix_ref, kzg_ref, kxyg_ref, y, z)

    def block1(q):
        g1 = plane_conv([gp2[q + i] for i in range(3)], kxy_ref, 1, True, y).astype(jnp.bfloat16)
        gpre = silu_grad(g1.astype(jnp.float32), pre1[q + 1])
        gax = jnp.dot(wt_ref[0], gpre, preferred_element_type=jnp.float32)
        gpl = depth_conv(gax, kz_ref, 0, True, z).astype(jnp.bfloat16)
        gp1_ref[q] = gpl
        around = [wide[q + 1 + i] for i in range(3)]
        weight_grads(0, gpre, ax1[q + 1], gax, pl1[q + 1], gpl, around, mix_ref, kzg_ref, kxyg_ref, y, z)

    def run(body, lo, hi, place=lambda i: i):
        def step(i, carry):
            body(place(i))
            return carry

        lax.fori_loop(lo, hi, step, 0)

    run(forward1, 2, own)
    finish_in()
    run(forward1, 0, 4, lambda i: i + (i // 2) * (own - 2))
    run(block2, 0, 2, lambda i: i * (own - 1))
    finish_g, drain_g = exchange(gp2, 1, 1, g_send, g_recv, gp2, 1)
    run(block2, 1, own - 1)
    run(block1, 1, own - 1)
    finish_g()
    run(block1, 0, 2, lambda i: i * (own - 1))
    drain_in()
    drain_g()


def on_device(volume, cotangent, kernels_xy, kernels_z, mixing):
    _, chans, own, depth, across = volume.shape
    lanes = depth * across
    f32, bf16 = jnp.float32, jnp.bfloat16
    vol = volume[0].reshape(chans, own, lanes).transpose(1, 0, 2)
    cot = cotangent[0].reshape(chans, own, lanes).transpose(1, 0, 2)
    kxy = jnp.broadcast_to(
        kernels_xy.astype(f32).reshape(2, chans, 9).transpose(0, 2, 1)[..., None], (2, 9, chans, 128)
    )
    kz = jnp.broadcast_to(kernels_z.astype(f32).transpose(0, 2, 1)[..., None], (2, 3, chans, 128))
    wt = mixing.transpose(0, 2, 1)
    ranks = lax.axis_size("sp")
    place = lax.axis_index("sp")
    spots = place * own - 1 + jnp.arange(own + 2, dtype=jnp.int32)
    mask = ((spots >= 0) & (spots < own * ranks)).astype(f32)
    plane = lambda n, t: jax.ShapeDtypeStruct((n, chans, lanes), t)
    gp1, mix, kzg, kxyg = pl.pallas_call(
        fused_kernel,
        out_shape=(
            plane(own, bf16),
            jax.ShapeDtypeStruct((2, chans, chans), f32),
            jax.ShapeDtypeStruct((2, 3, chans, 128), f32),
            jax.ShapeDtypeStruct((2, 9, chans, 128), f32),
        ),
        in_specs=[pl.BlockSpec(memory_space=pltpu.SMEM)] + [pl.BlockSpec(memory_space=pltpu.VMEM)] * 6,
        out_specs=[pl.BlockSpec(memory_space=pltpu.VMEM)] * 4,
        scratch_shapes=[
            pltpu.VMEM((own + 4, chans, lanes), bf16),
            pltpu.VMEM((own + 2, chans, lanes), bf16),
            pltpu.VMEM((own + 2, chans, lanes), f32),
            pltpu.VMEM((own + 2, chans, lanes), bf16),
            pltpu.VMEM((own + 2, chans, lanes), f32),
            pltpu.VMEM((own + 2, chans, lanes), bf16),
        ] + [pltpu.SemaphoreType.DMA((2,))] * 4,
        compiler_params=pltpu.CompilerParams(
            collective_id=1, has_side_effects=True, vmem_limit_bytes=VMEM_LIMIT
        ),
    )(mask, vol, cot, kxy, kz, mixing, wt)
    kz_sum = kzg.sum(axis=3).transpose(0, 2, 1)
    kxy_sum = kxyg.sum(axis=3).transpose(0, 2, 1).reshape(2, chans, 3, 3)
    summed, grad_in = settle_all((mix, kxy_sum, kz_sum), gp1, kxy)
    grad_in = grad_in.transpose(1, 0, 2).reshape(1, chans, own, depth, across)
    factor = 1.0 / math.sqrt(lax.axis_size("dp") * own * ranks * depth * across)
    return (grad_in, summed[0] * factor, summed[1] * factor, summed[2] * factor)


def solution(mesh):
    return jax.shard_map(
        on_device,
        mesh=mesh,
        in_specs=(P("dp", None, "sp", None, None), P("dp", None, "sp", None, None), P(), P(), P()),
        out_specs=(P("dp", None, "sp", None, None), P(), P(), P()),
        check_vma=False,
    )
```

```python
import functools
import math

import jax
import jax.numpy as jnp
from jax import lax
from jax.experimental import pallas as pl
from jax.experimental.pallas import tpu as pltpu
from jax.sharding import PartitionSpec as P

MESH = pl.DeviceIdType.MESH
VMEM_LIMIT = 56 * 1024 * 1024


def exchange_groups(axes, radix_bits):
    bits = []
    for name, size in axes:
        assert size & (size - 1) == 0
        for b in range(size.bit_length() - 1):
            bits.append((name, 1 << b))
    return [bits[i : i + radix_bits] for i in range(0, len(bits), radix_bits)]


def coords(shape):
    lane = lax.broadcasted_iota(jnp.int32, shape, 1)
    return jnp.bitwise_and(lane, 127), jnp.right_shift(lane, 7)


def at_y(a, d, y):
    if d == 0:
        return a
    rolled = pltpu.roll(a, (-d) % a.shape[1], 1)
    return jnp.where((y + d >= 0) & (y + d < 128), rolled, 0.0)


def at_z(a, d, z):
    if d == 0:
        return a
    rolled = pltpu.roll(a, (-128 * d) % a.shape[1], 1)
    return jnp.where((z + d >= 0) & (z + d < a.shape[1] // 128), rolled, 0.0)


def widen(k, lanes):
    return jnp.concatenate([k] * (lanes // k.shape[1]), axis=1)


def fold(a):
    total = a[:, :128]
    for g in range(1, a.shape[1] // 128):
        total = total + a[:, g * 128 : (g + 1) * 128]
    return total


def sigmoid(u):
    return 1.0 / (1.0 + jnp.exp(-u))


def plane_conv(planes, k_ref, b, flip, y):
    lanes = planes[0].shape[1]
    total = None
    for i in range(3):
        src = planes[i].astype(jnp.float32)
        for j in range(3):
            tap = (2 - i) * 3 + (2 - j) if flip else i * 3 + j
            term = widen(k_ref[b, tap], lanes) * at_y(src, j - 1, y)
            total = term if total is None else total + term
    return total


def depth_conv(a, kz_ref, b, flip, z):
    lanes = a.shape[1]
    total = None
    for t in range(3):
        tap = 2 - t if flip else t
        term = widen(kz_ref[b, tap], lanes) * at_z(a, t - 1, z)
        total = term if total is None else total + term
    return total


def silu_grad(g, pre):
    s = sigmoid(pre)
    return (g * (s * (1.0 + pre * (1.0 - s)))).astype(jnp.bfloat16)


def weight_grads(b, gpre, ax, gax, pl, gpl, around, mix_ref, kzg_ref, kxyg_ref, y, z):
    mix_ref[b] += lax.dot_general(
        gpre, ax, (((1,), (1,)), ((), ())), preferred_element_type=jnp.float32
    )
    for t in range(3):
        kzg_ref[b, t] += fold(gax * at_z(pl, t - 1, z))
    gplf = gpl.astype(jnp.float32)
    for i in range(3):
        src = around[i].astype(jnp.float32)
        for j in range(3):
            kxyg_ref[b, i * 3 + j] += fold(gplf * at_y(src, j - 1, y))


def whole_kernel(axes, groups, factor, mask_ref, vol_ref, cot_ref, kxy_ref, kz_ref, w_ref, wt_ref,
                 vg_ref, sums_ref,
                 wide, h2, pl1, ax1, pre1, gp2, gp1, pay, mix_ref, kzg_ref, kxyg_ref, recv, acc,
                 in_send, in_recv, g_send, g_recv, e_send, e_recv, send_sem, recv_sem):
    own = cot_ref.shape[0]
    y, z = coords(cot_ref.shape[1:])
    here = {name: lax.axis_index(name) for name, _ in axes}
    steps = []
    for group in groups:
        partners = []
        for offset in range(1, 1 << len(group)):
            where = dict(here)
            for k, (name, stride) in enumerate(group):
                if (offset >> k) & 1:
                    bit = (where[name] // stride) % 2
                    where[name] = where[name] + stride * (1 - 2 * bit)
            partners.append(tuple(where[n] for n, _ in axes))
        steps.append(partners)
    sp, last, dp = here["sp"], axes[0][1] - 1, here["dp"]
    left, right = (sp - 1, dp), (sp + 1, dp)
    has_left, has_right = sp > 0, sp < last
    span = 1 << len(groups[0])
    extra_left = has_left & (sp % span == 0)
    extra_right = has_right & (sp % span == span - 1)

    barrier = pltpu.get_barrier_semaphore()
    count = 0
    for partners in steps:
        for partner in partners:
            pl.semaphore_signal(barrier, inc=1, device_id=partner, device_id_type=MESH)
            count += 1

    @pl.when(extra_left)
    def _():
        pl.semaphore_signal(barrier, inc=1, device_id=left, device_id_type=MESH)

    @pl.when(extra_right)
    def _():
        pl.semaphore_signal(barrier, inc=1, device_id=right, device_id_type=MESH)

    pl.semaphore_wait(barrier, count + extra_left.astype(jnp.int32) + extra_right.astype(jnp.int32))

    def exchange(buf, first, count, send, recv, src, src_first):
        to_left = pltpu.make_async_remote_copy(
            src_ref=src.at[pl.ds(src_first, count)], dst_ref=buf.at[pl.ds(first + own, count)],
            send_sem=send.at[0], recv_sem=recv.at[1], device_id=left, device_id_type=MESH,
        )
        to_right = pltpu.make_async_remote_copy(
            src_ref=src.at[pl.ds(src_first + own - count, count)], dst_ref=buf.at[pl.ds(first - count, count)],
            send_sem=send.at[1], recv_sem=recv.at[0], device_id=right, device_id_type=MESH,
        )
        pl.when(has_left)(to_left.start)
        pl.when(has_right)(to_right.start)

        def finish():
            pl.when(has_left)(to_right.wait_recv)
            pl.when(has_right)(to_left.wait_recv)
            zeros = jnp.zeros((count,) + buf.shape[1:], buf.dtype)

            @pl.when(sp == 0)
            def _():
                buf[pl.ds(first - count, count)] = zeros

            @pl.when(sp == last)
            def _():
                buf[pl.ds(first + own, count)] = zeros

        def drain():
            pl.when(has_left)(to_left.wait_send)
            pl.when(has_right)(to_right.wait_send)

        return finish, drain

    mix_ref[...] = jnp.zeros_like(mix_ref)
    kzg_ref[...] = jnp.zeros_like(kzg_ref)
    kxyg_ref[...] = jnp.zeros_like(kxyg_ref)

    finish_in, drain_in = exchange(wide, 2, 2, in_send, in_recv, vol_ref, 0)
    wide[pl.ds(2, own)] = vol_ref[...]

    def forward1(p):
        planar = plane_conv([wide[p + i] for i in range(3)], kxy_ref, 0, False, y)
        axial = depth_conv(planar, kz_ref, 0, False, z).astype(jnp.bfloat16)
        pre = jnp.dot(w_ref[0], axial, preferred_element_type=jnp.float32)
        pl1[p] = planar
        ax1[p] = axial
        pre1[p] = pre
        h2[p] = (pre * sigmoid(pre) * mask_ref[p]).astype(jnp.bfloat16)

    def block2(q):
        around = [h2[q + i] for i in range(3)]
        planar = plane_conv(around, kxy_ref, 1, False, y)
        axial = depth_conv(planar, kz_ref, 1, False, z).astype(jnp.bfloat16)
        pre = jnp.dot(w_ref[1], axial, preferred_element_type=jnp.float32)
        gpre = silu_grad(cot_ref[q].astype(jnp.float32), pre)
        gax = jnp.dot(wt_ref[1], gpre, preferred_element_type=jnp.float32)
        gpl = depth_conv(gax, kz_ref, 1, True, z).astype(jnp.bfloat16)
        gp2[q + 1] = gpl
        weight_grads(1, gpre, axial, gax, planar, gpl, around, mix_ref, kzg_ref, kxyg_ref, y, z)

    def block1(q):
        g1 = plane_conv([gp2[q + i] for i in range(3)], kxy_ref, 1, True, y).astype(jnp.bfloat16)
        gpre = silu_grad(g1.astype(jnp.float32), pre1[q + 1])
        gax = jnp.dot(wt_ref[0], gpre, preferred_element_type=jnp.float32)
        gpl = depth_conv(gax, kz_ref, 0, True, z).astype(jnp.bfloat16)
        gp1[q + 1] = gpl
        around = [wide[q + 1 + i] for i in range(3)]
        weight_grads(0, gpre, ax1[q + 1], gax, pl1[q + 1], gpl, around, mix_ref, kzg_ref, kxyg_ref, y, z)

    def run(body, lo, hi, place=lambda i: i):
        def step(i, carry):
            body(place(i))
            return carry

        lax.fori_loop(lo, hi, step, 0)

    run(forward1, 2, own)
    finish_in()
    run(forward1, 0, 4, lambda i: i + (i // 2) * (own - 2))
    run(block2, 0, 2, lambda i: i * (own - 1))
    finish_g, drain_g = exchange(gp2, 1, 1, g_send, g_recv, gp2, 1)
    run(block2, 1, own - 1)
    run(block1, 1, own - 1)
    finish_g()
    run(block1, 0, 2, lambda i: i * (own - 1))
    finish_e, drain_e = exchange(gp1, 1, 1, e_send, e_recv, gp1, 1)
    drain_in()
    drain_g()

    lane = lax.broadcasted_iota(jnp.int32, pay.shape[1:], 1)
    chans = pay.shape[1]
    for b in range(2):
        packed = jnp.zeros(pay.shape[1:], jnp.float32)
        packed = jnp.where(lane < chans, jnp.concatenate(
            [mix_ref[b], jnp.zeros((chans, pay.shape[2] - chans), jnp.float32)], axis=1), packed)
        for t in range(3):
            packed = jnp.where(lane == chans + t, jnp.sum(kzg_ref[b, t], axis=1, keepdims=True), packed)
        for t in range(9):
            packed = jnp.where(lane == chans + 3 + t, jnp.sum(kxyg_ref[b, t], axis=1, keepdims=True), packed)
        pay[b] = packed

    def conv_plane(q):
        vg_ref[q] = plane_conv([gp1[q + i] for i in range(3)], kxy_ref, 0, True, y).astype(vg_ref.dtype)

    order = list(range(1, own - 1)) + [0, own - 1]
    halo_done = False
    src = pay
    copies = []
    slot = 0
    for g, partners in enumerate(steps):
        here_copies = []
        for k, partner in enumerate(partners):
            copy = pltpu.make_async_remote_copy(
                src_ref=src,
                dst_ref=recv.at[slot + k],
                send_sem=send_sem.at[slot + k],
                recv_sem=recv_sem.at[slot + k],
                device_id=partner,
                device_id_type=MESH,
            )
            copy.start()
            here_copies.append(copy)
        todo = order[g * own // len(steps) : (g + 1) * own // len(steps)]
        if (0 in todo or own - 1 in todo) and not halo_done:
            finish_e()
            halo_done = True
        for q in todo:
            conv_plane(q)
        for copy in here_copies:
            copy.wait_recv()
        copies += here_copies
        vals = [src[...]] + [recv[slot + k] for k in range(len(partners))]
        while len(vals) > 1:
            vals = [vals[i] + vals[i + 1] for i in range(0, len(vals), 2)]
        if g == len(steps) - 1:
            sums_ref[...] = vals[0] * factor
        else:
            acc[g] = vals[0]
            src = acc.at[g]
        slot += len(partners)
    for copy in copies:
        copy.wait_send()
    drain_e()


def on_device(volume, cotangent, kernels_xy, kernels_z, mixing):
    _, chans, own, depth, across = volume.shape
    lanes = depth * across
    f32, bf16 = jnp.float32, jnp.bfloat16
    vol = volume[0].reshape(chans, own, lanes).transpose(1, 0, 2)
    cot = cotangent[0].reshape(chans, own, lanes).transpose(1, 0, 2)
    kxy = jnp.broadcast_to(
        kernels_xy.astype(f32).reshape(2, chans, 9).transpose(0, 2, 1)[..., None], (2, 9, chans, 128)
    )
    kz = jnp.broadcast_to(kernels_z.astype(f32).transpose(0, 2, 1)[..., None], (2, 3, chans, 128))
    wt = mixing.transpose(0, 2, 1)
    ranks = lax.axis_size("sp")
    place = lax.axis_index("sp")
    spots = place * own - 1 + jnp.arange(own + 2, dtype=jnp.int32)
    mask = ((spots >= 0) & (spots < own * ranks)).astype(f32)
    axes = (("sp", ranks), ("dp", lax.axis_size("dp")))
    groups = exchange_groups(axes, 2)
    slots = sum((1 << len(g)) - 1 for g in groups)
    assert own >= 2 and own % len(groups) == 0 and chans + 12 <= 128
    factor = 1.0 / math.sqrt(lax.axis_size("dp") * own * ranks * depth * across)
    planes = lambda n, t: pltpu.VMEM((n, chans, lanes), t)
    grad_in, sums = pl.pallas_call(
        functools.partial(whole_kernel, axes, groups, factor),
        out_shape=(
            jax.ShapeDtypeStruct((own, chans, lanes), bf16),
            jax.ShapeDtypeStruct((2, chans, 128), f32),
        ),
        in_specs=[pl.BlockSpec(memory_space=pltpu.SMEM)] + [pl.BlockSpec(memory_space=pltpu.VMEM)] * 6,
        out_specs=[pl.BlockSpec(memory_space=pltpu.VMEM)] * 2,
        scratch_shapes=[
            planes(own + 4, bf16),
            planes(own + 2, bf16),
            planes(own + 2, f32),
            planes(own + 2, bf16),
            planes(own + 2, f32),
            planes(own + 2, bf16),
            planes(own + 2, bf16),
            pltpu.VMEM((2, chans, 128), f32),
            pltpu.VMEM((2, chans, chans), f32),
            pltpu.VMEM((2, 3, chans, 128), f32),
            pltpu.VMEM((2, 9, chans, 128), f32),
            pltpu.VMEM((slots, 2, chans, 128), f32),
            pltpu.VMEM((len(groups), 2, chans, 128), f32),
        ] + [pltpu.SemaphoreType.DMA((2,))] * 6 + [pltpu.SemaphoreType.DMA((slots,))] * 2,
        compiler_params=pltpu.CompilerParams(
            collective_id=0, has_side_effects=True, vmem_limit_bytes=VMEM_LIMIT
        ),
    )(mask, vol, cot, kxy, kz, mixing, wt)
    grad_in = grad_in.transpose(1, 0, 2).reshape(1, chans, own, depth, across)
    mixing_grad = sums[:, :, :chans]
    z_grad = sums[:, :, chans : chans + 3]
    xy_grad = sums[:, :, chans + 3 : chans + 12].reshape(2, chans, 3, 3)
    return (grad_in, mixing_grad, xy_grad, z_grad)


def solution(mesh):
    return jax.shard_map(
        on_device,
        mesh=mesh,
        in_specs=(P("dp", None, "sp", None, None), P("dp", None, "sp", None, None), P(), P(), P()),
        out_specs=(P("dp", None, "sp", None, None), P(), P(), P()),
        check_vma=False,
    )
```

```python
import functools
import math

import jax
import jax.numpy as jnp
from jax import lax
from jax.experimental import pallas as pl
from jax.experimental.pallas import tpu as pltpu
from jax.sharding import PartitionSpec as P

MESH = pl.DeviceIdType.MESH
VMEM_LIMIT = 56 * 1024 * 1024


def exchange_groups(axes, radix_bits):
    bits = []
    for name, size in axes:
        assert size & (size - 1) == 0
        for b in range(size.bit_length() - 1):
            bits.append((name, 1 << b))
    return [bits[i : i + radix_bits] for i in range(0, len(bits), radix_bits)]


def coords(shape):
    lane = lax.broadcasted_iota(jnp.int32, shape, 1)
    return jnp.bitwise_and(lane, 127), jnp.right_shift(lane, 7)


def at_y(a, d, y):
    if d == 0:
        return a
    rolled = pltpu.roll(a, (-d) % a.shape[1], 1)
    return jnp.where((y + d >= 0) & (y + d < 128), rolled, 0.0)


def at_z(a, d, z):
    if d == 0:
        return a
    rolled = pltpu.roll(a, (-128 * d) % a.shape[1], 1)
    return jnp.where((z + d >= 0) & (z + d < a.shape[1] // 128), rolled, 0.0)


def widen(k, lanes):
    return jnp.concatenate([k] * (lanes // k.shape[1]), axis=1)


def fold(a):
    total = a[:, :128]
    for g in range(1, a.shape[1] // 128):
        total = total + a[:, g * 128 : (g + 1) * 128]
    return total


def sigmoid(u):
    return 1.0 / (1.0 + jnp.exp(-u))


def plane_conv(planes, k_ref, b, flip, y):
    lanes = planes[0].shape[1]
    total = None
    for i in range(3):
        src = planes[i].astype(jnp.float32)
        for j in range(3):
            tap = (2 - i) * 3 + (2 - j) if flip else i * 3 + j
            term = widen(k_ref[b, tap], lanes) * at_y(src, j - 1, y)
            total = term if total is None else total + term
    return total


def depth_conv(a, kz_ref, b, flip, z):
    lanes = a.shape[1]
    total = None
    for t in range(3):
        tap = 2 - t if flip else t
        term = widen(kz_ref[b, tap], lanes) * at_z(a, t - 1, z)
        total = term if total is None else total + term
    return total


def silu_grad(g, pre):
    s = sigmoid(pre)
    return (g * (s * (1.0 + pre * (1.0 - s)))).astype(jnp.bfloat16)


def weight_grads(b, gpre, ax, gax, pl, gpl, around, mix_ref, kzg_ref, kxyg_ref, y, z):
    mix_ref[b] += lax.dot_general(
        gpre, ax, (((1,), (1,)), ((), ())), preferred_element_type=jnp.float32
    )
    for t in range(3):
        kzg_ref[b, t] += fold(gax * at_z(pl, t - 1, z))
    gplf = gpl.astype(jnp.float32)
    for i in range(3):
        src = around[i].astype(jnp.float32)
        for j in range(3):
            kxyg_ref[b, i * 3 + j] += fold(gplf * at_y(src, j - 1, y))


def whole_kernel(axes, groups, factor, vol_hbm, cot_hbm, kxy_ref, kz_ref, w_ref, wt_ref,
                 vg_hbm, sums_ref,
                 wide, cot_ref, vg_ref, h2, pl1, ax1, pre1, gp2, gp1, pay, mix_ref, kzg_ref, kxyg_ref, recv, acc,
                 in_send, in_recv, g_send, g_recv, e_send, e_recv, send_sem, recv_sem):
    own = cot_ref.shape[0]
    depth = vol_hbm.shape[2]
    y, z = coords(cot_ref.shape[1:])

    def to_planes(raw, buf, first):
        for x in range(own):
            v = pltpu.einshape("czy->zcy", raw[:, x].astype(jnp.float32))
            buf[first + x] = jnp.concatenate([v[k] for k in range(depth)], axis=1).astype(buf.dtype)

    here = {name: lax.axis_index(name) for name, _ in axes}
    steps = []
    for group in groups:
        partners = []
        for offset in range(1, 1 << len(group)):
            where = dict(here)
            for k, (name, stride) in enumerate(group):
                if (offset >> k) & 1:
                    bit = (where[name] // stride) % 2
                    where[name] = where[name] + stride * (1 - 2 * bit)
            partners.append(tuple(where[n] for n, _ in axes))
        steps.append(partners)
    sp, last, dp = here["sp"], axes[0][1] - 1, here["dp"]
    left, right = (sp - 1, dp), (sp + 1, dp)
    has_left, has_right = sp > 0, sp < last
    span = 1 << len(groups[0])
    extra_left = has_left & (sp % span == 0)
    extra_right = has_right & (sp % span == span - 1)

    barrier = pltpu.get_barrier_semaphore()
    count = 0
    for partners in steps:
        for partner in partners:
            pl.semaphore_signal(barrier, inc=1, device_id=partner, device_id_type=MESH)
            count += 1

    @pl.when(extra_left)
    def _():
        pl.semaphore_signal(barrier, inc=1, device_id=left, device_id_type=MESH)

    @pl.when(extra_right)
    def _():
        pl.semaphore_signal(barrier, inc=1, device_id=right, device_id_type=MESH)

    to_planes(vol_hbm, wide, 2)
    to_planes(cot_hbm, cot_ref, 0)
    pl.semaphore_wait(barrier, count + extra_left.astype(jnp.int32) + extra_right.astype(jnp.int32))

    def exchange(buf, first, count, send, recv, src, src_first):
        to_left = pltpu.make_async_remote_copy(
            src_ref=src.at[pl.ds(src_first, count)], dst_ref=buf.at[pl.ds(first + own, count)],
            send_sem=send.at[0], recv_sem=recv.at[1], device_id=left, device_id_type=MESH,
        )
        to_right = pltpu.make_async_remote_copy(
            src_ref=src.at[pl.ds(src_first + own - count, count)], dst_ref=buf.at[pl.ds(first - count, count)],
            send_sem=send.at[1], recv_sem=recv.at[0], device_id=right, device_id_type=MESH,
        )
        pl.when(has_left)(to_left.start)
        pl.when(has_right)(to_right.start)

        def finish():
            pl.when(has_left)(to_right.wait_recv)
            pl.when(has_right)(to_left.wait_recv)
            zeros = jnp.zeros((count,) + buf.shape[1:], buf.dtype)

            @pl.when(sp == 0)
            def _():
                buf[pl.ds(first - count, count)] = zeros

            @pl.when(sp == last)
            def _():
                buf[pl.ds(first + own, count)] = zeros

        def drain():
            pl.when(has_left)(to_left.wait_send)
            pl.when(has_right)(to_right.wait_send)

        return finish, drain

    mix_ref[...] = jnp.zeros_like(mix_ref)
    kzg_ref[...] = jnp.zeros_like(kzg_ref)
    kxyg_ref[...] = jnp.zeros_like(kxyg_ref)

    finish_in, drain_in = exchange(wide, 2, 2, in_send, in_recv, wide, 2)

    def forward1(p):
        planar = plane_conv([wide[p + i] for i in range(3)], kxy_ref, 0, False, y)
        axial = depth_conv(planar, kz_ref, 0, False, z).astype(jnp.bfloat16)
        pre = jnp.dot(w_ref[0], axial, preferred_element_type=jnp.float32)
        pl1[p] = planar
        ax1[p] = axial
        pre1[p] = pre
        spot = sp * own - 1 + p
        inside = ((spot >= 0) & (spot < own * (last + 1))).astype(jnp.float32)
        h2[p] = (pre * sigmoid(pre) * inside).astype(jnp.bfloat16)

    def block2(q):
        around = [h2[q + i] for i in range(3)]
        planar = plane_conv(around, kxy_ref, 1, False, y)
        axial = depth_conv(planar, kz_ref, 1, False, z).astype(jnp.bfloat16)
        pre = jnp.dot(w_ref[1], axial, preferred_element_type=jnp.float32)
        gpre = silu_grad(cot_ref[q].astype(jnp.float32), pre)
        gax = jnp.dot(wt_ref[1], gpre, preferred_element_type=jnp.float32)
        gpl = depth_conv(gax, kz_ref, 1, True, z).astype(jnp.bfloat16)
        gp2[q + 1] = gpl
        weight_grads(1, gpre, axial, gax, planar, gpl, around, mix_ref, kzg_ref, kxyg_ref, y, z)

    def block1(q):
        g1 = plane_conv([gp2[q + i] for i in range(3)], kxy_ref, 1, True, y).astype(jnp.bfloat16)
        gpre = silu_grad(g1.astype(jnp.float32), pre1[q + 1])
        gax = jnp.dot(wt_ref[0], gpre, preferred_element_type=jnp.float32)
        gpl = depth_conv(gax, kz_ref, 0, True, z).astype(jnp.bfloat16)
        gp1[q + 1] = gpl
        around = [wide[q + 1 + i] for i in range(3)]
        weight_grads(0, gpre, ax1[q + 1], gax, pl1[q + 1], gpl, around, mix_ref, kzg_ref, kxyg_ref, y, z)

    def run(body, lo, hi, place=lambda i: i):
        def step(i, carry):
            body(place(i))
            return carry

        lax.fori_loop(lo, hi, step, 0)

    run(forward1, 2, own)
    finish_in()
    run(forward1, 0, 4, lambda i: i + (i // 2) * (own - 2))
    run(block2, 0, 2, lambda i: i * (own - 1))
    finish_g, drain_g = exchange(gp2, 1, 1, g_send, g_recv, gp2, 1)
    run(block2, 1, own - 1)
    run(block1, 1, own - 1)
    finish_g()
    run(block1, 0, 2, lambda i: i * (own - 1))
    finish_e, drain_e = exchange(gp1, 1, 1, e_send, e_recv, gp1, 1)
    drain_in()
    drain_g()

    lane = lax.broadcasted_iota(jnp.int32, pay.shape[1:], 1)
    chans = pay.shape[1]
    for b in range(2):
        packed = jnp.zeros(pay.shape[1:], jnp.float32)
        packed = jnp.where(lane < chans, jnp.concatenate(
            [mix_ref[b], jnp.zeros((chans, pay.shape[2] - chans), jnp.float32)], axis=1), packed)
        for t in range(3):
            packed = jnp.where(lane == chans + t, jnp.sum(kzg_ref[b, t], axis=1, keepdims=True), packed)
        for t in range(9):
            packed = jnp.where(lane == chans + 3 + t, jnp.sum(kxyg_ref[b, t], axis=1, keepdims=True), packed)
        pay[b] = packed


    def conv_plane(q):
        vg_ref[q] = plane_conv([gp1[q + i] for i in range(3)], kxy_ref, 0, True, y).astype(vg_ref.dtype)
        v = vg_ref[q].astype(jnp.float32)
        v = jnp.stack([v[:, k * 128 : (k + 1) * 128] for k in range(depth)], axis=0)
        vg_hbm[:, q] = pltpu.einshape("zcy->czy", v).astype(vg_hbm.dtype)

    order = list(range(1, own - 1)) + [0, own - 1]
    halo_done = False
    src = pay
    copies = []
    slot = 0
    for g, partners in enumerate(steps):
        here_copies = []
        for k, partner in enumerate(partners):
            copy = pltpu.make_async_remote_copy(
                src_ref=src,
                dst_ref=recv.at[slot + k],
                send_sem=send_sem.at[slot + k],
                recv_sem=recv_sem.at[slot + k],
                device_id=partner,
                device_id_type=MESH,
            )
            copy.start()
            here_copies.append(copy)
        todo = order[g * own // len(steps) : (g + 1) * own // len(steps)]
        if (0 in todo or own - 1 in todo) and not halo_done:
            finish_e()
            halo_done = True
        for q in todo:
            conv_plane(q)
        for copy in here_copies:
            copy.wait_recv()
        copies += here_copies
        vals = [src[...]] + [recv[slot + k] for k in range(len(partners))]
        while len(vals) > 1:
            vals = [vals[i] + vals[i + 1] for i in range(0, len(vals), 2)]
        if g == len(steps) - 1:
            sums_ref[...] = vals[0] * factor
        else:
            acc[g] = vals[0]
            src = acc.at[g]
        slot += len(partners)
    for copy in copies:
        copy.wait_send()
    drain_e()


def on_device(volume, cotangent, kernels_xy, kernels_z, mixing):
    _, chans, own, depth, across = volume.shape
    lanes = depth * across
    f32, bf16 = jnp.float32, jnp.bfloat16
    kxy = jnp.broadcast_to(
        kernels_xy.astype(f32).reshape(2, chans, 9).transpose(0, 2, 1)[..., None], (2, 9, chans, 128)
    )
    kz = jnp.broadcast_to(kernels_z.astype(f32).transpose(0, 2, 1)[..., None], (2, 3, chans, 128))
    wt = mixing.transpose(0, 2, 1)
    ranks = lax.axis_size("sp")
    axes = (("sp", ranks), ("dp", lax.axis_size("dp")))
    groups = exchange_groups(axes, 2)
    slots = sum((1 << len(g)) - 1 for g in groups)
    assert own >= 2 and own % len(groups) == 0 and chans + 12 <= 128
    factor = 1.0 / math.sqrt(lax.axis_size("dp") * own * ranks * depth * across)
    planes = lambda n, t: pltpu.VMEM((n, chans, lanes), t)
    grad_in, sums = pl.pallas_call(
        functools.partial(whole_kernel, axes, groups, factor),
        out_shape=(
            jax.ShapeDtypeStruct((chans, own, depth, across), bf16),
            jax.ShapeDtypeStruct((2, chans, 128), f32),
        ),
        in_specs=[pl.BlockSpec(memory_space=pltpu.VMEM)] * 6,
        out_specs=[pl.BlockSpec(memory_space=pltpu.VMEM)] * 2,
        scratch_shapes=[
            planes(own + 4, bf16),
            planes(own, bf16),
            planes(own, bf16),
            planes(own + 2, bf16),
            planes(own + 2, f32),
            planes(own + 2, bf16),
            planes(own + 2, f32),
            planes(own + 2, bf16),
            planes(own + 2, bf16),
            pltpu.VMEM((2, chans, 128), f32),
            pltpu.VMEM((2, chans, chans), f32),
            pltpu.VMEM((2, 3, chans, 128), f32),
            pltpu.VMEM((2, 9, chans, 128), f32),
            pltpu.VMEM((slots, 2, chans, 128), f32),
            pltpu.VMEM((len(groups), 2, chans, 128), f32),
        ] + [pltpu.SemaphoreType.DMA((2,))] * 6 + [pltpu.SemaphoreType.DMA((slots,))] * 2,
        compiler_params=pltpu.CompilerParams(
            collective_id=0, has_side_effects=True, vmem_limit_bytes=VMEM_LIMIT
        ),
    )(volume[0], cotangent[0], kxy, kz, mixing, wt)
    grad_in = grad_in[None]
    mixing_grad = sums[:, :, :chans]
    z_grad = sums[:, :, chans : chans + 3]
    xy_grad = sums[:, :, chans + 3 : chans + 12].reshape(2, chans, 3, 3)
    return (grad_in, mixing_grad, xy_grad, z_grad)


def solution(mesh):
    return jax.shard_map(
        on_device,
        mesh=mesh,
        in_specs=(P("dp", None, "sp", None, None), P("dp", None, "sp", None, None), P(), P(), P()),
        out_specs=(P("dp", None, "sp", None, None), P(), P(), P()),
        check_vma=False,
    )
```

```python
import functools
import math

import jax
import jax.numpy as jnp
from jax import lax
from jax.experimental import pallas as pl
from jax.experimental.pallas import tpu as pltpu
from jax.sharding import PartitionSpec as P

MESH = pl.DeviceIdType.MESH
VMEM_LIMIT = 56 * 1024 * 1024


def exchange_groups(axes, radix_bits):
    bits = []
    for name, size in axes:
        assert size & (size - 1) == 0
        for b in range(size.bit_length() - 1):
            bits.append((name, 1 << b))
    return [bits[i : i + radix_bits] for i in range(0, len(bits), radix_bits)]


def coords(shape):
    lane = lax.broadcasted_iota(jnp.int32, shape, 1)
    return jnp.bitwise_and(lane, 127), jnp.right_shift(lane, 7)


def at_y(a, d, y):
    if d == 0:
        return a
    rolled = pltpu.roll(a, (-d) % a.shape[1], 1)
    return jnp.where((y + d >= 0) & (y + d < 128), rolled, 0.0)


def at_z(a, d, z):
    if d == 0:
        return a
    rolled = pltpu.roll(a, (-128 * d) % a.shape[1], 1)
    return jnp.where((z + d >= 0) & (z + d < a.shape[1] // 128), rolled, 0.0)


def widen(k, lanes):
    return jnp.broadcast_to(k, (k.shape[0], lanes))


def fold(a):
    total = a[:, :128]
    for g in range(1, a.shape[1] // 128):
        total = total + a[:, g * 128 : (g + 1) * 128]
    return total


def sigmoid(u):
    return 1.0 / (1.0 + jnp.exp(-u))


def plane_conv(planes, k_ref, b, flip, y):
    lanes = planes[0].shape[1]
    total = None
    for i in range(3):
        src = planes[i].astype(jnp.float32)
        for j in range(3):
            tap = (2 - i) * 3 + (2 - j) if flip else i * 3 + j
            term = widen(k_ref[b, :, tap : tap + 1], lanes) * at_y(src, j - 1, y)
            total = term if total is None else total + term
    return total


def depth_conv(a, kz_ref, b, flip, z):
    lanes = a.shape[1]
    total = None
    for t in range(3):
        tap = 2 - t if flip else t
        term = widen(kz_ref[b, :, 9 + tap : 10 + tap], lanes) * at_z(a, t - 1, z)
        total = term if total is None else total + term
    return total


def silu_grad(g, pre):
    s = sigmoid(pre)
    return (g * (s * (1.0 + pre * (1.0 - s)))).astype(jnp.bfloat16)


def weight_grads(b, gpre, ax, gax, pl, gpl, around, mix_ref, kzg_ref, kxyg_ref, y, z):
    mix_ref[b] += lax.dot_general(
        gpre, ax, (((1,), (1,)), ((), ())), preferred_element_type=jnp.float32
    )
    for t in range(3):
        kzg_ref[b, t] += fold(gax * at_z(pl, t - 1, z))
    gplf = gpl.astype(jnp.float32)
    for i in range(3):
        src = around[i].astype(jnp.float32)
        for j in range(3):
            kxyg_ref[b, i * 3 + j] += fold(gplf * at_y(src, j - 1, y))


def whole_kernel(axes, groups, factor, vol_hbm, cot_hbm, kxy_ref, w_ref,
                 vg_hbm, sums_ref,
                 wide, cot_ref, vg_ref, h2, pl1, ax1, pre1, gp2, gp1, pay, mix_ref, kzg_ref, kxyg_ref, recv, acc,
                 in_send, in_recv, g_send, g_recv, e_send, e_recv, send_sem, recv_sem):
    own = cot_ref.shape[0]
    depth = vol_hbm.shape[2]
    kz_ref = kxy_ref
    y, z = coords(cot_ref.shape[1:])

    def to_planes(raw, buf, first):
        for x in range(own):
            v = pltpu.einshape("czy->zcy", raw[:, x].astype(jnp.float32))
            buf[first + x] = jnp.concatenate([v[k] for k in range(depth)], axis=1).astype(buf.dtype)

    here = {name: lax.axis_index(name) for name, _ in axes}
    steps = []
    for group in groups:
        partners = []
        for offset in range(1, 1 << len(group)):
            where = dict(here)
            for k, (name, stride) in enumerate(group):
                if (offset >> k) & 1:
                    bit = (where[name] // stride) % 2
                    where[name] = where[name] + stride * (1 - 2 * bit)
            partners.append(tuple(where[n] for n, _ in axes))
        steps.append(partners)
    sp, last, dp = here["sp"], axes[0][1] - 1, here["dp"]
    left, right = (sp - 1, dp), (sp + 1, dp)
    has_left, has_right = sp > 0, sp < last
    span = 1 << len(groups[0])
    extra_left = has_left & (sp % span == 0)
    extra_right = has_right & (sp % span == span - 1)

    barrier = pltpu.get_barrier_semaphore()
    count = 0
    for partners in steps:
        for partner in partners:
            pl.semaphore_signal(barrier, inc=1, device_id=partner, device_id_type=MESH)
            count += 1

    @pl.when(extra_left)
    def _():
        pl.semaphore_signal(barrier, inc=1, device_id=left, device_id_type=MESH)

    @pl.when(extra_right)
    def _():
        pl.semaphore_signal(barrier, inc=1, device_id=right, device_id_type=MESH)

    to_planes(vol_hbm, wide, 2)
    to_planes(cot_hbm, cot_ref, 0)
    pl.semaphore_wait(barrier, count + extra_left.astype(jnp.int32) + extra_right.astype(jnp.int32))

    def exchange(buf, first, count, send, recv, src, src_first):
        to_left = pltpu.make_async_remote_copy(
            src_ref=src.at[pl.ds(src_first, count)], dst_ref=buf.at[pl.ds(first + own, count)],
            send_sem=send.at[0], recv_sem=recv.at[1], device_id=left, device_id_type=MESH,
        )
        to_right = pltpu.make_async_remote_copy(
            src_ref=src.at[pl.ds(src_first + own - count, count)], dst_ref=buf.at[pl.ds(first - count, count)],
            send_sem=send.at[1], recv_sem=recv.at[0], device_id=right, device_id_type=MESH,
        )
        pl.when(has_left)(to_left.start)
        pl.when(has_right)(to_right.start)

        def finish():
            pl.when(has_left)(to_right.wait_recv)
            pl.when(has_right)(to_left.wait_recv)
            zeros = jnp.zeros((count,) + buf.shape[1:], buf.dtype)

            @pl.when(sp == 0)
            def _():
                buf[pl.ds(first - count, count)] = zeros

            @pl.when(sp == last)
            def _():
                buf[pl.ds(first + own, count)] = zeros

        def drain():
            pl.when(has_left)(to_left.wait_send)
            pl.when(has_right)(to_right.wait_send)

        return finish, drain

    mix_ref[...] = jnp.zeros_like(mix_ref)
    kzg_ref[...] = jnp.zeros_like(kzg_ref)
    kxyg_ref[...] = jnp.zeros_like(kxyg_ref)

    finish_in, drain_in = exchange(wide, 2, 2, in_send, in_recv, wide, 2)

    def forward1(p):
        planar = plane_conv([wide[p + i] for i in range(3)], kxy_ref, 0, False, y)
        axial = depth_conv(planar, kz_ref, 0, False, z).astype(jnp.bfloat16)
        pre = jnp.dot(w_ref[0], axial, preferred_element_type=jnp.float32)
        pl1[p] = planar
        ax1[p] = axial
        pre1[p] = pre
        spot = sp * own - 1 + p
        inside = ((spot >= 0) & (spot < own * (last + 1))).astype(jnp.float32)
        h2[p] = (pre * sigmoid(pre) * inside).astype(jnp.bfloat16)

    def block2(q):
        around = [h2[q + i] for i in range(3)]
        planar = plane_conv(around, kxy_ref, 1, False, y)
        axial = depth_conv(planar, kz_ref, 1, False, z).astype(jnp.bfloat16)
        pre = jnp.dot(w_ref[1], axial, preferred_element_type=jnp.float32)
        gpre = silu_grad(cot_ref[q].astype(jnp.float32), pre)
        gax = lax.dot_general(w_ref[1], gpre, (((0,), (0,)), ((), ())), preferred_element_type=jnp.float32)
        gpl = depth_conv(gax, kz_ref, 1, True, z).astype(jnp.bfloat16)
        gp2[q + 1] = gpl
        weight_grads(1, gpre, axial, gax, planar, gpl, around, mix_ref, kzg_ref, kxyg_ref, y, z)

    def block1(q):
        g1 = plane_conv([gp2[q + i] for i in range(3)], kxy_ref, 1, True, y).astype(jnp.bfloat16)
        gpre = silu_grad(g1.astype(jnp.float32), pre1[q + 1])
        gax = lax.dot_general(w_ref[0], gpre, (((0,), (0,)), ((), ())), preferred_element_type=jnp.float32)
        gpl = depth_conv(gax, kz_ref, 0, True, z).astype(jnp.bfloat16)
        gp1[q + 1] = gpl
        around = [wide[q + 1 + i] for i in range(3)]
        weight_grads(0, gpre, ax1[q + 1], gax, pl1[q + 1], gpl, around, mix_ref, kzg_ref, kxyg_ref, y, z)

    def run(body, lo, hi, place=lambda i: i):
        def step(i, carry):
            body(place(i))
            return carry

        lax.fori_loop(lo, hi, step, 0)

    run(forward1, 2, own)
    finish_in()
    run(forward1, 0, 4, lambda i: i + (i // 2) * (own - 2))
    run(block2, 0, 2, lambda i: i * (own - 1))
    finish_g, drain_g = exchange(gp2, 1, 1, g_send, g_recv, gp2, 1)
    run(block2, 1, own - 1)
    run(block1, 1, own - 1)
    finish_g()
    run(block1, 0, 2, lambda i: i * (own - 1))
    finish_e, drain_e = exchange(gp1, 1, 1, e_send, e_recv, gp1, 1)
    drain_in()
    drain_g()

    lane = lax.broadcasted_iota(jnp.int32, pay.shape[1:], 1)
    chans = pay.shape[1]
    for b in range(2):
        packed = jnp.zeros(pay.shape[1:], jnp.float32)
        packed = jnp.where(lane < chans, jnp.concatenate(
            [mix_ref[b], jnp.zeros((chans, pay.shape[2] - chans), jnp.float32)], axis=1), packed)
        for t in range(3):
            packed = jnp.where(lane == chans + t, jnp.sum(kzg_ref[b, t], axis=1, keepdims=True), packed)
        for t in range(9):
            packed = jnp.where(lane == chans + 3 + t, jnp.sum(kxyg_ref[b, t], axis=1, keepdims=True), packed)
        pay[b] = packed


    def conv_plane(q):
        vg_ref[q] = plane_conv([gp1[q + i] for i in range(3)], kxy_ref, 0, True, y).astype(vg_ref.dtype)
        v = vg_ref[q].astype(jnp.float32)
        v = jnp.stack([v[:, k * 128 : (k + 1) * 128] for k in range(depth)], axis=0)
        vg_hbm[:, q] = pltpu.einshape("zcy->czy", v).astype(vg_hbm.dtype)

    order = list(range(1, own - 1)) + [0, own - 1]
    halo_done = False
    src = pay
    copies = []
    slot = 0
    for g, partners in enumerate(steps):
        here_copies = []
        for k, partner in enumerate(partners):
            copy = pltpu.make_async_remote_copy(
                src_ref=src,
                dst_ref=recv.at[slot + k],
                send_sem=send_sem.at[slot + k],
                recv_sem=recv_sem.at[slot + k],
                device_id=partner,
                device_id_type=MESH,
            )
            copy.start()
            here_copies.append(copy)
        todo = order[g * own // len(steps) : (g + 1) * own // len(steps)]
        if (0 in todo or own - 1 in todo) and not halo_done:
            finish_e()
            halo_done = True
        for q in todo:
            conv_plane(q)
        for copy in here_copies:
            copy.wait_recv()
        copies += here_copies
        vals = [src[...]] + [recv[slot + k] for k in range(len(partners))]
        while len(vals) > 1:
            vals = [vals[i] + vals[i + 1] for i in range(0, len(vals), 2)]
        if g == len(steps) - 1:
            sums_ref[...] = vals[0] * factor
        else:
            acc[g] = vals[0]
            src = acc.at[g]
        slot += len(partners)
    for copy in copies:
        copy.wait_send()
    drain_e()


def on_device(volume, cotangent, kernels_xy, kernels_z, mixing):
    _, chans, own, depth, across = volume.shape
    lanes = depth * across
    f32, bf16 = jnp.float32, jnp.bfloat16
    taps = jnp.concatenate(
        [kernels_xy.reshape(2, chans, 9), kernels_z], axis=2
    ).astype(f32)
    ranks = lax.axis_size("sp")
    axes = (("sp", ranks), ("dp", lax.axis_size("dp")))
    groups = exchange_groups(axes, 2)
    slots = sum((1 << len(g)) - 1 for g in groups)
    assert own >= 2 and own % len(groups) == 0 and chans + 12 <= 128
    factor = 1.0 / math.sqrt(lax.axis_size("dp") * own * ranks * depth * across)
    planes = lambda n, t: pltpu.VMEM((n, chans, lanes), t)
    grad_in, sums = pl.pallas_call(
        functools.partial(whole_kernel, axes, groups, factor),
        out_shape=(
            jax.ShapeDtypeStruct((chans, own, depth, across), bf16),
            jax.ShapeDtypeStruct((2, chans, 128), f32),
        ),
        in_specs=[pl.BlockSpec(memory_space=pltpu.VMEM)] * 4,
        out_specs=[pl.BlockSpec(memory_space=pltpu.VMEM)] * 2,
        scratch_shapes=[
            planes(own + 4, bf16),
            planes(own, bf16),
            planes(own, bf16),
            planes(own + 2, bf16),
            planes(own + 2, f32),
            planes(own + 2, bf16),
            planes(own + 2, f32),
            planes(own + 2, bf16),
            planes(own + 2, bf16),
            pltpu.VMEM((2, chans, 128), f32),
            pltpu.VMEM((2, chans, chans), f32),
            pltpu.VMEM((2, 3, chans, 128), f32),
            pltpu.VMEM((2, 9, chans, 128), f32),
            pltpu.VMEM((slots, 2, chans, 128), f32),
            pltpu.VMEM((len(groups), 2, chans, 128), f32),
        ] + [pltpu.SemaphoreType.DMA((2,))] * 6 + [pltpu.SemaphoreType.DMA((slots,))] * 2,
        compiler_params=pltpu.CompilerParams(
            collective_id=0, has_side_effects=True, vmem_limit_bytes=VMEM_LIMIT
        ),
    )(volume[0], cotangent[0], taps, mixing)
    grad_in = grad_in[None]
    mixing_grad = sums[:, :, :chans]
    z_grad = sums[:, :, chans : chans + 3]
    xy_grad = sums[:, :, chans + 3 : chans + 12].reshape(2, chans, 3, 3)
    return (grad_in, mixing_grad, xy_grad, z_grad)


def solution(mesh):
    return jax.shard_map(
        on_device,
        mesh=mesh,
        in_specs=(P("dp", None, "sp", None, None), P("dp", None, "sp", None, None), P(), P(), P()),
        out_specs=(P("dp", None, "sp", None, None), P(), P(), P()),
        check_vma=False,
    )
```

```python
import functools
import math

import jax
import jax.numpy as jnp
from jax import lax
from jax.experimental import pallas as pl
from jax.experimental.pallas import tpu as pltpu
from jax.sharding import PartitionSpec as P

MESH = pl.DeviceIdType.MESH
VMEM_LIMIT = 56 * 1024 * 1024


def exchange_groups(axes, radix_bits):
    bits = []
    for name, size in axes:
        assert size & (size - 1) == 0
        for b in range(size.bit_length() - 1):
            bits.append((name, 1 << b))
    return [bits[i : i + radix_bits] for i in range(0, len(bits), radix_bits)]


def coords(shape):
    lane = lax.broadcasted_iota(jnp.int32, shape, 1)
    return jnp.bitwise_and(lane, 127), jnp.right_shift(lane, 7)


def at_y(a, d, y):
    if d == 0:
        return a
    rolled = pltpu.roll(a, (-d) % a.shape[1], 1)
    return jnp.where((y + d >= 0) & (y + d < 128), rolled, 0.0)


def at_z(a, d, z):
    if d == 0:
        return a
    rolled = pltpu.roll(a, (-128 * d) % a.shape[1], 1)
    return jnp.where((z + d >= 0) & (z + d < a.shape[1] // 128), rolled, 0.0)


def widen(k, lanes):
    return jnp.broadcast_to(k, (k.shape[0], lanes))


def fold(a):
    total = a[:, :128]
    for g in range(1, a.shape[1] // 128):
        total = total + a[:, g * 128 : (g + 1) * 128]
    return total


def sigmoid(u):
    return 1.0 / (1.0 + jnp.exp(-u))


def plane_conv(planes, k_ref, b, flip, y):
    lanes = planes[0].shape[1]
    srcs = [p.astype(jnp.float32) for p in planes]
    total = None
    for j in range(3):
        column = None
        for i in range(3):
            tap = (2 - i) * 3 + (2 - j) if flip else i * 3 + j
            term = widen(k_ref[b, :, tap : tap + 1], lanes) * srcs[i]
            column = term if column is None else column + term
        column = at_y(column, j - 1, y)
        total = column if total is None else total + column
    return total


def depth_conv(a, kz_ref, b, flip, z):
    lanes = a.shape[1]
    total = None
    for t in range(3):
        tap = 2 - t if flip else t
        term = widen(kz_ref[b, :, 9 + tap : 10 + tap], lanes) * at_z(a, t - 1, z)
        total = term if total is None else total + term
    return total


def silu_grad(g, pre):
    s = sigmoid(pre)
    return (g * (s * (1.0 + pre * (1.0 - s)))).astype(jnp.bfloat16)


def weight_grads(b, gpre, ax, gax, pl, gpl, around, mix_ref, kzg_ref, kxyg_ref, y, z):
    mix_ref[b] += lax.dot_general(
        gpre, ax, (((1,), (1,)), ((), ())), preferred_element_type=jnp.float32
    )
    for t in range(3):
        kzg_ref[b, t] += fold(gax * at_z(pl, t - 1, z))
    gplf = gpl.astype(jnp.float32)
    srcs = [a.astype(jnp.float32) for a in around]
    for j in range(3):
        shifted = at_y(gplf, 1 - j, y)
        for i in range(3):
            kxyg_ref[b, i * 3 + j] += fold(shifted * srcs[i])


def whole_kernel(axes, groups, factor, vol_hbm, cot_hbm, kxy_ref, w_ref,
                 vg_hbm, sums_ref,
                 wide, cot_ref, vg_ref, h2, pl1, ax1, pre1, gp2, gp1, pay, mix_ref, kzg_ref, kxyg_ref, recv, acc,
                 in_send, in_recv, g_send, g_recv, e_send, e_recv, send_sem, recv_sem):
    own = cot_ref.shape[0]
    depth = vol_hbm.shape[2]
    kz_ref = kxy_ref
    y, z = coords(cot_ref.shape[1:])

    def to_planes(raw, buf, first):
        for x in range(own):
            v = pltpu.einshape("czy->zcy", raw[:, x].astype(jnp.float32))
            buf[first + x] = jnp.concatenate([v[k] for k in range(depth)], axis=1).astype(buf.dtype)

    here = {name: lax.axis_index(name) for name, _ in axes}
    steps = []
    for group in groups:
        partners = []
        for offset in range(1, 1 << len(group)):
            where = dict(here)
            for k, (name, stride) in enumerate(group):
                if (offset >> k) & 1:
                    bit = (where[name] // stride) % 2
                    where[name] = where[name] + stride * (1 - 2 * bit)
            partners.append(tuple(where[n] for n, _ in axes))
        steps.append(partners)
    sp, last, dp = here["sp"], axes[0][1] - 1, here["dp"]
    left, right = (sp - 1, dp), (sp + 1, dp)
    has_left, has_right = sp > 0, sp < last
    span = 1 << len(groups[0])
    extra_left = has_left & (sp % span == 0)
    extra_right = has_right & (sp % span == span - 1)

    barrier = pltpu.get_barrier_semaphore()
    count = 0
    for partners in steps:
        for partner in partners:
            pl.semaphore_signal(barrier, inc=1, device_id=partner, device_id_type=MESH)
            count += 1

    @pl.when(extra_left)
    def _():
        pl.semaphore_signal(barrier, inc=1, device_id=left, device_id_type=MESH)

    @pl.when(extra_right)
    def _():
        pl.semaphore_signal(barrier, inc=1, device_id=right, device_id_type=MESH)

    to_planes(vol_hbm, wide, 2)
    to_planes(cot_hbm, cot_ref, 0)
    pl.semaphore_wait(barrier, count + extra_left.astype(jnp.int32) + extra_right.astype(jnp.int32))

    def exchange(buf, first, count, send, recv, src, src_first):
        to_left = pltpu.make_async_remote_copy(
            src_ref=src.at[pl.ds(src_first, count)], dst_ref=buf.at[pl.ds(first + own, count)],
            send_sem=send.at[0], recv_sem=recv.at[1], device_id=left, device_id_type=MESH,
        )
        to_right = pltpu.make_async_remote_copy(
            src_ref=src.at[pl.ds(src_first + own - count, count)], dst_ref=buf.at[pl.ds(first - count, count)],
            send_sem=send.at[1], recv_sem=recv.at[0], device_id=right, device_id_type=MESH,
        )
        pl.when(has_left)(to_left.start)
        pl.when(has_right)(to_right.start)

        def finish():
            pl.when(has_left)(to_right.wait_recv)
            pl.when(has_right)(to_left.wait_recv)
            zeros = jnp.zeros((count,) + buf.shape[1:], buf.dtype)

            @pl.when(sp == 0)
            def _():
                buf[pl.ds(first - count, count)] = zeros

            @pl.when(sp == last)
            def _():
                buf[pl.ds(first + own, count)] = zeros

        def drain():
            pl.when(has_left)(to_left.wait_send)
            pl.when(has_right)(to_right.wait_send)

        return finish, drain

    mix_ref[...] = jnp.zeros_like(mix_ref)
    kzg_ref[...] = jnp.zeros_like(kzg_ref)
    kxyg_ref[...] = jnp.zeros_like(kxyg_ref)

    finish_in, drain_in = exchange(wide, 2, 2, in_send, in_recv, wide, 2)

    def forward1(p):
        planar = plane_conv([wide[p + i] for i in range(3)], kxy_ref, 0, False, y)
        axial = depth_conv(planar, kz_ref, 0, False, z).astype(jnp.bfloat16)
        pre = jnp.dot(w_ref[0], axial, preferred_element_type=jnp.float32)
        pl1[p] = planar
        ax1[p] = axial
        pre1[p] = pre
        spot = sp * own - 1 + p
        inside = ((spot >= 0) & (spot < own * (last + 1))).astype(jnp.float32)
        h2[p] = (pre * sigmoid(pre) * inside).astype(jnp.bfloat16)

    def block2(q):
        around = [h2[q + i] for i in range(3)]
        planar = plane_conv(around, kxy_ref, 1, False, y)
        axial = depth_conv(planar, kz_ref, 1, False, z).astype(jnp.bfloat16)
        pre = jnp.dot(w_ref[1], axial, preferred_element_type=jnp.float32)
        gpre = silu_grad(cot_ref[q].astype(jnp.float32), pre)
        gax = lax.dot_general(w_ref[1], gpre, (((0,), (0,)), ((), ())), preferred_element_type=jnp.float32)
        gpl = depth_conv(gax, kz_ref, 1, True, z).astype(jnp.bfloat16)
        gp2[q + 1] = gpl
        weight_grads(1, gpre, axial, gax, planar, gpl, around, mix_ref, kzg_ref, kxyg_ref, y, z)

    def block1(q):
        g1 = plane_conv([gp2[q + i] for i in range(3)], kxy_ref, 1, True, y).astype(jnp.bfloat16)
        gpre = silu_grad(g1.astype(jnp.float32), pre1[q + 1])
        gax = lax.dot_general(w_ref[0], gpre, (((0,), (0,)), ((), ())), preferred_element_type=jnp.float32)
        gpl = depth_conv(gax, kz_ref, 0, True, z).astype(jnp.bfloat16)
        gp1[q + 1] = gpl
        around = [wide[q + 1 + i] for i in range(3)]
        weight_grads(0, gpre, ax1[q + 1], gax, pl1[q + 1], gpl, around, mix_ref, kzg_ref, kxyg_ref, y, z)

    def run(body, lo, hi, place=lambda i: i):
        def step(i, carry):
            body(place(i))
            return carry

        lax.fori_loop(lo, hi, step, 0)

    run(forward1, 2, own)
    finish_in()
    run(forward1, 0, 4, lambda i: i + (i // 2) * (own - 2))
    run(block2, 0, 2, lambda i: i * (own - 1))
    finish_g, drain_g = exchange(gp2, 1, 1, g_send, g_recv, gp2, 1)
    run(block2, 1, own - 1)
    run(block1, 1, own - 1)
    finish_g()
    run(block1, 0, 2, lambda i: i * (own - 1))
    finish_e, drain_e = exchange(gp1, 1, 1, e_send, e_recv, gp1, 1)
    drain_in()
    drain_g()

    lane = lax.broadcasted_iota(jnp.int32, pay.shape[1:], 1)
    chans = pay.shape[1]
    for b in range(2):
        packed = jnp.zeros(pay.shape[1:], jnp.float32)
        packed = jnp.where(lane < chans, jnp.concatenate(
            [mix_ref[b], jnp.zeros((chans, pay.shape[2] - chans), jnp.float32)], axis=1), packed)
        for t in range(3):
            packed = jnp.where(lane == chans + t, jnp.sum(kzg_ref[b, t], axis=1, keepdims=True), packed)
        for t in range(9):
            packed = jnp.where(lane == chans + 3 + t, jnp.sum(kxyg_ref[b, t], axis=1, keepdims=True), packed)
        pay[b] = packed


    def conv_plane(q):
        vg_ref[q] = plane_conv([gp1[q + i] for i in range(3)], kxy_ref, 0, True, y).astype(vg_ref.dtype)
        v = vg_ref[q].astype(jnp.float32)
        v = jnp.stack([v[:, k * 128 : (k + 1) * 128] for k in range(depth)], axis=0)
        vg_hbm[:, q] = pltpu.einshape("zcy->czy", v).astype(vg_hbm.dtype)

    order = list(range(1, own - 1)) + [0, own - 1]
    halo_done = False
    src = pay
    copies = []
    slot = 0
    for g, partners in enumerate(steps):
        here_copies = []
        for k, partner in enumerate(partners):
            copy = pltpu.make_async_remote_copy(
                src_ref=src,
                dst_ref=recv.at[slot + k],
                send_sem=send_sem.at[slot + k],
                recv_sem=recv_sem.at[slot + k],
                device_id=partner,
                device_id_type=MESH,
            )
            copy.start()
            here_copies.append(copy)
        todo = order[g * own // len(steps) : (g + 1) * own // len(steps)]
        if (0 in todo or own - 1 in todo) and not halo_done:
            finish_e()
            halo_done = True
        for q in todo:
            conv_plane(q)
        for copy in here_copies:
            copy.wait_recv()
        copies += here_copies
        vals = [src[...]] + [recv[slot + k] for k in range(len(partners))]
        while len(vals) > 1:
            vals = [vals[i] + vals[i + 1] for i in range(0, len(vals), 2)]
        if g == len(steps) - 1:
            sums_ref[...] = vals[0] * factor
        else:
            acc[g] = vals[0]
            src = acc.at[g]
        slot += len(partners)
    for copy in copies:
        copy.wait_send()
    drain_e()


def on_device(volume, cotangent, kernels_xy, kernels_z, mixing):
    _, chans, own, depth, across = volume.shape
    lanes = depth * across
    f32, bf16 = jnp.float32, jnp.bfloat16
    taps = jnp.concatenate(
        [kernels_xy.reshape(2, chans, 9), kernels_z], axis=2
    ).astype(f32)
    ranks = lax.axis_size("sp")
    axes = (("sp", ranks), ("dp", lax.axis_size("dp")))
    groups = exchange_groups(axes, 2)
    slots = sum((1 << len(g)) - 1 for g in groups)
    assert own >= 2 and own % len(groups) == 0 and chans + 12 <= 128
    factor = 1.0 / math.sqrt(lax.axis_size("dp") * own * ranks * depth * across)
    planes = lambda n, t: pltpu.VMEM((n, chans, lanes), t)
    grad_in, sums = pl.pallas_call(
        functools.partial(whole_kernel, axes, groups, factor),
        out_shape=(
            jax.ShapeDtypeStruct((chans, own, depth, across), bf16),
            jax.ShapeDtypeStruct((2, chans, 128), f32),
        ),
        in_specs=[pl.BlockSpec(memory_space=pltpu.VMEM)] * 4,
        out_specs=[pl.BlockSpec(memory_space=pltpu.VMEM)] * 2,
        scratch_shapes=[
            planes(own + 4, bf16),
            planes(own, bf16),
            planes(own, bf16),
            planes(own + 2, bf16),
            planes(own + 2, f32),
            planes(own + 2, bf16),
            planes(own + 2, f32),
            planes(own + 2, bf16),
            planes(own + 2, bf16),
            pltpu.VMEM((2, chans, 128), f32),
            pltpu.VMEM((2, chans, chans), f32),
            pltpu.VMEM((2, 3, chans, 128), f32),
            pltpu.VMEM((2, 9, chans, 128), f32),
            pltpu.VMEM((slots, 2, chans, 128), f32),
            pltpu.VMEM((len(groups), 2, chans, 128), f32),
        ] + [pltpu.SemaphoreType.DMA((2,))] * 6 + [pltpu.SemaphoreType.DMA((slots,))] * 2,
        compiler_params=pltpu.CompilerParams(
            collective_id=0, has_side_effects=True, vmem_limit_bytes=VMEM_LIMIT
        ),
    )(volume[0], cotangent[0], taps, mixing)
    grad_in = grad_in[None]
    mixing_grad = sums[:, :, :chans]
    z_grad = sums[:, :, chans : chans + 3]
    xy_grad = sums[:, :, chans + 3 : chans + 12].reshape(2, chans, 3, 3)
    return (grad_in, mixing_grad, xy_grad, z_grad)


def solution(mesh):
    return jax.shard_map(
        on_device,
        mesh=mesh,
        in_specs=(P("dp", None, "sp", None, None), P("dp", None, "sp", None, None), P(), P(), P()),
        out_specs=(P("dp", None, "sp", None, None), P(), P(), P()),
        check_vma=False,
    )
```

```python
import functools
import math

import jax
import jax.numpy as jnp
from jax import lax
from jax.experimental import pallas as pl
from jax.experimental.pallas import tpu as pltpu
from jax.sharding import PartitionSpec as P

MESH = pl.DeviceIdType.MESH
VMEM_LIMIT = 56 * 1024 * 1024


def exchange_groups(axes, radix_bits):
    bits = []
    for name, size in axes:
        assert size & (size - 1) == 0
        for b in range(size.bit_length() - 1):
            bits.append((name, 1 << b))
    return [bits[i : i + radix_bits] for i in range(0, len(bits), radix_bits)]


def coords(shape):
    lane = lax.broadcasted_iota(jnp.int32, shape, 1)
    return jnp.bitwise_and(lane, 127), jnp.right_shift(lane, 7)


def at_y(a, d, y):
    if d == 0:
        return a
    rolled = pltpu.roll(a, (-d) % a.shape[1], 1)
    return jnp.where((y + d >= 0) & (y + d < 128), rolled, 0.0)


def at_z(a, d, z):
    if d == 0:
        return a
    rolled = pltpu.roll(a, (-128 * d) % a.shape[1], 1)
    return jnp.where((z + d >= 0) & (z + d < a.shape[1] // 128), rolled, 0.0)


def widen(k, lanes):
    return jnp.broadcast_to(k, (k.shape[0], lanes))


def fold(a):
    total = a[:, :128]
    for g in range(1, a.shape[1] // 128):
        total = total + a[:, g * 128 : (g + 1) * 128]
    return total


def sigmoid(u):
    return 1.0 / (1.0 + jnp.exp(-u))


def plane_conv(planes, k_ref, b, flip, y):
    lanes = planes[0].shape[1]
    srcs = [p.astype(jnp.float32) for p in planes]
    total = None
    for j in range(3):
        column = None
        for i in range(3):
            tap = (2 - i) * 3 + (2 - j) if flip else i * 3 + j
            term = widen(k_ref[b, :, tap : tap + 1], lanes) * srcs[i]
            column = term if column is None else column + term
        column = at_y(column, j - 1, y)
        total = column if total is None else total + column
    return total


def depth_conv(a, kz_ref, b, flip, z):
    lanes = a.shape[1]
    total = None
    for t in range(3):
        tap = 2 - t if flip else t
        term = widen(kz_ref[b, :, 9 + tap : 10 + tap], lanes) * at_z(a, t - 1, z)
        total = term if total is None else total + term
    return total


def silu_grad(g, pre):
    s = sigmoid(pre)
    return (g * (s * (1.0 + pre * (1.0 - s)))).astype(jnp.bfloat16)


def weight_grads(b, gpre, ax, gax, pl, gpl, around, mix_ref, kzg_ref, kxyg_ref, y, z):
    mix_ref[b] += lax.dot_general(
        gpre, ax, (((1,), (1,)), ((), ())), preferred_element_type=jnp.float32
    )
    for t in range(3):
        kzg_ref[b, t] += fold(gax * at_z(pl, t - 1, z))
    gplf = gpl.astype(jnp.float32)
    srcs = [a.astype(jnp.float32) for a in around]
    for j in range(3):
        shifted = at_y(gplf, 1 - j, y)
        for i in range(3):
            kxyg_ref[b, i * 3 + j] += fold(shifted * srcs[i])


def whole_kernel(axes, groups, factor, vol_hbm, cot_hbm, kxy_ref, w_ref,
                 vg_hbm, sums_ref,
                 wide, cot_ref, vg_ref, h2, pl1, ax1, pre1, gp2, gp1, pay, mix_ref, kzg_ref, kxyg_ref, recv, acc,
                 in_send, in_recv, g_send, g_recv, e_send, e_recv, h_send, h_recv, send_sem, recv_sem):
    own = cot_ref.shape[0]
    depth = vol_hbm.shape[2]
    kz_ref = kxy_ref
    y, z = coords(cot_ref.shape[1:])

    def to_planes(raw, buf, first):
        for x in range(own):
            v = pltpu.einshape("czy->zcy", raw[:, x].astype(jnp.float32))
            buf[first + x] = jnp.concatenate([v[k] for k in range(depth)], axis=1).astype(buf.dtype)

    here = {name: lax.axis_index(name) for name, _ in axes}
    steps = []
    for group in groups:
        partners = []
        for offset in range(1, 1 << len(group)):
            where = dict(here)
            for k, (name, stride) in enumerate(group):
                if (offset >> k) & 1:
                    bit = (where[name] // stride) % 2
                    where[name] = where[name] + stride * (1 - 2 * bit)
            partners.append(tuple(where[n] for n, _ in axes))
        steps.append(partners)
    sp, last, dp = here["sp"], axes[0][1] - 1, here["dp"]
    left, right = (sp - 1, dp), (sp + 1, dp)
    has_left, has_right = sp > 0, sp < last
    span = 1 << len(groups[0])
    extra_left = has_left & (sp % span == 0)
    extra_right = has_right & (sp % span == span - 1)

    barrier = pltpu.get_barrier_semaphore()
    count = 0
    for partners in steps:
        for partner in partners:
            pl.semaphore_signal(barrier, inc=1, device_id=partner, device_id_type=MESH)
            count += 1

    @pl.when(extra_left)
    def _():
        pl.semaphore_signal(barrier, inc=1, device_id=left, device_id_type=MESH)

    @pl.when(extra_right)
    def _():
        pl.semaphore_signal(barrier, inc=1, device_id=right, device_id_type=MESH)

    to_planes(vol_hbm, wide, 1)
    to_planes(cot_hbm, cot_ref, 0)
    pl.semaphore_wait(barrier, count + extra_left.astype(jnp.int32) + extra_right.astype(jnp.int32))

    def exchange(buf, first, count, send, recv, src, src_first):
        to_left = pltpu.make_async_remote_copy(
            src_ref=src.at[pl.ds(src_first, count)], dst_ref=buf.at[pl.ds(first + own, count)],
            send_sem=send.at[0], recv_sem=recv.at[1], device_id=left, device_id_type=MESH,
        )
        to_right = pltpu.make_async_remote_copy(
            src_ref=src.at[pl.ds(src_first + own - count, count)], dst_ref=buf.at[pl.ds(first - count, count)],
            send_sem=send.at[1], recv_sem=recv.at[0], device_id=right, device_id_type=MESH,
        )
        pl.when(has_left)(to_left.start)
        pl.when(has_right)(to_right.start)

        def finish():
            pl.when(has_left)(to_right.wait_recv)
            pl.when(has_right)(to_left.wait_recv)
            zeros = jnp.zeros((count,) + buf.shape[1:], buf.dtype)

            @pl.when(sp == 0)
            def _():
                buf[pl.ds(first - count, count)] = zeros

            @pl.when(sp == last)
            def _():
                buf[pl.ds(first + own, count)] = zeros

        def drain():
            pl.when(has_left)(to_left.wait_send)
            pl.when(has_right)(to_right.wait_send)

        return finish, drain

    mix_ref[...] = jnp.zeros_like(mix_ref)
    kzg_ref[...] = jnp.zeros_like(kzg_ref)
    kxyg_ref[...] = jnp.zeros_like(kxyg_ref)

    finish_in, drain_in = exchange(wide, 1, 1, in_send, in_recv, wide, 1)

    def forward1(p):
        planar = plane_conv([wide[p + i] for i in range(3)], kxy_ref, 0, False, y)
        axial = depth_conv(planar, kz_ref, 0, False, z).astype(jnp.bfloat16)
        pre = jnp.dot(w_ref[0], axial, preferred_element_type=jnp.float32)
        pl1[p] = planar
        ax1[p] = axial
        pre1[p] = pre
        h2[p + 1] = (pre * sigmoid(pre)).astype(jnp.bfloat16)

    def block2(q):
        around = [h2[q + i] for i in range(3)]
        planar = plane_conv(around, kxy_ref, 1, False, y)
        axial = depth_conv(planar, kz_ref, 1, False, z).astype(jnp.bfloat16)
        pre = jnp.dot(w_ref[1], axial, preferred_element_type=jnp.float32)
        gpre = silu_grad(cot_ref[q].astype(jnp.float32), pre)
        gax = lax.dot_general(w_ref[1], gpre, (((0,), (0,)), ((), ())), preferred_element_type=jnp.float32)
        gpl = depth_conv(gax, kz_ref, 1, True, z).astype(jnp.bfloat16)
        gp2[q + 1] = gpl
        weight_grads(1, gpre, axial, gax, planar, gpl, around, mix_ref, kzg_ref, kxyg_ref, y, z)

    def block1(q):
        g1 = plane_conv([gp2[q + i] for i in range(3)], kxy_ref, 1, True, y).astype(jnp.bfloat16)
        gpre = silu_grad(g1.astype(jnp.float32), pre1[q])
        gax = lax.dot_general(w_ref[0], gpre, (((0,), (0,)), ((), ())), preferred_element_type=jnp.float32)
        gpl = depth_conv(gax, kz_ref, 0, True, z).astype(jnp.bfloat16)
        gp1[q + 1] = gpl
        around = [wide[q + i] for i in range(3)]
        weight_grads(0, gpre, ax1[q], gax, pl1[q], gpl, around, mix_ref, kzg_ref, kxyg_ref, y, z)

    def run(body, lo, hi, place=lambda i: i):
        def step(i, carry):
            body(place(i))
            return carry

        lax.fori_loop(lo, hi, step, 0)

    run(forward1, 1, own - 1)
    finish_in()
    run(forward1, 0, 2, lambda i: i * (own - 1))
    finish_h, drain_h = exchange(h2, 1, 1, h_send, h_recv, h2, 1)
    run(block2, 1, own - 1)
    finish_h()
    run(block2, 0, 2, lambda i: i * (own - 1))
    finish_g, drain_g = exchange(gp2, 1, 1, g_send, g_recv, gp2, 1)
    run(block1, 1, own - 1)
    finish_g()
    run(block1, 0, 2, lambda i: i * (own - 1))
    finish_e, drain_e = exchange(gp1, 1, 1, e_send, e_recv, gp1, 1)
    drain_in()
    drain_h()
    drain_g()

    lane = lax.broadcasted_iota(jnp.int32, pay.shape[1:], 1)
    chans = pay.shape[1]
    for b in range(2):
        packed = jnp.zeros(pay.shape[1:], jnp.float32)
        packed = jnp.where(lane < chans, jnp.concatenate(
            [mix_ref[b], jnp.zeros((chans, pay.shape[2] - chans), jnp.float32)], axis=1), packed)
        for t in range(3):
            packed = jnp.where(lane == chans + t, jnp.sum(kzg_ref[b, t], axis=1, keepdims=True), packed)
        for t in range(9):
            packed = jnp.where(lane == chans + 3 + t, jnp.sum(kxyg_ref[b, t], axis=1, keepdims=True), packed)
        pay[b] = packed


    def conv_plane(q):
        vg_ref[q] = plane_conv([gp1[q + i] for i in range(3)], kxy_ref, 0, True, y).astype(vg_ref.dtype)
        v = vg_ref[q].astype(jnp.float32)
        v = jnp.stack([v[:, k * 128 : (k + 1) * 128] for k in range(depth)], axis=0)
        vg_hbm[:, q] = pltpu.einshape("zcy->czy", v).astype(vg_hbm.dtype)

    order = list(range(1, own - 1)) + [0, own - 1]
    halo_done = False
    src = pay
    copies = []
    slot = 0
    for g, partners in enumerate(steps):
        here_copies = []
        for k, partner in enumerate(partners):
            copy = pltpu.make_async_remote_copy(
                src_ref=src,
                dst_ref=recv.at[slot + k],
                send_sem=send_sem.at[slot + k],
                recv_sem=recv_sem.at[slot + k],
                device_id=partner,
                device_id_type=MESH,
            )
            copy.start()
            here_copies.append(copy)
        todo = order[g * own // len(steps) : (g + 1) * own // len(steps)]
        if (0 in todo or own - 1 in todo) and not halo_done:
            finish_e()
            halo_done = True
        for q in todo:
            conv_plane(q)
        for copy in here_copies:
            copy.wait_recv()
        copies += here_copies
        vals = [src[...]] + [recv[slot + k] for k in range(len(partners))]
        while len(vals) > 1:
            vals = [vals[i] + vals[i + 1] for i in range(0, len(vals), 2)]
        if g == len(steps) - 1:
            sums_ref[...] = vals[0] * factor
        else:
            acc[g] = vals[0]
            src = acc.at[g]
        slot += len(partners)
    for copy in copies:
        copy.wait_send()
    drain_e()


def on_device(volume, cotangent, kernels_xy, kernels_z, mixing):
    _, chans, own, depth, across = volume.shape
    lanes = depth * across
    f32, bf16 = jnp.float32, jnp.bfloat16
    taps = jnp.concatenate(
        [kernels_xy.reshape(2, chans, 9), kernels_z], axis=2
    ).astype(f32)
    ranks = lax.axis_size("sp")
    axes = (("sp", ranks), ("dp", lax.axis_size("dp")))
    groups = exchange_groups(axes, 2)
    slots = sum((1 << len(g)) - 1 for g in groups)
    assert own >= 2 and own % len(groups) == 0 and chans + 12 <= 128
    factor = 1.0 / math.sqrt(lax.axis_size("dp") * own * ranks * depth * across)
    planes = lambda n, t: pltpu.VMEM((n, chans, lanes), t)
    grad_in, sums = pl.pallas_call(
        functools.partial(whole_kernel, axes, groups, factor),
        out_shape=(
            jax.ShapeDtypeStruct((chans, own, depth, across), bf16),
            jax.ShapeDtypeStruct((2, chans, 128), f32),
        ),
        in_specs=[pl.BlockSpec(memory_space=pltpu.VMEM)] * 4,
        out_specs=[pl.BlockSpec(memory_space=pltpu.VMEM)] * 2,
        scratch_shapes=[
            planes(own + 2, bf16),
            planes(own, bf16),
            planes(own, bf16),
            planes(own + 2, bf16),
            planes(own, f32),
            planes(own, bf16),
            planes(own, f32),
            planes(own + 2, bf16),
            planes(own + 2, bf16),
            pltpu.VMEM((2, chans, 128), f32),
            pltpu.VMEM((2, chans, chans), f32),
            pltpu.VMEM((2, 3, chans, 128), f32),
            pltpu.VMEM((2, 9, chans, 128), f32),
            pltpu.VMEM((slots, 2, chans, 128), f32),
            pltpu.VMEM((len(groups), 2, chans, 128), f32),
        ] + [pltpu.SemaphoreType.DMA((2,))] * 8 + [pltpu.SemaphoreType.DMA((slots,))] * 2,
        compiler_params=pltpu.CompilerParams(
            collective_id=0, has_side_effects=True, vmem_limit_bytes=VMEM_LIMIT
        ),
    )(volume[0], cotangent[0], taps, mixing)
    grad_in = grad_in[None]
    mixing_grad = sums[:, :, :chans]
    z_grad = sums[:, :, chans : chans + 3]
    xy_grad = sums[:, :, chans + 3 : chans + 12].reshape(2, chans, 3, 3)
    return (grad_in, mixing_grad, xy_grad, z_grad)


def solution(mesh):
    return jax.shard_map(
        on_device,
        mesh=mesh,
        in_specs=(P("dp", None, "sp", None, None), P("dp", None, "sp", None, None), P(), P(), P()),
        out_specs=(P("dp", None, "sp", None, None), P(), P(), P()),
        check_vma=False,
    )
```

```python
import functools
import math

import jax
import jax.numpy as jnp
from jax import lax
from jax.experimental import pallas as pl
from jax.experimental.pallas import tpu as pltpu
from jax.sharding import PartitionSpec as P

MESH = pl.DeviceIdType.MESH
VMEM_LIMIT = 56 * 1024 * 1024


def exchange_groups(axes, radix_bits):
    bits = []
    for name, size in axes:
        assert size & (size - 1) == 0
        for b in range(size.bit_length() - 1):
            bits.append((name, 1 << b))
    bits = bits[1:]
    return [bits[i : i + radix_bits] for i in range(0, len(bits), radix_bits)]


def coords(shape):
    lane = lax.broadcasted_iota(jnp.int32, shape, 1)
    return jnp.bitwise_and(lane, 127), jnp.right_shift(lane, 7)


def at_y(a, d, y):
    if d == 0:
        return a
    rolled = pltpu.roll(a, (-d) % a.shape[1], 1)
    return jnp.where((y + d >= 0) & (y + d < 128), rolled, 0.0)


def at_z(a, d, z):
    if d == 0:
        return a
    rolled = pltpu.roll(a, (-128 * d) % a.shape[1], 1)
    return jnp.where((z + d >= 0) & (z + d < a.shape[1] // 128), rolled, 0.0)


def widen(k, lanes):
    return jnp.broadcast_to(k, (k.shape[0], lanes))


def fold(a):
    total = a[:, :128]
    for g in range(1, a.shape[1] // 128):
        total = total + a[:, g * 128 : (g + 1) * 128]
    return total


def sigmoid(u):
    return 1.0 / (1.0 + jnp.exp(-u))


def plane_conv(planes, k_ref, b, flip, y):
    lanes = planes[0].shape[1]
    srcs = [p.astype(jnp.float32) for p in planes]
    total = None
    for j in range(3):
        column = None
        for i in range(3):
            tap = (2 - i) * 3 + (2 - j) if flip else i * 3 + j
            term = widen(k_ref[b, :, tap : tap + 1], lanes) * srcs[i]
            column = term if column is None else column + term
        column = at_y(column, j - 1, y)
        total = column if total is None else total + column
    return total


def depth_conv(a, kz_ref, b, flip, z):
    lanes = a.shape[1]
    total = None
    for t in range(3):
        tap = 2 - t if flip else t
        term = widen(kz_ref[b, :, 9 + tap : 10 + tap], lanes) * at_z(a, t - 1, z)
        total = term if total is None else total + term
    return total


def silu_grad(g, pre):
    s = sigmoid(pre)
    return (g * (s * (1.0 + pre * (1.0 - s)))).astype(jnp.bfloat16)


def weight_grads(b, gpre, ax, gax, pl, gpl, around, mix_ref, kzg_ref, kxyg_ref, y, z):
    mix_ref[b] += lax.dot_general(
        gpre, ax, (((1,), (1,)), ((), ())), preferred_element_type=jnp.float32
    )
    for t in range(3):
        kzg_ref[b, t] += fold(gax * at_z(pl, t - 1, z))
    gplf = gpl.astype(jnp.float32)
    srcs = [a.astype(jnp.float32) for a in around]
    for j in range(3):
        shifted = at_y(gplf, 1 - j, y)
        for i in range(3):
            kxyg_ref[b, i * 3 + j] += fold(shifted * srcs[i])


def whole_kernel(axes, groups, factor, vol_hbm, cot_hbm, kxy_ref, w_ref,
                 vg_hbm, sums_ref,
                 wide, cot_ref, vg_ref, h2, pl1, ax1, pre1, gp2, gp1, pay, mix_ref, kzg_ref, kxyg_ref, recv, acc,
                 in_send, in_recv, g_send, g_recv, e_send, e_recv, h_send, h_recv, sw_send, sw_recv, send_sem, recv_sem,
                 half_in, acc0, fin):
    own = cot_ref.shape[0]
    depth = vol_hbm.shape[2]
    kz_ref = kxy_ref
    y, z = coords(cot_ref.shape[1:])

    def to_planes(raw, buf, first):
        for x in range(own):
            v = pltpu.einshape("czy->zcy", raw[:, x].astype(jnp.float32))
            buf[first + x] = jnp.concatenate([v[k] for k in range(depth)], axis=1).astype(buf.dtype)

    here = {name: lax.axis_index(name) for name, _ in axes}
    steps = []
    for group in groups:
        partners = []
        for offset in range(1, 1 << len(group)):
            where = dict(here)
            for k, (name, stride) in enumerate(group):
                if (offset >> k) & 1:
                    bit = (where[name] // stride) % 2
                    where[name] = where[name] + stride * (1 - 2 * bit)
            partners.append(tuple(where[n] for n, _ in axes))
        steps.append(partners)
    sp, last, dp = here["sp"], axes[0][1] - 1, here["dp"]
    left, right = (sp - 1, dp), (sp + 1, dp)
    has_left, has_right = sp > 0, sp < last
    core = sp % 2
    mate = (sp + 1 - 2 * core, dp)
    extra_left = has_left & (core == 0)
    extra_right = has_right & (core == 1)

    barrier = pltpu.get_barrier_semaphore()
    pl.semaphore_signal(barrier, inc=1, device_id=mate, device_id_type=MESH)
    count = 1
    for partners in steps:
        for partner in partners:
            pl.semaphore_signal(barrier, inc=1, device_id=partner, device_id_type=MESH)
            count += 1

    @pl.when(extra_left)
    def _():
        pl.semaphore_signal(barrier, inc=1, device_id=left, device_id_type=MESH)

    @pl.when(extra_right)
    def _():
        pl.semaphore_signal(barrier, inc=1, device_id=right, device_id_type=MESH)

    to_planes(vol_hbm, wide, 1)
    to_planes(cot_hbm, cot_ref, 0)
    pl.semaphore_wait(barrier, count + extra_left.astype(jnp.int32) + extra_right.astype(jnp.int32))

    def exchange(buf, first, count, send, recv, src, src_first):
        to_left = pltpu.make_async_remote_copy(
            src_ref=src.at[pl.ds(src_first, count)], dst_ref=buf.at[pl.ds(first + own, count)],
            send_sem=send.at[0], recv_sem=recv.at[1], device_id=left, device_id_type=MESH,
        )
        to_right = pltpu.make_async_remote_copy(
            src_ref=src.at[pl.ds(src_first + own - count, count)], dst_ref=buf.at[pl.ds(first - count, count)],
            send_sem=send.at[1], recv_sem=recv.at[0], device_id=right, device_id_type=MESH,
        )
        pl.when(has_left)(to_left.start)
        pl.when(has_right)(to_right.start)

        def finish():
            pl.when(has_left)(to_right.wait_recv)
            pl.when(has_right)(to_left.wait_recv)
            zeros = jnp.zeros((count,) + buf.shape[1:], buf.dtype)

            @pl.when(sp == 0)
            def _():
                buf[pl.ds(first - count, count)] = zeros

            @pl.when(sp == last)
            def _():
                buf[pl.ds(first + own, count)] = zeros

        def drain():
            pl.when(has_left)(to_left.wait_send)
            pl.when(has_right)(to_right.wait_send)

        return finish, drain

    mix_ref[...] = jnp.zeros_like(mix_ref)
    kzg_ref[...] = jnp.zeros_like(kzg_ref)
    kxyg_ref[...] = jnp.zeros_like(kxyg_ref)

    finish_in, drain_in = exchange(wide, 1, 1, in_send, in_recv, wide, 1)

    def forward1(p):
        planar = plane_conv([wide[p + i] for i in range(3)], kxy_ref, 0, False, y)
        axial = depth_conv(planar, kz_ref, 0, False, z).astype(jnp.bfloat16)
        pre = jnp.dot(w_ref[0], axial, preferred_element_type=jnp.float32)
        pl1[p] = planar
        ax1[p] = axial
        pre1[p] = pre
        h2[p + 1] = (pre * sigmoid(pre)).astype(jnp.bfloat16)

    def block2(q):
        around = [h2[q + i] for i in range(3)]
        planar = plane_conv(around, kxy_ref, 1, False, y)
        axial = depth_conv(planar, kz_ref, 1, False, z).astype(jnp.bfloat16)
        pre = jnp.dot(w_ref[1], axial, preferred_element_type=jnp.float32)
        gpre = silu_grad(cot_ref[q].astype(jnp.float32), pre)
        gax = lax.dot_general(w_ref[1], gpre, (((0,), (0,)), ((), ())), preferred_element_type=jnp.float32)
        gpl = depth_conv(gax, kz_ref, 1, True, z).astype(jnp.bfloat16)
        gp2[q + 1] = gpl
        weight_grads(1, gpre, axial, gax, planar, gpl, around, mix_ref, kzg_ref, kxyg_ref, y, z)

    def block1(q):
        g1 = plane_conv([gp2[q + i] for i in range(3)], kxy_ref, 1, True, y).astype(jnp.bfloat16)
        gpre = silu_grad(g1.astype(jnp.float32), pre1[q])
        gax = lax.dot_general(w_ref[0], gpre, (((0,), (0,)), ((), ())), preferred_element_type=jnp.float32)
        gpl = depth_conv(gax, kz_ref, 0, True, z).astype(jnp.bfloat16)
        gp1[q + 1] = gpl
        around = [wide[q + i] for i in range(3)]
        weight_grads(0, gpre, ax1[q], gax, pl1[q], gpl, around, mix_ref, kzg_ref, kxyg_ref, y, z)

    def run(body, lo, hi, place=lambda i: i):
        def step(i, carry):
            body(place(i))
            return carry

        lax.fori_loop(lo, hi, step, 0)

    run(forward1, 1, own - 1)
    finish_in()
    run(forward1, 0, 2, lambda i: i * (own - 1))
    finish_h, drain_h = exchange(h2, 1, 1, h_send, h_recv, h2, 1)
    run(block2, 1, own - 1)
    finish_h()
    run(block2, 0, 2, lambda i: i * (own - 1))
    finish_g, drain_g = exchange(gp2, 1, 1, g_send, g_recv, gp2, 1)
    run(block1, 1, own - 1)
    finish_g()
    run(block1, 0, 2, lambda i: i * (own - 1))
    finish_e, drain_e = exchange(gp1, 1, 1, e_send, e_recv, gp1, 1)
    drain_in()
    drain_h()
    drain_g()

    lane = lax.broadcasted_iota(jnp.int32, pay.shape[1:], 1)
    chans = pay.shape[1]
    for b in range(2):
        packed = jnp.zeros(pay.shape[1:], jnp.float32)
        packed = jnp.where(lane < chans, jnp.concatenate(
            [mix_ref[b], jnp.zeros((chans, pay.shape[2] - chans), jnp.float32)], axis=1), packed)
        for t in range(3):
            packed = jnp.where(lane == chans + t, jnp.sum(kzg_ref[b, t], axis=1, keepdims=True), packed)
        for t in range(9):
            packed = jnp.where(lane == chans + 3 + t, jnp.sum(kxyg_ref[b, t], axis=1, keepdims=True), packed)
        pay[b] = packed


    def conv_plane(q):
        vg_ref[q] = plane_conv([gp1[q + i] for i in range(3)], kxy_ref, 0, True, y).astype(vg_ref.dtype)
        v = vg_ref[q].astype(jnp.float32)
        v = jnp.stack([v[:, k * 128 : (k + 1) * 128] for k in range(depth)], axis=0)
        vg_hbm[:, q] = pltpu.einshape("zcy->czy", v).astype(vg_hbm.dtype)

    order = list(range(1, own - 1)) + [0, own - 1]
    halo_done = False
    swap = pltpu.make_async_remote_copy(
        src_ref=pay.at[1 - core], dst_ref=half_in, send_sem=sw_send.at[0], recv_sem=sw_recv.at[0],
        device_id=mate, device_id_type=MESH,
    )
    swap.start()
    swap.wait_recv()
    acc0[...] = pay[core] + half_in[...]
    src = acc0
    copies = []
    slot = 0
    for g, partners in enumerate(steps):
        here_copies = []
        for k, partner in enumerate(partners):
            copy = pltpu.make_async_remote_copy(
                src_ref=src,
                dst_ref=recv.at[slot + k],
                send_sem=send_sem.at[slot + k],
                recv_sem=recv_sem.at[slot + k],
                device_id=partner,
                device_id_type=MESH,
            )
            copy.start()
            here_copies.append(copy)
        todo = order[g * own // len(steps) : (g + 1) * own // len(steps)]
        if (0 in todo or own - 1 in todo) and not halo_done:
            finish_e()
            halo_done = True
        for q in todo:
            conv_plane(q)
        for copy in here_copies:
            copy.wait_recv()
        copies += here_copies
        vals = [src[...]] + [recv[slot + k] for k in range(len(partners))]
        while len(vals) > 1:
            vals = [vals[i] + vals[i + 1] for i in range(0, len(vals), 2)]
        acc[g] = vals[0]
        src = acc.at[g]
        slot += len(partners)
    fin[core] = src[...]
    back = pltpu.make_async_remote_copy(
        src_ref=fin.at[core], dst_ref=fin.at[core], send_sem=sw_send.at[1], recv_sem=sw_recv.at[1],
        device_id=mate, device_id_type=MESH,
    )
    back.start()
    back.wait_recv()
    sums_ref[...] = fin[...] * factor
    for copy in copies:
        copy.wait_send()
    swap.wait_send()
    back.wait_send()
    drain_e()


def on_device(volume, cotangent, kernels_xy, kernels_z, mixing):
    _, chans, own, depth, across = volume.shape
    lanes = depth * across
    f32, bf16 = jnp.float32, jnp.bfloat16
    taps = jnp.concatenate(
        [kernels_xy.reshape(2, chans, 9), kernels_z], axis=2
    ).astype(f32)
    ranks = lax.axis_size("sp")
    axes = (("sp", ranks), ("dp", lax.axis_size("dp")))
    groups = exchange_groups(axes, 2)
    slots = sum((1 << len(g)) - 1 for g in groups)
    assert own >= 2 and own % len(groups) == 0 and chans + 12 <= 128
    factor = 1.0 / math.sqrt(lax.axis_size("dp") * own * ranks * depth * across)
    planes = lambda n, t: pltpu.VMEM((n, chans, lanes), t)
    grad_in, sums = pl.pallas_call(
        functools.partial(whole_kernel, axes, groups, factor),
        out_shape=(
            jax.ShapeDtypeStruct((chans, own, depth, across), bf16),
            jax.ShapeDtypeStruct((2, chans, 128), f32),
        ),
        in_specs=[pl.BlockSpec(memory_space=pltpu.VMEM)] * 4,
        out_specs=[pl.BlockSpec(memory_space=pltpu.VMEM)] * 2,
        scratch_shapes=[
            planes(own + 2, bf16),
            planes(own, bf16),
            planes(own, bf16),
            planes(own + 2, bf16),
            planes(own, f32),
            planes(own, bf16),
            planes(own, f32),
            planes(own + 2, bf16),
            planes(own + 2, bf16),
            pltpu.VMEM((2, chans, 128), f32),
            pltpu.VMEM((2, chans, chans), f32),
            pltpu.VMEM((2, 3, chans, 128), f32),
            pltpu.VMEM((2, 9, chans, 128), f32),
            pltpu.VMEM((slots, chans, 128), f32),
            pltpu.VMEM((len(groups), chans, 128), f32),
        ] + [pltpu.SemaphoreType.DMA((2,))] * 10 + [pltpu.SemaphoreType.DMA((slots,))] * 2 + [
            pltpu.VMEM((chans, 128), f32),
            pltpu.VMEM((chans, 128), f32),
            pltpu.VMEM((2, chans, 128), f32),
        ],
        compiler_params=pltpu.CompilerParams(
            collective_id=0, has_side_effects=True, vmem_limit_bytes=VMEM_LIMIT
        ),
    )(volume[0], cotangent[0], taps, mixing)
    grad_in = grad_in[None]
    mixing_grad = sums[:, :, :chans]
    z_grad = sums[:, :, chans : chans + 3]
    xy_grad = sums[:, :, chans + 3 : chans + 12].reshape(2, chans, 3, 3)
    return (grad_in, mixing_grad, xy_grad, z_grad)


def solution(mesh):
    return jax.shard_map(
        on_device,
        mesh=mesh,
        in_specs=(P("dp", None, "sp", None, None), P("dp", None, "sp", None, None), P(), P(), P()),
        out_specs=(P("dp", None, "sp", None, None), P(), P(), P()),
        check_vma=False,
    )
```

```python
import functools
import math

import jax
import jax.numpy as jnp
from jax import lax
from jax.experimental import pallas as pl
from jax.experimental.pallas import tpu as pltpu
from jax.sharding import PartitionSpec as P

MESH = pl.DeviceIdType.MESH
VMEM_LIMIT = 56 * 1024 * 1024


def exchange_groups(axes, radix_bits):
    bits = []
    for name, size in axes:
        assert size & (size - 1) == 0
        for b in range(size.bit_length() - 1):
            bits.append((name, 1 << b))
    bits = bits[1:]
    return [bits[i : i + radix_bits] for i in range(0, len(bits), radix_bits)]


def coords(shape):
    lane = lax.broadcasted_iota(jnp.int32, shape, 1)
    return jnp.bitwise_and(lane, 127), jnp.right_shift(lane, 7)


def at_y(a, d, y):
    if d == 0:
        return a
    rolled = pltpu.roll(a, (-d) % a.shape[1], 1)
    return jnp.where((y + d >= 0) & (y + d < 128), rolled, 0.0)


def at_z(a, d, z):
    if d == 0:
        return a
    rolled = pltpu.roll(a, (-128 * d) % a.shape[1], 1)
    return jnp.where((z + d >= 0) & (z + d < a.shape[1] // 128), rolled, 0.0)


def widen(k, lanes):
    return jnp.broadcast_to(k, (k.shape[0], lanes))


def fold(a):
    total = a[:, :128]
    for g in range(1, a.shape[1] // 128):
        total = total + a[:, g * 128 : (g + 1) * 128]
    return total


def sigmoid(u):
    return 1.0 / (1.0 + jnp.exp(-u))


def plane_conv(planes, k_ref, b, flip, y):
    lanes = planes[0].shape[1]
    srcs = [p.astype(jnp.float32) for p in planes]
    total = None
    for j in range(3):
        column = None
        for i in range(3):
            tap = (2 - i) * 3 + (2 - j) if flip else i * 3 + j
            term = widen(k_ref[b, :, tap : tap + 1], lanes) * srcs[i]
            column = term if column is None else column + term
        column = at_y(column, j - 1, y)
        total = column if total is None else total + column
    return total


def depth_conv(a, kz_ref, b, flip, z):
    lanes = a.shape[1]
    total = None
    for t in range(3):
        tap = 2 - t if flip else t
        term = widen(kz_ref[b, :, 9 + tap : 10 + tap], lanes) * at_z(a, t - 1, z)
        total = term if total is None else total + term
    return total


def silu_grad(g, pre):
    s = sigmoid(pre)
    return (g * (s * (1.0 + pre * (1.0 - s)))).astype(jnp.bfloat16)


def weight_grads(b, gpre, ax, gax, pl, gpl, around, mix_ref, kzg_ref, kxyg_ref, y, z):
    mix_ref[b] += lax.dot_general(
        gpre, ax, (((1,), (1,)), ((), ())), preferred_element_type=jnp.float32
    )
    for t in range(3):
        kzg_ref[b, t] += fold(gax * at_z(pl, t - 1, z))
    gplf = gpl.astype(jnp.float32)
    srcs = [a.astype(jnp.float32) for a in around]
    for j in range(3):
        shifted = at_y(gplf, 1 - j, y)
        for i in range(3):
            kxyg_ref[b, i * 3 + j] += fold(shifted * srcs[i])


def whole_kernel(axes, groups, factor, vol_hbm, cot_hbm, kxy_ref, w_ref,
                 vg_hbm, sums_ref,
                 wide, cot_ref, vg_ref, h2, pl1, ax1, pre1, gp2, gp1, pay, mix_ref, kzg_ref, kxyg_ref, recv, acc,
                 in_send, in_recv, g_send, g_recv, e_send, e_recv, h_send, h_recv, sw_send, sw_recv, send_sem, recv_sem,
                 half_in, acc0, fin):
    own = cot_ref.shape[0]
    depth = vol_hbm.shape[2]
    kz_ref = kxy_ref
    y, z = coords(cot_ref.shape[1:])

    def to_planes(raw, buf, first):
        for x in range(own):
            v = pltpu.einshape("czy->zcy", raw[:, x].astype(jnp.float32))
            buf[first + x] = jnp.concatenate([v[k] for k in range(depth)], axis=1).astype(buf.dtype)

    here = {name: lax.axis_index(name) for name, _ in axes}
    steps = []
    for group in groups:
        partners = []
        for offset in range(1, 1 << len(group)):
            where = dict(here)
            for k, (name, stride) in enumerate(group):
                if (offset >> k) & 1:
                    bit = (where[name] // stride) % 2
                    where[name] = where[name] + stride * (1 - 2 * bit)
            partners.append(tuple(where[n] for n, _ in axes))
        steps.append(partners)
    sp, last, dp = here["sp"], axes[0][1] - 1, here["dp"]
    left, right = (sp - 1, dp), (sp + 1, dp)
    has_left, has_right = sp > 0, sp < last
    core = sp % 2
    mate = (sp + 1 - 2 * core, dp)
    extra_left = has_left & (core == 0)
    extra_right = has_right & (core == 1)

    barrier = pltpu.get_barrier_semaphore()
    pl.semaphore_signal(barrier, inc=1, device_id=mate, device_id_type=MESH)
    count = 1
    for partners in steps:
        for partner in partners:
            pl.semaphore_signal(barrier, inc=1, device_id=partner, device_id_type=MESH)
            count += 1

    @pl.when(extra_left)
    def _():
        pl.semaphore_signal(barrier, inc=1, device_id=left, device_id_type=MESH)

    @pl.when(extra_right)
    def _():
        pl.semaphore_signal(barrier, inc=1, device_id=right, device_id_type=MESH)

    to_planes(vol_hbm, wide, 1)
    to_planes(cot_hbm, cot_ref, 0)
    pl.semaphore_wait(barrier, count + extra_left.astype(jnp.int32) + extra_right.astype(jnp.int32))

    def exchange(buf, first, count, send, recv, src, src_first):
        to_left = pltpu.make_async_remote_copy(
            src_ref=src.at[pl.ds(src_first, count)], dst_ref=buf.at[pl.ds(first + own, count)],
            send_sem=send.at[0], recv_sem=recv.at[1], device_id=left, device_id_type=MESH,
        )
        to_right = pltpu.make_async_remote_copy(
            src_ref=src.at[pl.ds(src_first + own - count, count)], dst_ref=buf.at[pl.ds(first - count, count)],
            send_sem=send.at[1], recv_sem=recv.at[0], device_id=right, device_id_type=MESH,
        )
        pl.when(has_left)(to_left.start)
        pl.when(has_right)(to_right.start)

        def finish():
            pl.when(has_left)(to_right.wait_recv)
            pl.when(has_right)(to_left.wait_recv)
            zeros = jnp.zeros((count,) + buf.shape[1:], buf.dtype)

            @pl.when(sp == 0)
            def _():
                buf[pl.ds(first - count, count)] = zeros

            @pl.when(sp == last)
            def _():
                buf[pl.ds(first + own, count)] = zeros

        def drain():
            pl.when(has_left)(to_left.wait_send)
            pl.when(has_right)(to_right.wait_send)

        return finish, drain

    mix_ref[...] = jnp.zeros_like(mix_ref)
    kzg_ref[...] = jnp.zeros_like(kzg_ref)
    kxyg_ref[...] = jnp.zeros_like(kxyg_ref)

    finish_in, drain_in = exchange(wide, 1, 1, in_send, in_recv, wide, 1)

    def forward1(p):
        planar = plane_conv([wide[p + i] for i in range(3)], kxy_ref, 0, False, y)
        axial = depth_conv(planar, kz_ref, 0, False, z).astype(jnp.bfloat16)
        pre = jnp.dot(w_ref[0], axial, preferred_element_type=jnp.float32)
        pl1[p] = planar
        ax1[p] = axial
        pre1[p] = pre
        h2[p + 1] = (pre * sigmoid(pre)).astype(jnp.bfloat16)

    def block2(q):
        around = [h2[q + i] for i in range(3)]
        planar = plane_conv(around, kxy_ref, 1, False, y)
        axial = depth_conv(planar, kz_ref, 1, False, z).astype(jnp.bfloat16)
        pre = jnp.dot(w_ref[1], axial, preferred_element_type=jnp.float32)
        gpre = silu_grad(cot_ref[q].astype(jnp.float32), pre)
        gax = lax.dot_general(w_ref[1], gpre, (((0,), (0,)), ((), ())), preferred_element_type=jnp.float32)
        gpl = depth_conv(gax, kz_ref, 1, True, z).astype(jnp.bfloat16)
        gp2[q + 1] = gpl
        weight_grads(1, gpre, axial, gax, planar, gpl, around, mix_ref, kzg_ref, kxyg_ref, y, z)

    def block1(q):
        g1 = plane_conv([gp2[q + i] for i in range(3)], kxy_ref, 1, True, y).astype(jnp.bfloat16)
        gpre = silu_grad(g1.astype(jnp.float32), pre1[q])
        gax = lax.dot_general(w_ref[0], gpre, (((0,), (0,)), ((), ())), preferred_element_type=jnp.float32)
        gpl = depth_conv(gax, kz_ref, 0, True, z).astype(jnp.bfloat16)
        gp1[q + 1] = gpl
        around = [wide[q + i] for i in range(3)]
        weight_grads(0, gpre, ax1[q], gax, pl1[q], gpl, around, mix_ref, kzg_ref, kxyg_ref, y, z)

    def run(body, lo, hi, place=lambda i: i):
        def step(i, carry):
            body(place(i))
            return carry

        lax.fori_loop(lo, hi, step, 0)

    run(forward1, 1, own - 1)
    finish_in()
    run(forward1, 0, 2, lambda i: i * (own - 1))
    finish_h, drain_h = exchange(h2, 1, 1, h_send, h_recv, h2, 1)
    run(block2, 1, own - 1)
    finish_h()
    run(block2, 0, 2, lambda i: i * (own - 1))
    finish_g, drain_g = exchange(gp2, 1, 1, g_send, g_recv, gp2, 1)
    run(block1, 1, own - 1)
    finish_g()
    run(block1, 0, 2, lambda i: i * (own - 1))
    finish_e, drain_e = exchange(gp1, 1, 1, e_send, e_recv, gp1, 1)
    drain_in()
    drain_h()
    drain_g()

    lane = lax.broadcasted_iota(jnp.int32, pay.shape[1:], 1)
    chans = pay.shape[1]
    for b in range(2):
        packed = jnp.zeros(pay.shape[1:], jnp.float32)
        packed = jnp.where(lane < chans, jnp.concatenate(
            [mix_ref[b], jnp.zeros((chans, pay.shape[2] - chans), jnp.float32)], axis=1), packed)
        for t in range(3):
            packed = jnp.where(lane == chans + t, jnp.sum(kzg_ref[b, t], axis=1, keepdims=True), packed)
        for t in range(9):
            packed = jnp.where(lane == chans + 3 + t, jnp.sum(kxyg_ref[b, t], axis=1, keepdims=True), packed)
        pay[b] = packed


    def conv_plane(q):
        vg_ref[q] = plane_conv([gp1[q + i] for i in range(3)], kxy_ref, 0, True, y).astype(vg_ref.dtype)
        v = vg_ref[q].astype(jnp.float32)
        v = jnp.stack([v[:, k * 128 : (k + 1) * 128] for k in range(depth)], axis=0)
        vg_hbm[:, q] = pltpu.einshape("zcy->czy", v).astype(vg_hbm.dtype)

    order = list(range(1, own - 1)) + [0, own - 1]
    halo_done = False
    swap = pltpu.make_async_remote_copy(
        src_ref=pay.at[1 - core], dst_ref=half_in, send_sem=sw_send.at[0], recv_sem=sw_recv.at[0],
        device_id=mate, device_id_type=MESH,
    )
    swap.start()
    conv_plane(order[0])
    order = order[1:]
    swap.wait_recv()
    acc0[...] = pay[core] + half_in[...]
    src = acc0
    copies = []
    slot = 0
    for g, partners in enumerate(steps):
        here_copies = []
        for k, partner in enumerate(partners):
            copy = pltpu.make_async_remote_copy(
                src_ref=src,
                dst_ref=recv.at[slot + k],
                send_sem=send_sem.at[slot + k],
                recv_sem=recv_sem.at[slot + k],
                device_id=partner,
                device_id_type=MESH,
            )
            copy.start()
            here_copies.append(copy)
        todo = order[g * len(order) // len(steps) : (g + 1) * len(order) // len(steps)]
        if (0 in todo or own - 1 in todo) and not halo_done:
            finish_e()
            halo_done = True
        for q in todo:
            conv_plane(q)
        for copy in here_copies:
            copy.wait_recv()
        copies += here_copies
        vals = [src[...]] + [recv[slot + k] for k in range(len(partners))]
        while len(vals) > 1:
            vals = [vals[i] + vals[i + 1] for i in range(0, len(vals), 2)]
        acc[g] = vals[0]
        src = acc.at[g]
        slot += len(partners)
    fin[core] = src[...]
    back = pltpu.make_async_remote_copy(
        src_ref=fin.at[core], dst_ref=fin.at[core], send_sem=sw_send.at[1], recv_sem=sw_recv.at[1],
        device_id=mate, device_id_type=MESH,
    )
    back.start()
    back.wait_recv()
    sums_ref[...] = fin[...] * factor
    for copy in copies:
        copy.wait_send()
    swap.wait_send()
    back.wait_send()
    drain_e()


def on_device(volume, cotangent, kernels_xy, kernels_z, mixing):
    _, chans, own, depth, across = volume.shape
    lanes = depth * across
    f32, bf16 = jnp.float32, jnp.bfloat16
    taps = jnp.concatenate(
        [kernels_xy.reshape(2, chans, 9), kernels_z], axis=2
    ).astype(f32)
    ranks = lax.axis_size("sp")
    axes = (("sp", ranks), ("dp", lax.axis_size("dp")))
    groups = exchange_groups(axes, 2)
    slots = sum((1 << len(g)) - 1 for g in groups)
    assert own >= 3 and chans + 12 <= 128
    factor = 1.0 / math.sqrt(lax.axis_size("dp") * own * ranks * depth * across)
    planes = lambda n, t: pltpu.VMEM((n, chans, lanes), t)
    grad_in, sums = pl.pallas_call(
        functools.partial(whole_kernel, axes, groups, factor),
        out_shape=(
            jax.ShapeDtypeStruct((chans, own, depth, across), bf16),
            jax.ShapeDtypeStruct((2, chans, 128), f32),
        ),
        in_specs=[pl.BlockSpec(memory_space=pltpu.VMEM)] * 4,
        out_specs=[pl.BlockSpec(memory_space=pltpu.VMEM)] * 2,
        scratch_shapes=[
            planes(own + 2, bf16),
            planes(own, bf16),
            planes(own, bf16),
            planes(own + 2, bf16),
            planes(own, f32),
            planes(own, bf16),
            planes(own, f32),
            planes(own + 2, bf16),
            planes(own + 2, bf16),
            pltpu.VMEM((2, chans, 128), f32),
            pltpu.VMEM((2, chans, chans), f32),
            pltpu.VMEM((2, 3, chans, 128), f32),
            pltpu.VMEM((2, 9, chans, 128), f32),
            pltpu.VMEM((slots, chans, 128), f32),
            pltpu.VMEM((len(groups), chans, 128), f32),
        ] + [pltpu.SemaphoreType.DMA((2,))] * 10 + [pltpu.SemaphoreType.DMA((slots,))] * 2 + [
            pltpu.VMEM((chans, 128), f32),
            pltpu.VMEM((chans, 128), f32),
            pltpu.VMEM((2, chans, 128), f32),
        ],
        compiler_params=pltpu.CompilerParams(
            collective_id=0, has_side_effects=True, vmem_limit_bytes=VMEM_LIMIT
        ),
    )(volume[0], cotangent[0], taps, mixing)
    grad_in = grad_in[None]
    mixing_grad = sums[:, :, :chans]
    z_grad = sums[:, :, chans : chans + 3]
    xy_grad = sums[:, :, chans + 3 : chans + 12].reshape(2, chans, 3, 3)
    return (grad_in, mixing_grad, xy_grad, z_grad)


def solution(mesh):
    return jax.shard_map(
        on_device,
        mesh=mesh,
        in_specs=(P("dp", None, "sp", None, None), P("dp", None, "sp", None, None), P(), P(), P()),
        out_specs=(P("dp", None, "sp", None, None), P(), P(), P()),
        check_vma=False,
    )
```

```python
import functools
import math

import jax
import jax.numpy as jnp
from jax import lax
from jax.experimental import pallas as pl
from jax.experimental.pallas import tpu as pltpu
from jax.sharding import PartitionSpec as P

MESH = pl.DeviceIdType.MESH
VMEM_LIMIT = 56 * 1024 * 1024


def exchange_groups(axes, radix_bits):
    bits = []
    for name, size in axes:
        assert size & (size - 1) == 0
        for b in range(size.bit_length() - 1):
            bits.append((name, 1 << b))
    bits = bits[1:]
    sizes = [2, 1, 2, 2] if len(bits) == 7 else [radix_bits] * len(bits)
    groups, at = [], 0
    for size in sizes:
        if at < len(bits):
            groups.append(bits[at : at + size])
            at += size
    return groups


def coords(shape):
    lane = lax.broadcasted_iota(jnp.int32, shape, 1)
    return jnp.bitwise_and(lane, 127), jnp.right_shift(lane, 7)


def at_y(a, d, y):
    if d == 0:
        return a
    rolled = pltpu.roll(a, (-d) % a.shape[1], 1)
    return jnp.where((y + d >= 0) & (y + d < 128), rolled, 0.0)


def at_z(a, d, z):
    if d == 0:
        return a
    rolled = pltpu.roll(a, (-128 * d) % a.shape[1], 1)
    return jnp.where((z + d >= 0) & (z + d < a.shape[1] // 128), rolled, 0.0)


def widen(k, lanes):
    return jnp.broadcast_to(k, (k.shape[0], lanes))


def fold(a):
    total = a[:, :128]
    for g in range(1, a.shape[1] // 128):
        total = total + a[:, g * 128 : (g + 1) * 128]
    return total


def sigmoid(u):
    return 1.0 / (1.0 + jnp.exp(-u))


def plane_conv(planes, k_ref, b, flip, y):
    lanes = planes[0].shape[1]
    srcs = [p.astype(jnp.float32) for p in planes]
    total = None
    for j in range(3):
        column = None
        for i in range(3):
            tap = (2 - i) * 3 + (2 - j) if flip else i * 3 + j
            term = widen(k_ref[b, :, tap : tap + 1], lanes) * srcs[i]
            column = term if column is None else column + term
        column = at_y(column, j - 1, y)
        total = column if total is None else total + column
    return total


def depth_conv(a, kz_ref, b, flip, z):
    lanes = a.shape[1]
    total = None
    for t in range(3):
        tap = 2 - t if flip else t
        term = widen(kz_ref[b, :, 9 + tap : 10 + tap], lanes) * at_z(a, t - 1, z)
        total = term if total is None else total + term
    return total


def silu_grad(g, pre):
    s = sigmoid(pre)
    return (g * (s * (1.0 + pre * (1.0 - s)))).astype(jnp.bfloat16)


def weight_grads(b, gpre, ax, gax, pl, gpl, around, mix_ref, kzg_ref, kxyg_ref, y, z):
    mix_ref[b] += lax.dot_general(
        gpre, ax, (((1,), (1,)), ((), ())), preferred_element_type=jnp.float32
    )
    for t in range(3):
        kzg_ref[b, t] += fold(gax * at_z(pl, t - 1, z))
    gplf = gpl.astype(jnp.float32)
    srcs = [a.astype(jnp.float32) for a in around]
    for j in range(3):
        shifted = at_y(gplf, 1 - j, y)
        for i in range(3):
            kxyg_ref[b, i * 3 + j] += fold(shifted * srcs[i])


def whole_kernel(axes, groups, factor, vol_hbm, cot_hbm, kxy_ref, w_ref,
                 vg_hbm, sums_ref,
                 wide, cot_ref, vg_ref, h2, pl1, ax1, pre1, gp2, gp1, pay, mix_ref, kzg_ref, kxyg_ref, recv, acc,
                 in_send, in_recv, g_send, g_recv, e_send, e_recv, h_send, h_recv, sw_send, sw_recv, send_sem, recv_sem,
                 half_in, acc0, fin):
    own = cot_ref.shape[0]
    depth = vol_hbm.shape[2]
    kz_ref = kxy_ref
    y, z = coords(cot_ref.shape[1:])

    def to_planes(raw, buf, first):
        for x in range(own):
            v = pltpu.einshape("czy->zcy", raw[:, x].astype(jnp.float32))
            buf[first + x] = jnp.concatenate([v[k] for k in range(depth)], axis=1).astype(buf.dtype)

    here = {name: lax.axis_index(name) for name, _ in axes}
    steps = []
    for group in groups:
        partners = []
        for offset in range(1, 1 << len(group)):
            where = dict(here)
            for k, (name, stride) in enumerate(group):
                if (offset >> k) & 1:
                    bit = (where[name] // stride) % 2
                    where[name] = where[name] + stride * (1 - 2 * bit)
            partners.append(tuple(where[n] for n, _ in axes))
        steps.append(partners)
    sp, last, dp = here["sp"], axes[0][1] - 1, here["dp"]
    left, right = (sp - 1, dp), (sp + 1, dp)
    has_left, has_right = sp > 0, sp < last
    core = sp % 2
    mate = (sp + 1 - 2 * core, dp)
    extra_left = has_left & (core == 0)
    extra_right = has_right & (core == 1)

    barrier = pltpu.get_barrier_semaphore()
    pl.semaphore_signal(barrier, inc=1, device_id=mate, device_id_type=MESH)
    count = 1
    for partners in steps:
        for partner in partners:
            pl.semaphore_signal(barrier, inc=1, device_id=partner, device_id_type=MESH)
            count += 1

    @pl.when(extra_left)
    def _():
        pl.semaphore_signal(barrier, inc=1, device_id=left, device_id_type=MESH)

    @pl.when(extra_right)
    def _():
        pl.semaphore_signal(barrier, inc=1, device_id=right, device_id_type=MESH)

    to_planes(vol_hbm, wide, 1)
    to_planes(cot_hbm, cot_ref, 0)
    pl.semaphore_wait(barrier, count + extra_left.astype(jnp.int32) + extra_right.astype(jnp.int32))

    def exchange(buf, first, count, send, recv, src, src_first):
        to_left = pltpu.make_async_remote_copy(
            src_ref=src.at[pl.ds(src_first, count)], dst_ref=buf.at[pl.ds(first + own, count)],
            send_sem=send.at[0], recv_sem=recv.at[1], device_id=left, device_id_type=MESH,
        )
        to_right = pltpu.make_async_remote_copy(
            src_ref=src.at[pl.ds(src_first + own - count, count)], dst_ref=buf.at[pl.ds(first - count, count)],
            send_sem=send.at[1], recv_sem=recv.at[0], device_id=right, device_id_type=MESH,
        )
        pl.when(has_left)(to_left.start)
        pl.when(has_right)(to_right.start)

        def finish():
            pl.when(has_left)(to_right.wait_recv)
            pl.when(has_right)(to_left.wait_recv)
            zeros = jnp.zeros((count,) + buf.shape[1:], buf.dtype)

            @pl.when(sp == 0)
            def _():
                buf[pl.ds(first - count, count)] = zeros

            @pl.when(sp == last)
            def _():
                buf[pl.ds(first + own, count)] = zeros

        def drain():
            pl.when(has_left)(to_left.wait_send)
            pl.when(has_right)(to_right.wait_send)

        return finish, drain

    mix_ref[...] = jnp.zeros_like(mix_ref)
    kzg_ref[...] = jnp.zeros_like(kzg_ref)
    kxyg_ref[...] = jnp.zeros_like(kxyg_ref)

    finish_in, drain_in = exchange(wide, 1, 1, in_send, in_recv, wide, 1)

    def forward1(p):
        planar = plane_conv([wide[p + i] for i in range(3)], kxy_ref, 0, False, y)
        axial = depth_conv(planar, kz_ref, 0, False, z).astype(jnp.bfloat16)
        pre = jnp.dot(w_ref[0], axial, preferred_element_type=jnp.float32)
        pl1[p] = planar
        ax1[p] = axial
        pre1[p] = pre
        h2[p + 1] = (pre * sigmoid(pre)).astype(jnp.bfloat16)

    def block2(q):
        around = [h2[q + i] for i in range(3)]
        planar = plane_conv(around, kxy_ref, 1, False, y)
        axial = depth_conv(planar, kz_ref, 1, False, z).astype(jnp.bfloat16)
        pre = jnp.dot(w_ref[1], axial, preferred_element_type=jnp.float32)
        gpre = silu_grad(cot_ref[q].astype(jnp.float32), pre)
        gax = lax.dot_general(w_ref[1], gpre, (((0,), (0,)), ((), ())), preferred_element_type=jnp.float32)
        gpl = depth_conv(gax, kz_ref, 1, True, z).astype(jnp.bfloat16)
        gp2[q + 1] = gpl
        weight_grads(1, gpre, axial, gax, planar, gpl, around, mix_ref, kzg_ref, kxyg_ref, y, z)

    def block1(q):
        g1 = plane_conv([gp2[q + i] for i in range(3)], kxy_ref, 1, True, y).astype(jnp.bfloat16)
        gpre = silu_grad(g1.astype(jnp.float32), pre1[q])
        gax = lax.dot_general(w_ref[0], gpre, (((0,), (0,)), ((), ())), preferred_element_type=jnp.float32)
        gpl = depth_conv(gax, kz_ref, 0, True, z).astype(jnp.bfloat16)
        gp1[q + 1] = gpl
        around = [wide[q + i] for i in range(3)]
        weight_grads(0, gpre, ax1[q], gax, pl1[q], gpl, around, mix_ref, kzg_ref, kxyg_ref, y, z)

    def run(body, lo, hi, place=lambda i: i):
        def step(i, carry):
            body(place(i))
            return carry

        lax.fori_loop(lo, hi, step, 0)

    run(forward1, 1, own - 1)
    finish_in()
    run(forward1, 0, 2, lambda i: i * (own - 1))
    finish_h, drain_h = exchange(h2, 1, 1, h_send, h_recv, h2, 1)
    run(block2, 1, own - 1)
    finish_h()
    run(block2, 0, 2, lambda i: i * (own - 1))
    finish_g, drain_g = exchange(gp2, 1, 1, g_send, g_recv, gp2, 1)
    run(block1, 1, own - 1)
    finish_g()
    run(block1, 0, 2, lambda i: i * (own - 1))
    finish_e, drain_e = exchange(gp1, 1, 1, e_send, e_recv, gp1, 1)
    drain_in()
    drain_h()
    drain_g()

    lane = lax.broadcasted_iota(jnp.int32, pay.shape[1:], 1)
    chans = pay.shape[1]
    for b in range(2):
        packed = jnp.zeros(pay.shape[1:], jnp.float32)
        packed = jnp.where(lane < chans, jnp.concatenate(
            [mix_ref[b], jnp.zeros((chans, pay.shape[2] - chans), jnp.float32)], axis=1), packed)
        for t in range(3):
            packed = jnp.where(lane == chans + t, jnp.sum(kzg_ref[b, t], axis=1, keepdims=True), packed)
        for t in range(9):
            packed = jnp.where(lane == chans + 3 + t, jnp.sum(kxyg_ref[b, t], axis=1, keepdims=True), packed)
        pay[b] = packed


    def conv_plane(q):
        vg_ref[q] = plane_conv([gp1[q + i] for i in range(3)], kxy_ref, 0, True, y).astype(vg_ref.dtype)
        v = vg_ref[q].astype(jnp.float32)
        v = jnp.stack([v[:, k * 128 : (k + 1) * 128] for k in range(depth)], axis=0)
        vg_hbm[:, q] = pltpu.einshape("zcy->czy", v).astype(vg_hbm.dtype)

    order = list(range(1, own - 1)) + [0, own - 1]
    halo_done = False
    swap = pltpu.make_async_remote_copy(
        src_ref=pay.at[1 - core], dst_ref=half_in, send_sem=sw_send.at[0], recv_sem=sw_recv.at[0],
        device_id=mate, device_id_type=MESH,
    )
    swap.start()
    swap.wait_recv()
    acc0[...] = pay[core] + half_in[...]
    src = acc0
    copies = []
    slot = 0
    for g, partners in enumerate(steps):
        here_copies = []
        for k, partner in enumerate(partners):
            copy = pltpu.make_async_remote_copy(
                src_ref=src,
                dst_ref=recv.at[slot + k],
                send_sem=send_sem.at[slot + k],
                recv_sem=recv_sem.at[slot + k],
                device_id=partner,
                device_id_type=MESH,
            )
            copy.start()
            here_copies.append(copy)
        todo = order[g * own // len(steps) : (g + 1) * own // len(steps)]
        if (0 in todo or own - 1 in todo) and not halo_done:
            finish_e()
            halo_done = True
        for q in todo:
            conv_plane(q)
        for copy in here_copies:
            copy.wait_recv()
        copies += here_copies
        vals = [src[...]] + [recv[slot + k] for k in range(len(partners))]
        while len(vals) > 1:
            vals = [vals[i] + vals[i + 1] for i in range(0, len(vals), 2)]
        acc[g] = vals[0]
        src = acc.at[g]
        slot += len(partners)
    fin[core] = src[...]
    back = pltpu.make_async_remote_copy(
        src_ref=fin.at[core], dst_ref=fin.at[core], send_sem=sw_send.at[1], recv_sem=sw_recv.at[1],
        device_id=mate, device_id_type=MESH,
    )
    back.start()
    back.wait_recv()
    sums_ref[...] = fin[...] * factor
    for copy in copies:
        copy.wait_send()
    swap.wait_send()
    back.wait_send()
    drain_e()


def on_device(volume, cotangent, kernels_xy, kernels_z, mixing):
    _, chans, own, depth, across = volume.shape
    lanes = depth * across
    f32, bf16 = jnp.float32, jnp.bfloat16
    taps = jnp.concatenate(
        [kernels_xy.reshape(2, chans, 9), kernels_z], axis=2
    ).astype(f32)
    ranks = lax.axis_size("sp")
    axes = (("sp", ranks), ("dp", lax.axis_size("dp")))
    groups = exchange_groups(axes, 2)
    slots = sum((1 << len(g)) - 1 for g in groups)
    assert own >= 2 and own % len(groups) == 0 and chans + 12 <= 128
    factor = 1.0 / math.sqrt(lax.axis_size("dp") * own * ranks * depth * across)
    planes = lambda n, t: pltpu.VMEM((n, chans, lanes), t)
    grad_in, sums = pl.pallas_call(
        functools.partial(whole_kernel, axes, groups, factor),
        out_shape=(
            jax.ShapeDtypeStruct((chans, own, depth, across), bf16),
            jax.ShapeDtypeStruct((2, chans, 128), f32),
        ),
        in_specs=[pl.BlockSpec(memory_space=pltpu.VMEM)] * 4,
        out_specs=[pl.BlockSpec(memory_space=pltpu.VMEM)] * 2,
        scratch_shapes=[
            planes(own + 2, bf16),
            planes(own, bf16),
            planes(own, bf16),
            planes(own + 2, bf16),
            planes(own, f32),
            planes(own, bf16),
            planes(own, f32),
            planes(own + 2, bf16),
            planes(own + 2, bf16),
            pltpu.VMEM((2, chans, 128), f32),
            pltpu.VMEM((2, chans, chans), f32),
            pltpu.VMEM((2, 3, chans, 128), f32),
            pltpu.VMEM((2, 9, chans, 128), f32),
            pltpu.VMEM((slots, chans, 128), f32),
            pltpu.VMEM((len(groups), chans, 128), f32),
        ] + [pltpu.SemaphoreType.DMA((2,))] * 10 + [pltpu.SemaphoreType.DMA((slots,))] * 2 + [
            pltpu.VMEM((chans, 128), f32),
            pltpu.VMEM((chans, 128), f32),
            pltpu.VMEM((2, chans, 128), f32),
        ],
        compiler_params=pltpu.CompilerParams(
            collective_id=0, has_side_effects=True, vmem_limit_bytes=VMEM_LIMIT
        ),
    )(volume[0], cotangent[0], taps, mixing)
    grad_in = grad_in[None]
    mixing_grad = sums[:, :, :chans]
    z_grad = sums[:, :, chans : chans + 3]
    xy_grad = sums[:, :, chans + 3 : chans + 12].reshape(2, chans, 3, 3)
    return (grad_in, mixing_grad, xy_grad, z_grad)


def solution(mesh):
    return jax.shard_map(
        on_device,
        mesh=mesh,
        in_specs=(P("dp", None, "sp", None, None), P("dp", None, "sp", None, None), P(), P(), P()),
        out_specs=(P("dp", None, "sp", None, None), P(), P(), P()),
        check_vma=False,
    )
```

```python
import functools
import math

import jax
import jax.numpy as jnp
from jax import lax
from jax.experimental import pallas as pl
from jax.experimental.pallas import tpu as pltpu
from jax.sharding import PartitionSpec as P

MESH = pl.DeviceIdType.MESH
VMEM_LIMIT = 56 * 1024 * 1024


def exchange_groups(axes, radix_bits):
    bits = []
    for name, size in axes:
        assert size & (size - 1) == 0
        for b in range(size.bit_length() - 1):
            bits.append((name, 1 << b))
    bits = bits[1:]
    sizes = [1, 2, 2, 2] if len(bits) == 7 else [radix_bits] * len(bits)
    groups, at = [], 0
    for size in sizes:
        if at < len(bits):
            groups.append(bits[at : at + size])
            at += size
    return groups


def coords(shape):
    lane = lax.broadcasted_iota(jnp.int32, shape, 1)
    return jnp.bitwise_and(lane, 127), jnp.right_shift(lane, 7)


def at_y(a, d, y):
    if d == 0:
        return a
    rolled = pltpu.roll(a, (-d) % a.shape[1], 1)
    return jnp.where((y + d >= 0) & (y + d < 128), rolled, 0.0)


def at_z(a, d, z):
    if d == 0:
        return a
    rolled = pltpu.roll(a, (-128 * d) % a.shape[1], 1)
    return jnp.where((z + d >= 0) & (z + d < a.shape[1] // 128), rolled, 0.0)


def widen(k, lanes):
    return jnp.broadcast_to(k, (k.shape[0], lanes))


def fold(a):
    total = a[:, :128]
    for g in range(1, a.shape[1] // 128):
        total = total + a[:, g * 128 : (g + 1) * 128]
    return total


def sigmoid(u):
    return 1.0 / (1.0 + jnp.exp(-u))


def plane_conv(planes, k_ref, b, flip, y):
    lanes = planes[0].shape[1]
    srcs = [p.astype(jnp.float32) for p in planes]
    total = None
    for j in range(3):
        column = None
        for i in range(3):
            tap = (2 - i) * 3 + (2 - j) if flip else i * 3 + j
            term = widen(k_ref[b, :, tap : tap + 1], lanes) * srcs[i]
            column = term if column is None else column + term
        column = at_y(column, j - 1, y)
        total = column if total is None else total + column
    return total


def depth_conv(a, kz_ref, b, flip, z):
    lanes = a.shape[1]
    total = None
    for t in range(3):
        tap = 2 - t if flip else t
        term = widen(kz_ref[b, :, 9 + tap : 10 + tap], lanes) * at_z(a, t - 1, z)
        total = term if total is None else total + term
    return total


def silu_grad(g, pre):
    s = sigmoid(pre)
    return (g * (s * (1.0 + pre * (1.0 - s)))).astype(jnp.bfloat16)


def weight_grads(b, gpre, ax, gax, pl, gpl, around, mix_ref, kzg_ref, kxyg_ref, y, z):
    mix_ref[b] += lax.dot_general(
        gpre, ax, (((1,), (1,)), ((), ())), preferred_element_type=jnp.float32
    )
    for t in range(3):
        kzg_ref[b, t] += fold(gax * at_z(pl, t - 1, z))
    gplf = gpl.astype(jnp.float32)
    srcs = [a.astype(jnp.float32) for a in around]
    for j in range(3):
        shifted = at_y(gplf, 1 - j, y)
        for i in range(3):
            kxyg_ref[b, i * 3 + j] += fold(shifted * srcs[i])


def whole_kernel(axes, groups, factor, vol_hbm, cot_hbm, kxy_ref, w_ref,
                 vg_hbm, sums_ref,
                 wide, cot_ref, vg_ref, h2, pl1, ax1, pre1, gp2, gp1, pay, mix_ref, kzg_ref, kxyg_ref, recv, acc,
                 in_send, in_recv, g_send, g_recv, e_send, e_recv, h_send, h_recv, sw_send, sw_recv, send_sem, recv_sem,
                 half_in, acc0, fin):
    own = cot_ref.shape[0]
    depth = vol_hbm.shape[2]
    kz_ref = kxy_ref
    y, z = coords(cot_ref.shape[1:])

    def to_planes(raw, buf, first):
        for x in range(own):
            v = pltpu.einshape("czy->zcy", raw[:, x].astype(jnp.float32))
            buf[first + x] = jnp.concatenate([v[k] for k in range(depth)], axis=1).astype(buf.dtype)

    here = {name: lax.axis_index(name) for name, _ in axes}
    steps = []
    for group in groups:
        partners = []
        for offset in range(1, 1 << len(group)):
            where = dict(here)
            for k, (name, stride) in enumerate(group):
                if (offset >> k) & 1:
                    bit = (where[name] // stride) % 2
                    where[name] = where[name] + stride * (1 - 2 * bit)
            partners.append(tuple(where[n] for n, _ in axes))
        steps.append(partners)
    sp, last, dp = here["sp"], axes[0][1] - 1, here["dp"]
    left, right = (sp - 1, dp), (sp + 1, dp)
    has_left, has_right = sp > 0, sp < last
    core = sp % 2
    mate = (sp + 1 - 2 * core, dp)
    extra_left = has_left & (core == 0)
    extra_right = has_right & (core == 1)

    barrier = pltpu.get_barrier_semaphore()
    pl.semaphore_signal(barrier, inc=1, device_id=mate, device_id_type=MESH)
    count = 1
    for partners in steps:
        for partner in partners:
            pl.semaphore_signal(barrier, inc=1, device_id=partner, device_id_type=MESH)
            count += 1

    @pl.when(extra_left)
    def _():
        pl.semaphore_signal(barrier, inc=1, device_id=left, device_id_type=MESH)

    @pl.when(extra_right)
    def _():
        pl.semaphore_signal(barrier, inc=1, device_id=right, device_id_type=MESH)

    to_planes(vol_hbm, wide, 1)
    to_planes(cot_hbm, cot_ref, 0)
    pl.semaphore_wait(barrier, count + extra_left.astype(jnp.int32) + extra_right.astype(jnp.int32))

    def exchange(buf, first, count, send, recv, src, src_first):
        to_left = pltpu.make_async_remote_copy(
            src_ref=src.at[pl.ds(src_first, count)], dst_ref=buf.at[pl.ds(first + own, count)],
            send_sem=send.at[0], recv_sem=recv.at[1], device_id=left, device_id_type=MESH,
        )
        to_right = pltpu.make_async_remote_copy(
            src_ref=src.at[pl.ds(src_first + own - count, count)], dst_ref=buf.at[pl.ds(first - count, count)],
            send_sem=send.at[1], recv_sem=recv.at[0], device_id=right, device_id_type=MESH,
        )
        pl.when(has_left)(to_left.start)
        pl.when(has_right)(to_right.start)

        def finish():
            pl.when(has_left)(to_right.wait_recv)
            pl.when(has_right)(to_left.wait_recv)
            zeros = jnp.zeros((count,) + buf.shape[1:], buf.dtype)

            @pl.when(sp == 0)
            def _():
                buf[pl.ds(first - count, count)] = zeros

            @pl.when(sp == last)
            def _():
                buf[pl.ds(first + own, count)] = zeros

        def drain():
            pl.when(has_left)(to_left.wait_send)
            pl.when(has_right)(to_right.wait_send)

        return finish, drain

    mix_ref[...] = jnp.zeros_like(mix_ref)
    kzg_ref[...] = jnp.zeros_like(kzg_ref)
    kxyg_ref[...] = jnp.zeros_like(kxyg_ref)

    finish_in, drain_in = exchange(wide, 1, 1, in_send, in_recv, wide, 1)

    def forward1(p):
        planar = plane_conv([wide[p + i] for i in range(3)], kxy_ref, 0, False, y)
        axial = depth_conv(planar, kz_ref, 0, False, z).astype(jnp.bfloat16)
        pre = jnp.dot(w_ref[0], axial, preferred_element_type=jnp.float32)
        pl1[p] = planar
        ax1[p] = axial
        pre1[p] = pre
        h2[p + 1] = (pre * sigmoid(pre)).astype(jnp.bfloat16)

    def block2(q):
        around = [h2[q + i] for i in range(3)]
        planar = plane_conv(around, kxy_ref, 1, False, y)
        axial = depth_conv(planar, kz_ref, 1, False, z).astype(jnp.bfloat16)
        pre = jnp.dot(w_ref[1], axial, preferred_element_type=jnp.float32)
        gpre = silu_grad(cot_ref[q].astype(jnp.float32), pre)
        gax = lax.dot_general(w_ref[1], gpre, (((0,), (0,)), ((), ())), preferred_element_type=jnp.float32)
        gpl = depth_conv(gax, kz_ref, 1, True, z).astype(jnp.bfloat16)
        gp2[q + 1] = gpl
        weight_grads(1, gpre, axial, gax, planar, gpl, around, mix_ref, kzg_ref, kxyg_ref, y, z)

    def block1(q):
        g1 = plane_conv([gp2[q + i] for i in range(3)], kxy_ref, 1, True, y).astype(jnp.bfloat16)
        gpre = silu_grad(g1.astype(jnp.float32), pre1[q])
        gax = lax.dot_general(w_ref[0], gpre, (((0,), (0,)), ((), ())), preferred_element_type=jnp.float32)
        gpl = depth_conv(gax, kz_ref, 0, True, z).astype(jnp.bfloat16)
        gp1[q + 1] = gpl
        around = [wide[q + i] for i in range(3)]
        weight_grads(0, gpre, ax1[q], gax, pl1[q], gpl, around, mix_ref, kzg_ref, kxyg_ref, y, z)

    def run(body, lo, hi, place=lambda i: i):
        def step(i, carry):
            body(place(i))
            return carry

        lax.fori_loop(lo, hi, step, 0)

    run(forward1, 1, own - 1)
    finish_in()
    run(forward1, 0, 2, lambda i: i * (own - 1))
    finish_h, drain_h = exchange(h2, 1, 1, h_send, h_recv, h2, 1)
    run(block2, 1, own - 1)
    finish_h()
    run(block2, 0, 2, lambda i: i * (own - 1))
    finish_g, drain_g = exchange(gp2, 1, 1, g_send, g_recv, gp2, 1)
    run(block1, 1, own - 1)
    finish_g()
    run(block1, 0, 2, lambda i: i * (own - 1))
    finish_e, drain_e = exchange(gp1, 1, 1, e_send, e_recv, gp1, 1)
    drain_in()
    drain_h()
    drain_g()

    lane = lax.broadcasted_iota(jnp.int32, pay.shape[1:], 1)
    chans = pay.shape[1]
    for b in range(2):
        packed = jnp.zeros(pay.shape[1:], jnp.float32)
        packed = jnp.where(lane < chans, jnp.concatenate(
            [mix_ref[b], jnp.zeros((chans, pay.shape[2] - chans), jnp.float32)], axis=1), packed)
        for t in range(3):
            packed = jnp.where(lane == chans + t, jnp.sum(kzg_ref[b, t], axis=1, keepdims=True), packed)
        for t in range(9):
            packed = jnp.where(lane == chans + 3 + t, jnp.sum(kxyg_ref[b, t], axis=1, keepdims=True), packed)
        pay[b] = packed


    def conv_plane(q):
        vg_ref[q] = plane_conv([gp1[q + i] for i in range(3)], kxy_ref, 0, True, y).astype(vg_ref.dtype)
        v = vg_ref[q].astype(jnp.float32)
        v = jnp.stack([v[:, k * 128 : (k + 1) * 128] for k in range(depth)], axis=0)
        vg_hbm[:, q] = pltpu.einshape("zcy->czy", v).astype(vg_hbm.dtype)

    order = list(range(1, own - 1)) + [0, own - 1]
    halo_done = False
    swap = pltpu.make_async_remote_copy(
        src_ref=pay.at[1 - core], dst_ref=half_in, send_sem=sw_send.at[0], recv_sem=sw_recv.at[0],
        device_id=mate, device_id_type=MESH,
    )
    swap.start()
    swap.wait_recv()
    acc0[...] = pay[core] + half_in[...]
    src = acc0
    copies = []
    slot = 0
    for g, partners in enumerate(steps):
        here_copies = []
        for k, partner in enumerate(partners):
            copy = pltpu.make_async_remote_copy(
                src_ref=src,
                dst_ref=recv.at[slot + k],
                send_sem=send_sem.at[slot + k],
                recv_sem=recv_sem.at[slot + k],
                device_id=partner,
                device_id_type=MESH,
            )
            copy.start()
            here_copies.append(copy)
        todo = order[g * own // len(steps) : (g + 1) * own // len(steps)]
        if (0 in todo or own - 1 in todo) and not halo_done:
            finish_e()
            halo_done = True
        for q in todo:
            conv_plane(q)
        for copy in here_copies:
            copy.wait_recv()
        copies += here_copies
        vals = [src[...]] + [recv[slot + k] for k in range(len(partners))]
        while len(vals) > 1:
            vals = [vals[i] + vals[i + 1] for i in range(0, len(vals), 2)]
        acc[g] = vals[0]
        src = acc.at[g]
        slot += len(partners)
    fin[core] = src[...]
    back = pltpu.make_async_remote_copy(
        src_ref=fin.at[core], dst_ref=fin.at[core], send_sem=sw_send.at[1], recv_sem=sw_recv.at[1],
        device_id=mate, device_id_type=MESH,
    )
    back.start()
    back.wait_recv()
    sums_ref[...] = fin[...] * factor
    for copy in copies:
        copy.wait_send()
    swap.wait_send()
    back.wait_send()
    drain_e()


def on_device(volume, cotangent, kernels_xy, kernels_z, mixing):
    _, chans, own, depth, across = volume.shape
    lanes = depth * across
    f32, bf16 = jnp.float32, jnp.bfloat16
    taps = jnp.concatenate(
        [kernels_xy.reshape(2, chans, 9), kernels_z], axis=2
    ).astype(f32)
    ranks = lax.axis_size("sp")
    axes = (("sp", ranks), ("dp", lax.axis_size("dp")))
    groups = exchange_groups(axes, 2)
    slots = sum((1 << len(g)) - 1 for g in groups)
    assert own >= 2 and own % len(groups) == 0 and chans + 12 <= 128
    factor = 1.0 / math.sqrt(lax.axis_size("dp") * own * ranks * depth * across)
    planes = lambda n, t: pltpu.VMEM((n, chans, lanes), t)
    grad_in, sums = pl.pallas_call(
        functools.partial(whole_kernel, axes, groups, factor),
        out_shape=(
            jax.ShapeDtypeStruct((chans, own, depth, across), bf16),
            jax.ShapeDtypeStruct((2, chans, 128), f32),
        ),
        in_specs=[pl.BlockSpec(memory_space=pltpu.VMEM)] * 4,
        out_specs=[pl.BlockSpec(memory_space=pltpu.VMEM)] * 2,
        scratch_shapes=[
            planes(own + 2, bf16),
            planes(own, bf16),
            planes(own, bf16),
            planes(own + 2, bf16),
            planes(own, f32),
            planes(own, bf16),
            planes(own, f32),
            planes(own + 2, bf16),
            planes(own + 2, bf16),
            pltpu.VMEM((2, chans, 128), f32),
            pltpu.VMEM((2, chans, chans), f32),
            pltpu.VMEM((2, 3, chans, 128), f32),
            pltpu.VMEM((2, 9, chans, 128), f32),
            pltpu.VMEM((slots, chans, 128), f32),
            pltpu.VMEM((len(groups), chans, 128), f32),
        ] + [pltpu.SemaphoreType.DMA((2,))] * 10 + [pltpu.SemaphoreType.DMA((slots,))] * 2 + [
            pltpu.VMEM((chans, 128), f32),
            pltpu.VMEM((chans, 128), f32),
            pltpu.VMEM((2, chans, 128), f32),
        ],
        compiler_params=pltpu.CompilerParams(
            collective_id=0, has_side_effects=True, vmem_limit_bytes=VMEM_LIMIT
        ),
    )(volume[0], cotangent[0], taps, mixing)
    grad_in = grad_in[None]
    mixing_grad = sums[:, :, :chans]
    z_grad = sums[:, :, chans : chans + 3]
    xy_grad = sums[:, :, chans + 3 : chans + 12].reshape(2, chans, 3, 3)
    return (grad_in, mixing_grad, xy_grad, z_grad)


def solution(mesh):
    return jax.shard_map(
        on_device,
        mesh=mesh,
        in_specs=(P("dp", None, "sp", None, None), P("dp", None, "sp", None, None), P(), P(), P()),
        out_specs=(P("dp", None, "sp", None, None), P(), P(), P()),
        check_vma=False,
    )
```

```python
import functools
import math

import jax
import jax.numpy as jnp
from jax import lax
from jax.experimental import pallas as pl
from jax.experimental.pallas import tpu as pltpu
from jax.sharding import PartitionSpec as P

MESH = pl.DeviceIdType.MESH
VMEM_LIMIT = 56 * 1024 * 1024


def exchange_groups(axes, radix_bits):
    bits = []
    for name, size in axes:
        assert size & (size - 1) == 0
        for b in range(size.bit_length() - 1):
            bits.append((name, 1 << b))
    bits = bits[1:]
    sizes = [1, 2, 2, 2] if len(bits) == 7 else [radix_bits] * len(bits)
    groups, at = [], 0
    for size in sizes:
        if at < len(bits):
            groups.append(bits[at : at + size])
            at += size
    return groups


def coords(shape):
    lane = lax.broadcasted_iota(jnp.int32, shape, 1)
    return jnp.bitwise_and(lane, 127), jnp.right_shift(lane, 7)


def at_y(a, d, y):
    if d == 0:
        return a
    rolled = pltpu.roll(a, (-d) % a.shape[1], 1)
    return jnp.where((y + d >= 0) & (y + d < 128), rolled, 0.0)


def at_z(a, d, z):
    if d == 0:
        return a
    rolled = pltpu.roll(a, (-128 * d) % a.shape[1], 1)
    return jnp.where((z + d >= 0) & (z + d < a.shape[1] // 128), rolled, 0.0)


def widen(k, lanes):
    return jnp.broadcast_to(k, (k.shape[0], lanes))


def fold(a):
    total = a[:, :128]
    for g in range(1, a.shape[1] // 128):
        total = total + a[:, g * 128 : (g + 1) * 128]
    return total


def sigmoid(u):
    return 1.0 / (1.0 + jnp.exp(-u))


def plane_conv(planes, k_ref, b, flip, y):
    lanes = planes[0].shape[1]
    srcs = [p.astype(jnp.float32) for p in planes]
    total = None
    for j in range(3):
        column = None
        for i in range(3):
            tap = (2 - i) * 3 + (2 - j) if flip else i * 3 + j
            term = widen(k_ref[b, :, tap : tap + 1], lanes) * srcs[i]
            column = term if column is None else column + term
        column = at_y(column, j - 1, y)
        total = column if total is None else total + column
    return total


def depth_conv(a, kz_ref, b, flip, z):
    lanes = a.shape[1]
    total = None
    for t in range(3):
        tap = 2 - t if flip else t
        term = widen(kz_ref[b, :, 9 + tap : 10 + tap], lanes) * at_z(a, t - 1, z)
        total = term if total is None else total + term
    return total


def silu_grad(g, pre, s=None):
    s = sigmoid(pre) if s is None else s
    return (g * (s * (1.0 + pre * (1.0 - s)))).astype(jnp.bfloat16)


def weight_grads(b, gpre, ax, gax, pl, gpl, around, mix_ref, kzg_ref, kxyg_ref, y, z):
    mix_ref[b] += lax.dot_general(
        gpre, ax, (((1,), (1,)), ((), ())), preferred_element_type=jnp.float32
    )
    for t in range(3):
        kzg_ref[b, t] += fold(gax * at_z(pl, t - 1, z))
    gplf = gpl.astype(jnp.float32)
    srcs = [a.astype(jnp.float32) for a in around]
    for j in range(3):
        shifted = at_y(gplf, 1 - j, y)
        for i in range(3):
            kxyg_ref[b, i * 3 + j] += fold(shifted * srcs[i])


def whole_kernel(axes, groups, factor, vol_hbm, cot_hbm, kxy_ref, w_ref,
                 vg_hbm, sums_ref,
                 wide, cot_ref, vg_ref, h2, pl1, ax1, pre1, gp2, gp1, pay, mix_ref, kzg_ref, kxyg_ref, recv, acc,
                 in_send, in_recv, g_send, g_recv, e_send, e_recv, h_send, h_recv, sw_send, sw_recv, send_sem, recv_sem,
                 half_in, acc0, fin, sig1):
    own = cot_ref.shape[0]
    depth = vol_hbm.shape[2]
    kz_ref = kxy_ref
    y, z = coords(cot_ref.shape[1:])

    def to_planes(raw, buf, first):
        for x in range(own):
            v = pltpu.einshape("czy->zcy", raw[:, x].astype(jnp.float32))
            buf[first + x] = jnp.concatenate([v[k] for k in range(depth)], axis=1).astype(buf.dtype)

    here = {name: lax.axis_index(name) for name, _ in axes}
    steps = []
    for group in groups:
        partners = []
        for offset in range(1, 1 << len(group)):
            where = dict(here)
            for k, (name, stride) in enumerate(group):
                if (offset >> k) & 1:
                    bit = (where[name] // stride) % 2
                    where[name] = where[name] + stride * (1 - 2 * bit)
            partners.append(tuple(where[n] for n, _ in axes))
        steps.append(partners)
    sp, last, dp = here["sp"], axes[0][1] - 1, here["dp"]
    left, right = (sp - 1, dp), (sp + 1, dp)
    has_left, has_right = sp > 0, sp < last
    core = sp % 2
    mate = (sp + 1 - 2 * core, dp)
    extra_left = has_left & (core == 0)
    extra_right = has_right & (core == 1)

    barrier = pltpu.get_barrier_semaphore()
    pl.semaphore_signal(barrier, inc=1, device_id=mate, device_id_type=MESH)
    count = 1
    for partners in steps:
        for partner in partners:
            pl.semaphore_signal(barrier, inc=1, device_id=partner, device_id_type=MESH)
            count += 1

    @pl.when(extra_left)
    def _():
        pl.semaphore_signal(barrier, inc=1, device_id=left, device_id_type=MESH)

    @pl.when(extra_right)
    def _():
        pl.semaphore_signal(barrier, inc=1, device_id=right, device_id_type=MESH)

    to_planes(vol_hbm, wide, 1)
    to_planes(cot_hbm, cot_ref, 0)
    pl.semaphore_wait(barrier, count + extra_left.astype(jnp.int32) + extra_right.astype(jnp.int32))

    def exchange(buf, first, count, send, recv, src, src_first):
        to_left = pltpu.make_async_remote_copy(
            src_ref=src.at[pl.ds(src_first, count)], dst_ref=buf.at[pl.ds(first + own, count)],
            send_sem=send.at[0], recv_sem=recv.at[1], device_id=left, device_id_type=MESH,
        )
        to_right = pltpu.make_async_remote_copy(
            src_ref=src.at[pl.ds(src_first + own - count, count)], dst_ref=buf.at[pl.ds(first - count, count)],
            send_sem=send.at[1], recv_sem=recv.at[0], device_id=right, device_id_type=MESH,
        )
        pl.when(has_left)(to_left.start)
        pl.when(has_right)(to_right.start)

        def finish():
            pl.when(has_left)(to_right.wait_recv)
            pl.when(has_right)(to_left.wait_recv)
            zeros = jnp.zeros((count,) + buf.shape[1:], buf.dtype)

            @pl.when(sp == 0)
            def _():
                buf[pl.ds(first - count, count)] = zeros

            @pl.when(sp == last)
            def _():
                buf[pl.ds(first + own, count)] = zeros

        def drain():
            pl.when(has_left)(to_left.wait_send)
            pl.when(has_right)(to_right.wait_send)

        return finish, drain

    mix_ref[...] = jnp.zeros_like(mix_ref)
    kzg_ref[...] = jnp.zeros_like(kzg_ref)
    kxyg_ref[...] = jnp.zeros_like(kxyg_ref)

    finish_in, drain_in = exchange(wide, 1, 1, in_send, in_recv, wide, 1)

    def forward1(p):
        planar = plane_conv([wide[p + i] for i in range(3)], kxy_ref, 0, False, y)
        axial = depth_conv(planar, kz_ref, 0, False, z).astype(jnp.bfloat16)
        pre = jnp.dot(w_ref[0], axial, preferred_element_type=jnp.float32)
        pl1[p] = planar
        ax1[p] = axial
        pre1[p] = pre
        s = sigmoid(pre)
        sig1[p] = s
        h2[p + 1] = (pre * s).astype(jnp.bfloat16)

    def block2(q):
        around = [h2[q + i] for i in range(3)]
        planar = plane_conv(around, kxy_ref, 1, False, y)
        axial = depth_conv(planar, kz_ref, 1, False, z).astype(jnp.bfloat16)
        pre = jnp.dot(w_ref[1], axial, preferred_element_type=jnp.float32)
        gpre = silu_grad(cot_ref[q].astype(jnp.float32), pre)
        gax = lax.dot_general(w_ref[1], gpre, (((0,), (0,)), ((), ())), preferred_element_type=jnp.float32)
        gpl = depth_conv(gax, kz_ref, 1, True, z).astype(jnp.bfloat16)
        gp2[q + 1] = gpl
        weight_grads(1, gpre, axial, gax, planar, gpl, around, mix_ref, kzg_ref, kxyg_ref, y, z)

    def block1(q):
        g1 = plane_conv([gp2[q + i] for i in range(3)], kxy_ref, 1, True, y).astype(jnp.bfloat16)
        gpre = silu_grad(g1.astype(jnp.float32), pre1[q], sig1[q])
        gax = lax.dot_general(w_ref[0], gpre, (((0,), (0,)), ((), ())), preferred_element_type=jnp.float32)
        gpl = depth_conv(gax, kz_ref, 0, True, z).astype(jnp.bfloat16)
        gp1[q + 1] = gpl
        around = [wide[q + i] for i in range(3)]
        weight_grads(0, gpre, ax1[q], gax, pl1[q], gpl, around, mix_ref, kzg_ref, kxyg_ref, y, z)

    def run(body, lo, hi, place=lambda i: i):
        def step(i, carry):
            body(place(i))
            return carry

        lax.fori_loop(lo, hi, step, 0)

    run(forward1, 1, own - 1)
    finish_in()
    run(forward1, 0, 2, lambda i: i * (own - 1))
    finish_h, drain_h = exchange(h2, 1, 1, h_send, h_recv, h2, 1)
    run(block2, 1, own - 1)
    finish_h()
    run(block2, 0, 2, lambda i: i * (own - 1))
    finish_g, drain_g = exchange(gp2, 1, 1, g_send, g_recv, gp2, 1)
    run(block1, 1, own - 1)
    finish_g()
    run(block1, 0, 2, lambda i: i * (own - 1))
    finish_e, drain_e = exchange(gp1, 1, 1, e_send, e_recv, gp1, 1)
    drain_in()
    drain_h()
    drain_g()

    lane = lax.broadcasted_iota(jnp.int32, pay.shape[1:], 1)
    chans = pay.shape[1]
    for b in range(2):
        packed = jnp.zeros(pay.shape[1:], jnp.float32)
        packed = jnp.where(lane < chans, jnp.concatenate(
            [mix_ref[b], jnp.zeros((chans, pay.shape[2] - chans), jnp.float32)], axis=1), packed)
        for t in range(3):
            packed = jnp.where(lane == chans + t, jnp.sum(kzg_ref[b, t], axis=1, keepdims=True), packed)
        for t in range(9):
            packed = jnp.where(lane == chans + 3 + t, jnp.sum(kxyg_ref[b, t], axis=1, keepdims=True), packed)
        pay[b] = packed


    def conv_plane(q):
        vg_ref[q] = plane_conv([gp1[q + i] for i in range(3)], kxy_ref, 0, True, y).astype(vg_ref.dtype)
        v = vg_ref[q].astype(jnp.float32)
        v = jnp.stack([v[:, k * 128 : (k + 1) * 128] for k in range(depth)], axis=0)
        vg_hbm[:, q] = pltpu.einshape("zcy->czy", v).astype(vg_hbm.dtype)

    order = list(range(1, own - 1)) + [0, own - 1]
    halo_done = False
    swap = pltpu.make_async_remote_copy(
        src_ref=pay.at[1 - core], dst_ref=half_in, send_sem=sw_send.at[0], recv_sem=sw_recv.at[0],
        device_id=mate, device_id_type=MESH,
    )
    swap.start()
    swap.wait_recv()
    acc0[...] = pay[core] + half_in[...]
    src = acc0
    copies = []
    slot = 0
    for g, partners in enumerate(steps):
        here_copies = []
        for k, partner in enumerate(partners):
            copy = pltpu.make_async_remote_copy(
                src_ref=src,
                dst_ref=recv.at[slot + k],
                send_sem=send_sem.at[slot + k],
                recv_sem=recv_sem.at[slot + k],
                device_id=partner,
                device_id_type=MESH,
            )
            copy.start()
            here_copies.append(copy)
        todo = order[g * own // len(steps) : (g + 1) * own // len(steps)]
        if (0 in todo or own - 1 in todo) and not halo_done:
            finish_e()
            halo_done = True
        for q in todo:
            conv_plane(q)
        for copy in here_copies:
            copy.wait_recv()
        copies += here_copies
        vals = [src[...]] + [recv[slot + k] for k in range(len(partners))]
        while len(vals) > 1:
            vals = [vals[i] + vals[i + 1] for i in range(0, len(vals), 2)]
        acc[g] = vals[0]
        src = acc.at[g]
        slot += len(partners)
    fin[core] = src[...]
    back = pltpu.make_async_remote_copy(
        src_ref=fin.at[core], dst_ref=fin.at[core], send_sem=sw_send.at[1], recv_sem=sw_recv.at[1],
        device_id=mate, device_id_type=MESH,
    )
    back.start()
    back.wait_recv()
    sums_ref[...] = fin[...] * factor
    for copy in copies:
        copy.wait_send()
    swap.wait_send()
    back.wait_send()
    drain_e()


def on_device(volume, cotangent, kernels_xy, kernels_z, mixing):
    _, chans, own, depth, across = volume.shape
    lanes = depth * across
    f32, bf16 = jnp.float32, jnp.bfloat16
    taps = jnp.concatenate(
        [kernels_xy.reshape(2, chans, 9), kernels_z], axis=2
    ).astype(f32)
    ranks = lax.axis_size("sp")
    axes = (("sp", ranks), ("dp", lax.axis_size("dp")))
    groups = exchange_groups(axes, 2)
    slots = sum((1 << len(g)) - 1 for g in groups)
    assert own >= 2 and own % len(groups) == 0 and chans + 12 <= 128
    factor = 1.0 / math.sqrt(lax.axis_size("dp") * own * ranks * depth * across)
    planes = lambda n, t: pltpu.VMEM((n, chans, lanes), t)
    grad_in, sums = pl.pallas_call(
        functools.partial(whole_kernel, axes, groups, factor),
        out_shape=(
            jax.ShapeDtypeStruct((chans, own, depth, across), bf16),
            jax.ShapeDtypeStruct((2, chans, 128), f32),
        ),
        in_specs=[pl.BlockSpec(memory_space=pltpu.VMEM)] * 4,
        out_specs=[pl.BlockSpec(memory_space=pltpu.VMEM)] * 2,
        scratch_shapes=[
            planes(own + 2, bf16),
            planes(own, bf16),
            planes(own, bf16),
            planes(own + 2, bf16),
            planes(own, f32),
            planes(own, bf16),
            planes(own, f32),
            planes(own + 2, bf16),
            planes(own + 2, bf16),
            pltpu.VMEM((2, chans, 128), f32),
            pltpu.VMEM((2, chans, chans), f32),
            pltpu.VMEM((2, 3, chans, 128), f32),
            pltpu.VMEM((2, 9, chans, 128), f32),
            pltpu.VMEM((slots, chans, 128), f32),
            pltpu.VMEM((len(groups), chans, 128), f32),
        ] + [pltpu.SemaphoreType.DMA((2,))] * 10 + [pltpu.SemaphoreType.DMA((slots,))] * 2 + [
            pltpu.VMEM((chans, 128), f32),
            pltpu.VMEM((chans, 128), f32),
            pltpu.VMEM((2, chans, 128), f32),
            planes(own, f32),
        ],
        compiler_params=pltpu.CompilerParams(
            collective_id=0, has_side_effects=True, vmem_limit_bytes=VMEM_LIMIT
        ),
    )(volume[0], cotangent[0], taps, mixing)
    grad_in = grad_in[None]
    mixing_grad = sums[:, :, :chans]
    z_grad = sums[:, :, chans : chans + 3]
    xy_grad = sums[:, :, chans + 3 : chans + 12].reshape(2, chans, 3, 3)
    return (grad_in, mixing_grad, xy_grad, z_grad)


def solution(mesh):
    return jax.shard_map(
        on_device,
        mesh=mesh,
        in_specs=(P("dp", None, "sp", None, None), P("dp", None, "sp", None, None), P(), P(), P()),
        out_specs=(P("dp", None, "sp", None, None), P(), P(), P()),
        check_vma=False,
    )
```

```python
import functools
import math

import jax
import jax.numpy as jnp
from jax import lax
from jax.experimental import pallas as pl
from jax.experimental.pallas import tpu as pltpu
from jax.sharding import PartitionSpec as P

MESH = pl.DeviceIdType.MESH
VMEM_LIMIT = 56 * 1024 * 1024


def exchange_groups(axes, radix_bits):
    bits = []
    for name, size in axes:
        assert size & (size - 1) == 0
        for b in range(size.bit_length() - 1):
            bits.append((name, 1 << b))
    bits = bits[1:]
    if len(bits) == 7:
        return [[bits[i] for i in group] for group in ((1, 2), (3, 4), (0, 5, 6))]
    return [bits[i : i + radix_bits] for i in range(0, len(bits), radix_bits)]


def coords(shape):
    lane = lax.broadcasted_iota(jnp.int32, shape, 1)
    return jnp.bitwise_and(lane, 127), jnp.right_shift(lane, 7)


def at_y(a, d, y):
    if d == 0:
        return a
    rolled = pltpu.roll(a, (-d) % a.shape[1], 1)
    return jnp.where((y + d >= 0) & (y + d < 128), rolled, 0.0)


def at_z(a, d, z):
    if d == 0:
        return a
    rolled = pltpu.roll(a, (-128 * d) % a.shape[1], 1)
    return jnp.where((z + d >= 0) & (z + d < a.shape[1] // 128), rolled, 0.0)


def widen(k, lanes):
    return jnp.broadcast_to(k, (k.shape[0], lanes))


def fold(a):
    total = a[:, :128]
    for g in range(1, a.shape[1] // 128):
        total = total + a[:, g * 128 : (g + 1) * 128]
    return total


def sigmoid(u):
    return 1.0 / (1.0 + jnp.exp(-u))


def plane_conv(planes, k_ref, b, flip, y):
    lanes = planes[0].shape[1]
    srcs = [p.astype(jnp.float32) for p in planes]
    total = None
    for j in range(3):
        column = None
        for i in range(3):
            tap = (2 - i) * 3 + (2 - j) if flip else i * 3 + j
            term = widen(k_ref[b, :, tap : tap + 1], lanes) * srcs[i]
            column = term if column is None else column + term
        column = at_y(column, j - 1, y)
        total = column if total is None else total + column
    return total


def depth_conv(a, kz_ref, b, flip, z):
    lanes = a.shape[1]
    total = None
    for t in range(3):
        tap = 2 - t if flip else t
        term = widen(kz_ref[b, :, 9 + tap : 10 + tap], lanes) * at_z(a, t - 1, z)
        total = term if total is None else total + term
    return total


def silu_grad(g, pre, s=None):
    s = sigmoid(pre) if s is None else s
    return (g * (s * (1.0 + pre * (1.0 - s)))).astype(jnp.bfloat16)


def weight_grads(b, gpre, ax, gax, pl, gpl, around, mix_ref, kzg_ref, kxyg_ref, y, z):
    mix_ref[b] += lax.dot_general(
        gpre, ax, (((1,), (1,)), ((), ())), preferred_element_type=jnp.float32
    )
    for t in range(3):
        kzg_ref[b, t] += fold(gax * at_z(pl, t - 1, z))
    gplf = gpl.astype(jnp.float32)
    srcs = [a.astype(jnp.float32) for a in around]
    for j in range(3):
        shifted = at_y(gplf, 1 - j, y)
        for i in range(3):
            kxyg_ref[b, i * 3 + j] += fold(shifted * srcs[i])


def whole_kernel(axes, groups, factor, vol_hbm, cot_hbm, kxy_ref, w_ref,
                 vg_hbm, sums_ref,
                 wide, cot_ref, vg_ref, h2, pl1, ax1, pre1, gp2, gp1, pay, mix_ref, kzg_ref, kxyg_ref, recv, acc,
                 in_send, in_recv, g_send, g_recv, e_send, e_recv, h_send, h_recv, sw_send, sw_recv, send_sem, recv_sem,
                 half_in, acc0, fin, sig1):
    own = cot_ref.shape[0]
    depth = vol_hbm.shape[2]
    kz_ref = kxy_ref
    y, z = coords(cot_ref.shape[1:])

    def to_planes(raw, buf, first):
        for x in range(own):
            v = pltpu.einshape("czy->zcy", raw[:, x].astype(jnp.float32))
            buf[first + x] = jnp.concatenate([v[k] for k in range(depth)], axis=1).astype(buf.dtype)

    here = {name: lax.axis_index(name) for name, _ in axes}
    steps = []
    for group in groups:
        partners = []
        for offset in range(1, 1 << len(group)):
            where = dict(here)
            for k, (name, stride) in enumerate(group):
                if (offset >> k) & 1:
                    bit = (where[name] // stride) % 2
                    where[name] = where[name] + stride * (1 - 2 * bit)
            partners.append(tuple(where[n] for n, _ in axes))
        steps.append(partners)
    sp, last, dp = here["sp"], axes[0][1] - 1, here["dp"]
    left, right = (sp - 1, dp), (sp + 1, dp)
    has_left, has_right = sp > 0, sp < last
    core = sp % 2
    mate = (sp + 1 - 2 * core, dp)
    extra_left = has_left & (core == 0)
    extra_right = has_right & (core == 1)

    barrier = pltpu.get_barrier_semaphore()
    pl.semaphore_signal(barrier, inc=1, device_id=mate, device_id_type=MESH)
    count = 1
    for partners in steps:
        for partner in partners:
            pl.semaphore_signal(barrier, inc=1, device_id=partner, device_id_type=MESH)
            count += 1

    @pl.when(extra_left)
    def _():
        pl.semaphore_signal(barrier, inc=1, device_id=left, device_id_type=MESH)

    @pl.when(extra_right)
    def _():
        pl.semaphore_signal(barrier, inc=1, device_id=right, device_id_type=MESH)

    to_planes(vol_hbm, wide, 1)
    to_planes(cot_hbm, cot_ref, 0)
    pl.semaphore_wait(barrier, count + extra_left.astype(jnp.int32) + extra_right.astype(jnp.int32))

    def exchange(buf, first, count, send, recv, src, src_first):
        to_left = pltpu.make_async_remote_copy(
            src_ref=src.at[pl.ds(src_first, count)], dst_ref=buf.at[pl.ds(first + own, count)],
            send_sem=send.at[0], recv_sem=recv.at[1], device_id=left, device_id_type=MESH,
        )
        to_right = pltpu.make_async_remote_copy(
            src_ref=src.at[pl.ds(src_first + own - count, count)], dst_ref=buf.at[pl.ds(first - count, count)],
            send_sem=send.at[1], recv_sem=recv.at[0], device_id=right, device_id_type=MESH,
        )
        pl.when(has_left)(to_left.start)
        pl.when(has_right)(to_right.start)

        def finish():
            pl.when(has_left)(to_right.wait_recv)
            pl.when(has_right)(to_left.wait_recv)
            zeros = jnp.zeros((count,) + buf.shape[1:], buf.dtype)

            @pl.when(sp == 0)
            def _():
                buf[pl.ds(first - count, count)] = zeros

            @pl.when(sp == last)
            def _():
                buf[pl.ds(first + own, count)] = zeros

        def drain():
            pl.when(has_left)(to_left.wait_send)
            pl.when(has_right)(to_right.wait_send)

        return finish, drain

    mix_ref[...] = jnp.zeros_like(mix_ref)
    kzg_ref[...] = jnp.zeros_like(kzg_ref)
    kxyg_ref[...] = jnp.zeros_like(kxyg_ref)

    finish_in, drain_in = exchange(wide, 1, 1, in_send, in_recv, wide, 1)

    def forward1(p):
        planar = plane_conv([wide[p + i] for i in range(3)], kxy_ref, 0, False, y)
        axial = depth_conv(planar, kz_ref, 0, False, z).astype(jnp.bfloat16)
        pre = jnp.dot(w_ref[0], axial, preferred_element_type=jnp.float32)
        pl1[p] = planar
        ax1[p] = axial
        pre1[p] = pre
        s = sigmoid(pre)
        sig1[p] = s
        h2[p + 1] = (pre * s).astype(jnp.bfloat16)

    def block2(q):
        around = [h2[q + i] for i in range(3)]
        planar = plane_conv(around, kxy_ref, 1, False, y)
        axial = depth_conv(planar, kz_ref, 1, False, z).astype(jnp.bfloat16)
        pre = jnp.dot(w_ref[1], axial, preferred_element_type=jnp.float32)
        gpre = silu_grad(cot_ref[q].astype(jnp.float32), pre)
        gax = lax.dot_general(w_ref[1], gpre, (((0,), (0,)), ((), ())), preferred_element_type=jnp.float32)
        gpl = depth_conv(gax, kz_ref, 1, True, z).astype(jnp.bfloat16)
        gp2[q + 1] = gpl
        weight_grads(1, gpre, axial, gax, planar, gpl, around, mix_ref, kzg_ref, kxyg_ref, y, z)

    def block1(q):
        g1 = plane_conv([gp2[q + i] for i in range(3)], kxy_ref, 1, True, y).astype(jnp.bfloat16)
        gpre = silu_grad(g1.astype(jnp.float32), pre1[q], sig1[q])
        gax = lax.dot_general(w_ref[0], gpre, (((0,), (0,)), ((), ())), preferred_element_type=jnp.float32)
        gpl = depth_conv(gax, kz_ref, 0, True, z).astype(jnp.bfloat16)
        gp1[q + 1] = gpl
        around = [wide[q + i] for i in range(3)]
        weight_grads(0, gpre, ax1[q], gax, pl1[q], gpl, around, mix_ref, kzg_ref, kxyg_ref, y, z)

    def run(body, lo, hi, place=lambda i: i):
        def step(i, carry):
            body(place(i))
            return carry

        lax.fori_loop(lo, hi, step, 0)

    run(forward1, 1, own - 1)
    finish_in()
    run(forward1, 0, 2, lambda i: i * (own - 1))
    finish_h, drain_h = exchange(h2, 1, 1, h_send, h_recv, h2, 1)
    run(block2, 1, own - 1)
    finish_h()
    run(block2, 0, 2, lambda i: i * (own - 1))
    finish_g, drain_g = exchange(gp2, 1, 1, g_send, g_recv, gp2, 1)
    run(block1, 1, own - 1)
    finish_g()
    run(block1, 0, 2, lambda i: i * (own - 1))
    finish_e, drain_e = exchange(gp1, 1, 1, e_send, e_recv, gp1, 1)
    drain_in()
    drain_h()
    drain_g()

    lane = lax.broadcasted_iota(jnp.int32, pay.shape[1:], 1)
    chans = pay.shape[1]
    for b in range(2):
        packed = jnp.zeros(pay.shape[1:], jnp.float32)
        packed = jnp.where(lane < chans, jnp.concatenate(
            [mix_ref[b], jnp.zeros((chans, pay.shape[2] - chans), jnp.float32)], axis=1), packed)
        for t in range(3):
            packed = jnp.where(lane == chans + t, jnp.sum(kzg_ref[b, t], axis=1, keepdims=True), packed)
        for t in range(9):
            packed = jnp.where(lane == chans + 3 + t, jnp.sum(kxyg_ref[b, t], axis=1, keepdims=True), packed)
        pay[b] = packed


    def conv_plane(q):
        vg_ref[q] = plane_conv([gp1[q + i] for i in range(3)], kxy_ref, 0, True, y).astype(vg_ref.dtype)
        v = vg_ref[q].astype(jnp.float32)
        v = jnp.stack([v[:, k * 128 : (k + 1) * 128] for k in range(depth)], axis=0)
        vg_hbm[:, q] = pltpu.einshape("zcy->czy", v).astype(vg_hbm.dtype)

    order = list(range(1, own - 1)) + [0, own - 1]
    halo_done = False
    swap = pltpu.make_async_remote_copy(
        src_ref=pay.at[1 - core], dst_ref=half_in, send_sem=sw_send.at[0], recv_sem=sw_recv.at[0],
        device_id=mate, device_id_type=MESH,
    )
    swap.start()
    swap.wait_recv()
    acc0[...] = pay[core] + half_in[...]
    src = acc0
    copies = []
    slot = 0
    for g, partners in enumerate(steps):
        here_copies = []
        for k, partner in enumerate(partners):
            copy = pltpu.make_async_remote_copy(
                src_ref=src,
                dst_ref=recv.at[slot + k],
                send_sem=send_sem.at[slot + k],
                recv_sem=recv_sem.at[slot + k],
                device_id=partner,
                device_id_type=MESH,
            )
            copy.start()
            here_copies.append(copy)
        todo = order[g * own // len(steps) : (g + 1) * own // len(steps)]
        if (0 in todo or own - 1 in todo) and not halo_done:
            finish_e()
            halo_done = True
        for q in todo:
            conv_plane(q)
        for copy in here_copies:
            copy.wait_recv()
        copies += here_copies
        vals = [src[...]] + [recv[slot + k] for k in range(len(partners))]
        while len(vals) > 1:
            vals = [vals[i] + vals[i + 1] for i in range(0, len(vals), 2)]
        acc[g] = vals[0]
        src = acc.at[g]
        slot += len(partners)
    fin[core] = src[...]
    back = pltpu.make_async_remote_copy(
        src_ref=fin.at[core], dst_ref=fin.at[core], send_sem=sw_send.at[1], recv_sem=sw_recv.at[1],
        device_id=mate, device_id_type=MESH,
    )
    back.start()
    back.wait_recv()
    sums_ref[...] = fin[...] * factor
    for copy in copies:
        copy.wait_send()
    swap.wait_send()
    back.wait_send()
    drain_e()


def on_device(volume, cotangent, kernels_xy, kernels_z, mixing):
    _, chans, own, depth, across = volume.shape
    lanes = depth * across
    f32, bf16 = jnp.float32, jnp.bfloat16
    taps = jnp.concatenate(
        [kernels_xy.reshape(2, chans, 9), kernels_z], axis=2
    ).astype(f32)
    ranks = lax.axis_size("sp")
    axes = (("sp", ranks), ("dp", lax.axis_size("dp")))
    groups = exchange_groups(axes, 2)
    slots = sum((1 << len(g)) - 1 for g in groups)
    assert own >= 2 and chans + 12 <= 128
    factor = 1.0 / math.sqrt(lax.axis_size("dp") * own * ranks * depth * across)
    planes = lambda n, t: pltpu.VMEM((n, chans, lanes), t)
    grad_in, sums = pl.pallas_call(
        functools.partial(whole_kernel, axes, groups, factor),
        out_shape=(
            jax.ShapeDtypeStruct((chans, own, depth, across), bf16),
            jax.ShapeDtypeStruct((2, chans, 128), f32),
        ),
        in_specs=[pl.BlockSpec(memory_space=pltpu.VMEM)] * 4,
        out_specs=[pl.BlockSpec(memory_space=pltpu.VMEM)] * 2,
        scratch_shapes=[
            planes(own + 2, bf16),
            planes(own, bf16),
            planes(own, bf16),
            planes(own + 2, bf16),
            planes(own, f32),
            planes(own, bf16),
            planes(own, f32),
            planes(own + 2, bf16),
            planes(own + 2, bf16),
            pltpu.VMEM((2, chans, 128), f32),
            pltpu.VMEM((2, chans, chans), f32),
            pltpu.VMEM((2, 3, chans, 128), f32),
            pltpu.VMEM((2, 9, chans, 128), f32),
            pltpu.VMEM((slots, chans, 128), f32),
            pltpu.VMEM((len(groups), chans, 128), f32),
        ] + [pltpu.SemaphoreType.DMA((2,))] * 10 + [pltpu.SemaphoreType.DMA((slots,))] * 2 + [
            pltpu.VMEM((chans, 128), f32),
            pltpu.VMEM((chans, 128), f32),
            pltpu.VMEM((2, chans, 128), f32),
            planes(own, f32),
        ],
        compiler_params=pltpu.CompilerParams(
            collective_id=0, has_side_effects=True, vmem_limit_bytes=VMEM_LIMIT
        ),
    )(volume[0], cotangent[0], taps, mixing)
    grad_in = grad_in[None]
    mixing_grad = sums[:, :, :chans]
    z_grad = sums[:, :, chans : chans + 3]
    xy_grad = sums[:, :, chans + 3 : chans + 12].reshape(2, chans, 3, 3)
    return (grad_in, mixing_grad, xy_grad, z_grad)


def solution(mesh):
    return jax.shard_map(
        on_device,
        mesh=mesh,
        in_specs=(P("dp", None, "sp", None, None), P("dp", None, "sp", None, None), P(), P(), P()),
        out_specs=(P("dp", None, "sp", None, None), P(), P(), P()),
        check_vma=False,
    )
```

```python
import functools
import math

import jax
import jax.numpy as jnp
from jax import lax
from jax.experimental import pallas as pl
from jax.experimental.pallas import tpu as pltpu
from jax.sharding import PartitionSpec as P

MESH = pl.DeviceIdType.MESH
VMEM_LIMIT = 56 * 1024 * 1024


def exchange_groups(axes, radix_bits):
    bits = []
    for name, size in axes:
        assert size & (size - 1) == 0
        for b in range(size.bit_length() - 1):
            bits.append((name, 1 << b))
    bits = bits[1:]
    if len(bits) == 7:
        return [[bits[i] for i in group] for group in ((1, 2), (3, 4), (0, 5, 6))]
    return [bits[i : i + radix_bits] for i in range(0, len(bits), radix_bits)]


def coords(shape):
    lane = lax.broadcasted_iota(jnp.int32, shape, 1)
    return jnp.bitwise_and(lane, 127), jnp.right_shift(lane, 7)


def at_y(a, d, y):
    if d == 0:
        return a
    rolled = pltpu.roll(a, (-d) % a.shape[1], 1)
    return jnp.where((y + d >= 0) & (y + d < 128), rolled, 0.0)


def at_z(a, d, z):
    if d == 0:
        return a
    rolled = pltpu.roll(a, (-128 * d) % a.shape[1], 1)
    return jnp.where((z + d >= 0) & (z + d < a.shape[1] // 128), rolled, 0.0)


def widen(k, lanes):
    return jnp.broadcast_to(k, (k.shape[0], lanes))


def fold(a):
    total = a[:, :128]
    for g in range(1, a.shape[1] // 128):
        total = total + a[:, g * 128 : (g + 1) * 128]
    return total


def sigmoid(u):
    return 1.0 / (1.0 + jnp.exp(-u))


def plane_conv(planes, k_ref, b, flip, y):
    lanes = planes[0].shape[1]
    srcs = [p.astype(jnp.float32) for p in planes]
    total = None
    for j in range(3):
        column = None
        for i in range(3):
            tap = (2 - i) * 3 + (2 - j) if flip else i * 3 + j
            term = widen(k_ref[b, :, tap : tap + 1], lanes) * srcs[i]
            column = term if column is None else column + term
        column = at_y(column, j - 1, y)
        total = column if total is None else total + column
    return total


def depth_conv(a, kz_ref, b, flip, z):
    lanes = a.shape[1]
    total = None
    for t in range(3):
        tap = 2 - t if flip else t
        term = widen(kz_ref[b, :, 9 + tap : 10 + tap], lanes) * at_z(a, t - 1, z)
        total = term if total is None else total + term
    return total


def silu_grad(g, pre, s=None):
    s = sigmoid(pre) if s is None else s
    return (g * (s * (1.0 + pre * (1.0 - s)))).astype(jnp.bfloat16)


def weight_grads(b, gpre, ax, gax, pl, gpl, around, mix_ref, kzg_ref, kxyg_ref, y, z):
    mix_ref[b] += lax.dot_general(
        gpre, ax, (((1,), (1,)), ((), ())), preferred_element_type=jnp.float32
    )
    for t in range(3):
        kzg_ref[b, t] += fold(gax * at_z(pl, t - 1, z))
    gplf = gpl.astype(jnp.float32)
    srcs = [a.astype(jnp.float32) for a in around]
    for j in range(3):
        shifted = at_y(gplf, 1 - j, y)
        for i in range(3):
            kxyg_ref[b, i * 3 + j] += fold(shifted * srcs[i])


def whole_kernel(axes, groups, factor, vol_hbm, cot_hbm, kxy_ref, w_ref,
                 vg_hbm, sums_ref,
                 wide, cot_ref, vg_ref, h2, pl1, ax1, pre1, gp2, gp1, pay, mix_ref, kzg_ref, kxyg_ref, recv, acc,
                 in_send, in_recv, g_send, g_recv, e_send, e_recv, h_send, h_recv, sw_send, sw_recv, send_sem, recv_sem,
                 half_in, acc0, fin, sig1):
    own = cot_ref.shape[0]
    depth = vol_hbm.shape[2]
    kz_ref = kxy_ref
    y, z = coords(cot_ref.shape[1:])

    def to_planes(raw, buf, first):
        for x in range(own):
            v = pltpu.einshape("czy->zcy", raw[:, x].astype(jnp.float32))
            buf[first + x] = jnp.concatenate([v[k] for k in range(depth)], axis=1).astype(buf.dtype)

    here = {name: lax.axis_index(name) for name, _ in axes}
    steps = []
    for group in groups:
        partners = []
        for offset in range(1, 1 << len(group)):
            where = dict(here)
            for k, (name, stride) in enumerate(group):
                if (offset >> k) & 1:
                    bit = (where[name] // stride) % 2
                    where[name] = where[name] + stride * (1 - 2 * bit)
            partners.append(tuple(where[n] for n, _ in axes))
        steps.append(partners)
    sp, last, dp = here["sp"], axes[0][1] - 1, here["dp"]
    left, right = (sp - 1, dp), (sp + 1, dp)
    has_left, has_right = sp > 0, sp < last
    core = sp % 2
    mate = (sp + 1 - 2 * core, dp)
    extra_left = has_left & (core == 0)
    extra_right = has_right & (core == 1)

    barrier = pltpu.get_barrier_semaphore()
    pl.semaphore_signal(barrier, inc=1, device_id=mate, device_id_type=MESH)
    count = 1
    for partners in steps:
        for partner in partners:
            pl.semaphore_signal(barrier, inc=1, device_id=partner, device_id_type=MESH)
            count += 1

    @pl.when(extra_left)
    def _():
        pl.semaphore_signal(barrier, inc=1, device_id=left, device_id_type=MESH)

    @pl.when(extra_right)
    def _():
        pl.semaphore_signal(barrier, inc=1, device_id=right, device_id_type=MESH)

    to_planes(vol_hbm, wide, 1)
    to_planes(cot_hbm, cot_ref, 0)
    mix_ref[...] = jnp.zeros_like(mix_ref)
    kzg_ref[...] = jnp.zeros_like(kzg_ref)
    kxyg_ref[...] = jnp.zeros_like(kxyg_ref)
    pl.semaphore_wait(barrier, count + extra_left.astype(jnp.int32) + extra_right.astype(jnp.int32))

    def exchange(buf, first, count, send, recv, src, src_first):
        to_left = pltpu.make_async_remote_copy(
            src_ref=src.at[pl.ds(src_first, count)], dst_ref=buf.at[pl.ds(first + own, count)],
            send_sem=send.at[0], recv_sem=recv.at[1], device_id=left, device_id_type=MESH,
        )
        to_right = pltpu.make_async_remote_copy(
            src_ref=src.at[pl.ds(src_first + own - count, count)], dst_ref=buf.at[pl.ds(first - count, count)],
            send_sem=send.at[1], recv_sem=recv.at[0], device_id=right, device_id_type=MESH,
        )
        pl.when(has_left)(to_left.start)
        pl.when(has_right)(to_right.start)

        def finish():
            pl.when(has_left)(to_right.wait_recv)
            pl.when(has_right)(to_left.wait_recv)
            zeros = jnp.zeros((count,) + buf.shape[1:], buf.dtype)

            @pl.when(sp == 0)
            def _():
                buf[pl.ds(first - count, count)] = zeros

            @pl.when(sp == last)
            def _():
                buf[pl.ds(first + own, count)] = zeros

        def drain():
            pl.when(has_left)(to_left.wait_send)
            pl.when(has_right)(to_right.wait_send)

        return finish, drain


    finish_in, drain_in = exchange(wide, 1, 1, in_send, in_recv, wide, 1)

    def forward1(p):
        planar = plane_conv([wide[p + i] for i in range(3)], kxy_ref, 0, False, y)
        axial = depth_conv(planar, kz_ref, 0, False, z).astype(jnp.bfloat16)
        pre = jnp.dot(w_ref[0], axial, preferred_element_type=jnp.float32)
        pl1[p] = planar
        ax1[p] = axial
        pre1[p] = pre
        s = sigmoid(pre)
        sig1[p] = s
        h2[p + 1] = (pre * s).astype(jnp.bfloat16)

    def block2(q):
        around = [h2[q + i] for i in range(3)]
        planar = plane_conv(around, kxy_ref, 1, False, y)
        axial = depth_conv(planar, kz_ref, 1, False, z).astype(jnp.bfloat16)
        pre = jnp.dot(w_ref[1], axial, preferred_element_type=jnp.float32)
        gpre = silu_grad(cot_ref[q].astype(jnp.float32), pre)
        gax = lax.dot_general(w_ref[1], gpre, (((0,), (0,)), ((), ())), preferred_element_type=jnp.float32)
        gpl = depth_conv(gax, kz_ref, 1, True, z).astype(jnp.bfloat16)
        gp2[q + 1] = gpl
        weight_grads(1, gpre, axial, gax, planar, gpl, around, mix_ref, kzg_ref, kxyg_ref, y, z)

    def block1(q):
        g1 = plane_conv([gp2[q + i] for i in range(3)], kxy_ref, 1, True, y).astype(jnp.bfloat16)
        gpre = silu_grad(g1.astype(jnp.float32), pre1[q], sig1[q])
        gax = lax.dot_general(w_ref[0], gpre, (((0,), (0,)), ((), ())), preferred_element_type=jnp.float32)
        gpl = depth_conv(gax, kz_ref, 0, True, z).astype(jnp.bfloat16)
        gp1[q + 1] = gpl
        around = [wide[q + i] for i in range(3)]
        weight_grads(0, gpre, ax1[q], gax, pl1[q], gpl, around, mix_ref, kzg_ref, kxyg_ref, y, z)

    def run(body, lo, hi, place=lambda i: i):
        def step(i, carry):
            body(place(i))
            return carry

        lax.fori_loop(lo, hi, step, 0)

    run(forward1, 1, own - 1)
    finish_in()
    run(forward1, 0, 2, lambda i: i * (own - 1))
    finish_h, drain_h = exchange(h2, 1, 1, h_send, h_recv, h2, 1)
    run(block2, 1, own - 1)
    finish_h()
    run(block2, 0, 2, lambda i: i * (own - 1))
    finish_g, drain_g = exchange(gp2, 1, 1, g_send, g_recv, gp2, 1)
    run(block1, 1, own - 1)
    finish_g()
    run(block1, 0, 2, lambda i: i * (own - 1))
    finish_e, drain_e = exchange(gp1, 1, 1, e_send, e_recv, gp1, 1)
    drain_in()
    drain_h()
    drain_g()

    lane = lax.broadcasted_iota(jnp.int32, pay.shape[1:], 1)
    chans = pay.shape[1]
    for b in range(2):
        packed = jnp.zeros(pay.shape[1:], jnp.float32)
        packed = jnp.where(lane < chans, jnp.concatenate(
            [mix_ref[b], jnp.zeros((chans, pay.shape[2] - chans), jnp.float32)], axis=1), packed)
        for t in range(3):
            packed = jnp.where(lane == chans + t, jnp.sum(kzg_ref[b, t], axis=1, keepdims=True), packed)
        for t in range(9):
            packed = jnp.where(lane == chans + 3 + t, jnp.sum(kxyg_ref[b, t], axis=1, keepdims=True), packed)
        pay[b] = packed


    def conv_plane(q):
        vg_ref[q] = plane_conv([gp1[q + i] for i in range(3)], kxy_ref, 0, True, y).astype(vg_ref.dtype)
        v = vg_ref[q].astype(jnp.float32)
        v = jnp.stack([v[:, k * 128 : (k + 1) * 128] for k in range(depth)], axis=0)
        vg_hbm[:, q] = pltpu.einshape("zcy->czy", v).astype(vg_hbm.dtype)

    order = list(range(1, own - 1)) + [0, own - 1]
    halo_done = False
    swap = pltpu.make_async_remote_copy(
        src_ref=pay.at[1 - core], dst_ref=half_in, send_sem=sw_send.at[0], recv_sem=sw_recv.at[0],
        device_id=mate, device_id_type=MESH,
    )
    swap.start()
    swap.wait_recv()
    acc0[...] = pay[core] + half_in[...]
    src = acc0
    copies = []
    slot = 0
    for g, partners in enumerate(steps):
        here_copies = []
        for k, partner in enumerate(partners):
            copy = pltpu.make_async_remote_copy(
                src_ref=src,
                dst_ref=recv.at[slot + k],
                send_sem=send_sem.at[slot + k],
                recv_sem=recv_sem.at[slot + k],
                device_id=partner,
                device_id_type=MESH,
            )
            copy.start()
            here_copies.append(copy)
        todo = order[g * own // len(steps) : (g + 1) * own // len(steps)]
        if (0 in todo or own - 1 in todo) and not halo_done:
            finish_e()
            halo_done = True
        for q in todo:
            conv_plane(q)
        for copy in here_copies:
            copy.wait_recv()
        copies += here_copies
        vals = [src[...]] + [recv[slot + k] for k in range(len(partners))]
        while len(vals) > 1:
            vals = [vals[i] + vals[i + 1] for i in range(0, len(vals), 2)]
        acc[g] = vals[0]
        src = acc.at[g]
        slot += len(partners)
    fin[core] = src[...]
    back = pltpu.make_async_remote_copy(
        src_ref=fin.at[core], dst_ref=fin.at[core], send_sem=sw_send.at[1], recv_sem=sw_recv.at[1],
        device_id=mate, device_id_type=MESH,
    )
    back.start()
    back.wait_recv()
    sums_ref[...] = fin[...] * factor
    for copy in copies:
        copy.wait_send()
    swap.wait_send()
    back.wait_send()
    drain_e()


def on_device(volume, cotangent, kernels_xy, kernels_z, mixing):
    _, chans, own, depth, across = volume.shape
    lanes = depth * across
    f32, bf16 = jnp.float32, jnp.bfloat16
    taps = jnp.concatenate(
        [kernels_xy.reshape(2, chans, 9), kernels_z], axis=2
    ).astype(f32)
    ranks = lax.axis_size("sp")
    axes = (("sp", ranks), ("dp", lax.axis_size("dp")))
    groups = exchange_groups(axes, 2)
    slots = sum((1 << len(g)) - 1 for g in groups)
    assert own >= 2 and chans + 12 <= 128
    factor = 1.0 / math.sqrt(lax.axis_size("dp") * own * ranks * depth * across)
    planes = lambda n, t: pltpu.VMEM((n, chans, lanes), t)
    grad_in, sums = pl.pallas_call(
        functools.partial(whole_kernel, axes, groups, factor),
        out_shape=(
            jax.ShapeDtypeStruct((chans, own, depth, across), bf16),
            jax.ShapeDtypeStruct((2, chans, 128), f32),
        ),
        in_specs=[pl.BlockSpec(memory_space=pltpu.VMEM)] * 4,
        out_specs=[pl.BlockSpec(memory_space=pltpu.VMEM)] * 2,
        scratch_shapes=[
            planes(own + 2, bf16),
            planes(own, bf16),
            planes(own, bf16),
            planes(own + 2, bf16),
            planes(own, f32),
            planes(own, bf16),
            planes(own, f32),
            planes(own + 2, bf16),
            planes(own + 2, bf16),
            pltpu.VMEM((2, chans, 128), f32),
            pltpu.VMEM((2, chans, chans), f32),
            pltpu.VMEM((2, 3, chans, 128), f32),
            pltpu.VMEM((2, 9, chans, 128), f32),
            pltpu.VMEM((slots, chans, 128), f32),
            pltpu.VMEM((len(groups), chans, 128), f32),
        ] + [pltpu.SemaphoreType.DMA((2,))] * 10 + [pltpu.SemaphoreType.DMA((slots,))] * 2 + [
            pltpu.VMEM((chans, 128), f32),
            pltpu.VMEM((chans, 128), f32),
            pltpu.VMEM((2, chans, 128), f32),
            planes(own, f32),
        ],
        compiler_params=pltpu.CompilerParams(
            collective_id=0, has_side_effects=True, vmem_limit_bytes=VMEM_LIMIT
        ),
    )(volume[0], cotangent[0], taps, mixing)
    grad_in = grad_in[None]
    mixing_grad = sums[:, :, :chans]
    z_grad = sums[:, :, chans : chans + 3]
    xy_grad = sums[:, :, chans + 3 : chans + 12].reshape(2, chans, 3, 3)
    return (grad_in, mixing_grad, xy_grad, z_grad)


def solution(mesh):
    return jax.shard_map(
        on_device,
        mesh=mesh,
        in_specs=(P("dp", None, "sp", None, None), P("dp", None, "sp", None, None), P(), P(), P()),
        out_specs=(P("dp", None, "sp", None, None), P(), P(), P()),
        check_vma=False,
    )
```
